128 devices in a mesh: seq: 8 (over x, core), exp: 16 (over y, z).
Axes of the slice: x: 4, y: 4, z: 4, core: 2. Of those that a mesh axis runs over, the one named last changes fastest.
Arguments:
- xin: bfloat16 [512, 4, 8192], P('seq', None, 'exp'), may hold values from -6 to 6
- zin: bfloat16 [512, 4, 8192], P('seq', None, 'exp'), may hold values from -6 to 6
- conv_weight: float32 [4, 8192], P(None, 'exp'), may hold values from -3 to 3
- conv_bias: float32 [8192], P('exp'), may hold values from -3 to 3
- xproj_weight: bfloat16 [8192, 288], P('exp'), may hold values from -0.0625 to 0.0625
- dtproj_weight: bfloat16 [256, 8192], P(None, 'exp'), may hold values from -0.375 to 0.375
- dt_bias: float32 [8192], P('exp'), may hold values from -5 to -3
- a_log: float32 [16, 8192], P(None, 'exp'), may hold values from -3 to 1
- skip: float32 [8192], P('exp'), may hold values from 0.2 to 1
- out_weight: bfloat16 [8192, 4096], P('exp'), may hold values from -0.0625 to 0.0625
- resid: bfloat16 [512, 4, 4096], P(('seq', 'exp')), may hold values from -6 to 6
- norm_gain: float32 [4096], replicated, may hold values from 0.5 to 1.5
- expert_ids: int32 [512, 4, 2], P(('seq', 'exp')), may hold values from 0 to 7, all different within a row; in each aligned block of 16 rows (0 to 15, 16 to 31, ..., all dimensions but the last counted through in order) at most 8 rows name the same one
- gate_weights: bfloat16 [512, 4, 2], P(('seq', 'exp')), may hold values from 0.19921875 to 1
- w_gate: bfloat16 [16, 4096, 6144], P('exp', None, 'seq'), may hold values from -0.09375 to 0.09375
- w_up: bfloat16 [16, 4096, 6144], P('exp', None, 'seq'), may hold values from -0.09375 to 0.09375
- w_down: bfloat16 [16, 6144, 4096], P('exp', 'seq'), may hold values from -0.0546875 to 0.0546875
Outputs:
- layer_out: bfloat16 [512, 4, 4096], P(('seq', 'exp'))
The draws below stay inside these ranges and needn't reach their ends.
Inputs may be any that keep to these rules, and one draw needn't show every extreme that they name: `expert_ids`: tokens are ordered by position, then document; in each aligned block of 16 such tokens (the tokens of one device), every expert is named at most 8 times, and in every draw some expert is named exactly 8 times in some block. Each token names 2 different experts.
All inputs are finite; a program needn't handle non-finite values.
Results may differ from the reference program's by a relative error of at most 0.03.
Values may be sent and summed in bfloat16 or wider, within the bound.
No kernel may reach another device: no remote copies, remote signals or barrier semaphores. Data moves between devices by JAX's collectives and lax.ppermute only.
A program may use at most 128 MiB of HBM per device.

```python
import math
import jax
import jax.numpy as jnp
import numpy as np
from jax import lax

D = 4096
EI = 8192
STATE = 16
CONV = 4
RANK = 256
EXPERTS = 8
TOPK = 2
FF = 12288
SEQS = 4
LENGTH = 512
SPLITS = 2
FF_PART = 6144
ROWS = 16
CAP = 8
N_SEQ = 8
N_EXP = 16


def level_of(own_key, extent, cuts, smallest, high):
    loudness = 1.0
    for dim, blocks in cuts:
        steps = jax.random.uniform(jax.random.fold_in(jax.random.fold_in(own_key, 6), dim), (blocks,), jnp.float32, smallest / len(cuts), high / len(cuts))
        loudness = loudness * jnp.repeat(jnp.exp(steps), extent[dim] // blocks).reshape((-1,) + (1,) * (len(extent) - 1 - dim))
    return loudness


def shared_out(rng, own, number, rows, amount, top, reach, lean):
    ranking = jax.random.permutation(rng, amount)
    crowded, common = load_shares(amount, rows * top, reach, lean, True), load_shares(amount, rows * top, reach, lean, False)
    places = jnp.arange(amount)

    def named(sizes, rotation):
        used = int((sizes > 0).sum())
        fixed = max(1, used // 4)
        moved = fixed + (places - fixed + rotation * (used - fixed)) % max(1, amount - fixed)
        return jnp.zeros((amount,), jnp.int32).at[ranking[jnp.where(places < fixed, places, moved)]].set(jnp.asarray(sizes, jnp.int32))

    sizes = jnp.where(number % 4 == 0, named(crowded, number // 4), named(common, number - number // 4 - 1))
    mixed = jax.random.permutation(jax.random.fold_in(own, 3), amount)
    donor, taker = mixed[0:amount // 2 * 2:2], mixed[1:amount // 2 * 2:2]
    room = jnp.minimum(sizes[donor] - 1, reach - sizes[taker]) // 2
    room = jnp.where((donor == ranking[0]) | (taker == ranking[0]) | (sizes[taker] == 0), 0, jnp.maximum(room, 0))
    moved = jax.random.randint(jax.random.fold_in(own, 4), (amount // 2,), 0, 1 << 20) % (room + 1)
    sizes = sizes.at[donor].add(-moved).at[taker].add(moved)
    members = jnp.searchsorted(jnp.cumsum(sizes), jnp.arange(rows * top), side="right").astype(jnp.int32)
    listing = members.reshape(top, rows).T
    listing = listing[jax.random.permutation(jax.random.fold_in(own, 1), rows)]
    rotation = jax.random.randint(jax.random.fold_in(own, 2), (rows, 1), 0, top)
    return jnp.take_along_axis(listing, (jnp.arange(top)[None, :] + rotation) % top, axis=1)


def load_shares(amount, total, most, lean, full):
    loads = [(1 << 20) // math.isqrt(standing ** lean) + 1 for standing in range(1, amount + 1)]
    largest = most if full else min(most, max(-(-total // amount), total * loads[0] // sum(loads)))
    least = 1 if total - largest >= amount - 1 else 0
    holding, rest = [largest] + [least] * (amount - 1), total - largest - least * (amount - 1)
    while rest > 0:
        candidates = [i for i in range(1, amount) if holding[i] < largest] or [i for i in range(1, amount) if holding[i] < most]
        whole, left = sum([loads[i] for i in candidates]), rest
        for i in candidates:
            more = min(most - holding[i], max(1, left * loads[i] // whole), rest)
            holding[i] = holding[i] + more
            rest = rest - more
    return np.array(holding)


def scatter_about(own_key, extent, scale, reach, pieces=(), kind=jnp.bfloat16):
    values = jax.random.normal(own_key, extent, jnp.float32) * scale
    if len(pieces) > 0:
        values = level_of(own_key, extent, pieces, -0.22, 0.18) * values
    return jnp.clip(values, min=-reach, max=reach).astype(kind)


def setup_inputs(seed: int = 0) -> dict:
    splits = jax.random.split(jax.random.key(seed), 18)
    xin = scatter_about(splits[0], (LENGTH, SEQS, EI), 1.0, 6.0, ((0, 8), (2, 16)))
    zin = scatter_about(splits[1], (LENGTH, SEQS, EI), 1.0, 6.0, ((0, 8), (2, 16)))
    conv_weight = scatter_about(splits[2], (CONV, EI), 0.5, 3.0, ((1, 16),), jnp.float32)
    conv_bias = scatter_about(splits[3], (EI,), 0.5, 3.0, ((0, 16),), jnp.float32)
    xproj_weight = scatter_about(splits[4], (EI, RANK + 2 * STATE), EI ** -0.5, 0.0625, ((0, 16),))
    dtproj_weight = scatter_about(splits[5], (RANK, EI), RANK ** -0.5, 0.375, ((1, 16),))
    dt_bias = jnp.clip(-5.0 + 2.0 * jax.random.uniform(splits[6], (EI,), jnp.float32) ** level_of(splits[6], (EI,), ((0, 16),), -0.2, 0.2), -5.0, -3.0)
    a_log = jnp.clip(-3.0 + 4.0 * jax.random.uniform(splits[7], (STATE, EI), jnp.float32) ** level_of(splits[7], (STATE, EI), ((1, 16),), -0.2, 0.2), -3.0, 1.0)
    skip = jnp.clip(0.2 + 0.8 * jax.random.uniform(splits[8], (EI,), jnp.float32) ** level_of(splits[8], (EI,), ((0, 16),), -0.2, 0.2), 0.2, 1.0)
    out_weight = scatter_about(splits[9], (EI, D), EI ** -0.5, 0.0625, ((0, 16),))
    resid = scatter_about(splits[10], (LENGTH, SEQS, D), 1.0, 6.0, ((0, 128),))
    norm_gain = jnp.clip(1.0 + 0.1 * jax.random.normal(splits[11], (D,), jnp.float32), 0.5, 1.5)
    expert_ids_keys = jax.random.split(jax.random.fold_in(splits[12], 1), LENGTH * SEQS // ROWS)
    expert_ids_turns = jax.random.permutation(jax.random.fold_in(splits[12], 3), LENGTH * SEQS // ROWS)
    expert_ids = jax.vmap(lambda own, number: shared_out(jax.random.fold_in(splits[12], 2), own, number, ROWS, EXPERTS, TOPK, CAP, 2))(expert_ids_keys, expert_ids_turns).reshape((LENGTH, SEQS, TOPK))
    gate_weights = jnp.clip(0.19921875 + 0.80078125 * jax.random.uniform(splits[13], (LENGTH, SEQS, TOPK), jnp.float32) ** level_of(splits[13], (LENGTH, SEQS, TOPK), ((0, 128),), -0.2, 0.2), 0.19921875, 1.0).astype(jnp.bfloat16)
    w_gate = scatter_about(splits[14], (N_EXP, D, FF_PART), D ** -0.5, 0.09375, ((0, 16), (2, 8)))
    w_up = scatter_about(splits[15], (N_EXP, D, FF_PART), D ** -0.5, 0.09375, ((0, 16), (2, 8)))
    w_down = scatter_about(splits[16], (N_EXP, FF_PART, D), FF ** -0.5, 0.0546875, ((0, 16), (1, 8)))
    return {"xin": xin, "zin": zin, "conv_weight": conv_weight, "conv_bias": conv_bias, "xproj_weight": xproj_weight, "dtproj_weight": dtproj_weight, "dt_bias": dt_bias, "a_log": a_log, "skip": skip, "out_weight": out_weight, "resid": resid, "norm_gain": norm_gain, "expert_ids": expert_ids, "gate_weights": gate_weights, "w_gate": w_gate, "w_up": w_up, "w_down": w_down}


def conv_inputs(window, conv_weight, conv_bias, length):
    running = jnp.zeros(window[:length].shape, jnp.float32) + conv_bias
    for offset in range(CONV):
        running = running + conv_weight[offset] * window[offset:offset + length]
    return running

def make_step(decay_rate):

    def advance(carry_state, series_now):
        step_now, input_now, read_now, value_now = series_now
        factor = jnp.exp(step_now[:, None, :] * decay_rate[None])
        carry_state = factor * carry_state + (step_now * value_now)[:, None, :] * input_now[:, :, None]
        return (carry_state, lax.optimization_barrier(jnp.sum(read_now[:, :, None] * carry_state, axis=1)))
    return advance

def slot_select(route_ids, capacity):
    flat_ids = route_ids.reshape(-1)
    onehot = (flat_ids[:, None] == jnp.arange(EXPERTS, dtype=jnp.int32)[None, :]).astype(jnp.int32)
    before = lax.optimization_barrier(jnp.sum((jnp.cumsum(onehot, axis=0) - onehot) * onehot, axis=1))
    target = flat_ids * capacity + before
    matches = jnp.arange(EXPERTS * capacity, dtype=jnp.int32)[:, None] == target[None, :]
    return matches.reshape(EXPERTS * capacity, route_ids.shape[0], route_ids.shape[1])

def reference(xin, zin, conv_weight, conv_bias, xproj_weight, dtproj_weight, dt_bias, a_log, skip, out_weight, resid, norm_gain, expert_ids, gate_weights, w_gate, w_up, w_down):
    xf = xin.astype(jnp.float32)
    window = jnp.concatenate([jnp.zeros((CONV - 1,) + xf.shape[1:], jnp.float32), xf], axis=0)
    inner_act = jax.nn.silu(conv_inputs(window, conv_weight, conv_bias, LENGTH)).astype(jnp.bfloat16)
    inner_f = inner_act.astype(jnp.float32)
    projected = jnp.einsum('pbc,cr->pbr', inner_f, xproj_weight.astype(jnp.float32))
    low_rank = projected[..., :RANK].astype(jnp.bfloat16)
    in_state = projected[..., RANK:RANK + STATE]
    out_state = projected[..., RANK + STATE:]
    step_size = jax.nn.softplus(jnp.einsum('pbr,rc->pbc', low_rank.astype(jnp.float32), dtproj_weight.astype(jnp.float32)) + dt_bias)
    decay_rate = -jnp.exp(a_log)
    zero_state = jnp.zeros((SEQS, STATE, EI), jnp.float32)
    ignored, ssm_out = lax.scan(make_step(decay_rate), zero_state, (step_size, in_state, out_state, inner_f))
    mixed_in = ((ssm_out + skip * inner_f) * jax.nn.silu(zin.astype(jnp.float32))).astype(jnp.bfloat16)
    hidden_state = resid.astype(jnp.float32) + jnp.einsum('pbc,cd->pbd', mixed_in.astype(jnp.float32), out_weight.astype(jnp.float32))
    norm_scale = lax.rsqrt(lax.optimization_barrier(jnp.mean(hidden_state * hidden_state, axis=-1, keepdims=True)) + 1e-05)
    normed = (hidden_state * norm_scale * norm_gain).astype(jnp.bfloat16)
    tokens = normed.reshape(-1, ROWS, D)
    route_ids = expert_ids.reshape(-1, ROWS, TOPK)
    gate_vals = gate_weights.astype(jnp.float32).reshape(-1, ROWS, TOPK)
    matches = jax.vmap(lambda block_ids: slot_select(block_ids, CAP))(route_ids)
    chosen = lax.optimization_barrier(jnp.sum(matches.astype(jnp.float32), axis=3))
    buffer = jnp.einsum('nqr,nrd->qnd', chosen, tokens.astype(jnp.float32), precision=lax.Precision.HIGHEST).astype(jnp.bfloat16)
    buffer = buffer.reshape(EXPERTS, -1, D)
    part_width = FF_PART // N_SEQ

    def run_expert(expert):
        row_block = buffer[expert]
        running = jnp.zeros(row_block.shape, jnp.float32)
        for split_index in range(SPLITS):
            gate_full = w_gate[split_index * EXPERTS + expert]
            up_full = w_up[split_index * EXPERTS + expert]
            down_full = w_down[split_index * EXPERTS + expert]
            for part_index in range(N_SEQ):
                low = part_index * part_width
                gate_act = jnp.dot(row_block, gate_full[:, low:low + part_width], preferred_element_type=jnp.float32)
                up_act = jnp.dot(row_block, up_full[:, low:low + part_width], preferred_element_type=jnp.float32)
                hidden = (jax.nn.silu(gate_act) * up_act).astype(jnp.bfloat16)
                term = jnp.dot(hidden, down_full[low:low + part_width], preferred_element_type=jnp.float32).astype(jnp.bfloat16)
                running = running + term.astype(jnp.float32)
        return running
    results = lax.map(run_expert, jnp.arange(EXPERTS, dtype=jnp.int32))
    results = results.reshape(EXPERTS * CAP, -1, D)
    weights = lax.optimization_barrier(jnp.sum(matches.astype(jnp.float32) * gate_vals[:, None, :, :], axis=3))
    expert_out = jnp.einsum('nqr,qnd->nrd', weights, results, precision=lax.Precision.HIGHEST)
    return (hidden_state + expert_out.reshape(hidden_state.shape)).astype(jnp.bfloat16)
```

```python
import jax
import jax.numpy as jnp
from jax import lax
from jax.sharding import PartitionSpec as P

D = 4096
STATE = 16
CONV = 4
RANK = 256
EXPERTS = 8
TOPK = 2
F32 = jnp.float32
BF16 = jnp.bfloat16


def z_shift(by):
    return [(y * 4 + z, y * 4 + (z + by) % 4) for y in range(4) for z in range(4)]


def y_shift(by):
    return [(y * 4 + z, (y + by) % 4 * 4 + z) for y in range(4) for z in range(4)]


def x_shift(by):
    return [(x * 2 + c, (x + by) % 4 * 2 + c) for x in range(4) for c in range(2)]


CORE = [(x * 2 + c, x * 2 + 1 - c) for x in range(4) for c in range(2)]


def passed_along(value, axis, by):
    count = lax.axis_size(axis)
    pairs = [(i, i + by) for i in range(count) if 0 <= i + by < count]
    return lax.ppermute(value, axis, pairs)


def summed_over_exp(value):
    for shift in (z_shift, y_shift):
        sent = value.astype(BF16)
        parts = [lax.ppermute(sent, "exp", shift(by)) for by in (1, 2, 3)]
        value = sent.astype(F32)
        for part in parts:
            value = value + part.astype(F32)
    return value


def conv_inputs(window, conv_weight, conv_bias, length):
    running = jnp.zeros(window[:length].shape, F32) + conv_bias
    for offset in range(CONV):
        running = running + conv_weight[offset] * window[offset : offset + length]
    return running


def make_step(decay_rate):

    def advance(carry_state, series_now):
        step_now, input_now, read_now, value_now = series_now
        factor = jnp.exp(step_now[:, None, :] * decay_rate[None])
        carry_state = (
            factor * carry_state + (step_now * value_now)[:, None, :] * input_now[:, :, None]
        )
        return (carry_state, jnp.sum(read_now[:, :, None] * carry_state, axis=1))

    return advance


def entering(step_total, final_local, decay_rate):
    place = lax.axis_index("seq")
    high = step_total.astype(BF16)
    low = (step_total - high.astype(F32)).astype(BF16)
    packed = jnp.concatenate([final_local.astype(BF16), high[:, None], low[:, None]], axis=1)
    gathered = lax.all_gather(packed, "seq")
    state = jnp.zeros_like(final_local)
    for section in range(lax.axis_size("seq") - 1):
        total = gathered[section, :, STATE].astype(F32) + gathered[section, :, STATE + 1].astype(F32)
        decay = jnp.exp(total[:, None, :] * decay_rate[None])
        later = decay * state + gathered[section, :, :STATE].astype(F32)
        state = jnp.where(section < place, later, state)
    return state


def slot_select(route_ids, capacity):
    flat_ids = route_ids.reshape(-1)
    onehot = (flat_ids[:, None] == jnp.arange(EXPERTS, dtype=jnp.int32)[None, :]).astype(jnp.int32)
    before = jnp.sum((jnp.cumsum(onehot, axis=0) - onehot) * onehot, axis=1)
    target = flat_ids * capacity + before
    matches = jnp.arange(EXPERTS * capacity, dtype=jnp.int32)[:, None] == target[None, :]
    return matches.reshape(EXPERTS * capacity, route_ids.shape[0], route_ids.shape[1])


def expert_block(rows, w_gate, w_up, w_down):
    gate_act = jnp.dot(rows, w_gate, preferred_element_type=F32)
    up_act = jnp.dot(rows, w_up, preferred_element_type=F32)
    hidden = (jax.nn.silu(gate_act) * up_act).astype(BF16)
    return jnp.dot(hidden, w_down, preferred_element_type=F32).astype(BF16)


def swapped(value):
    return lax.ppermute(value, "seq", CORE)


def experts(own, w_gate, w_up, w_down):
    count = own.shape[0]
    half = count // 2

    def block(rows):
        return expert_block(rows, w_gate, w_up, w_down)

    left = lax.ppermute(own, "seq", x_shift(1))
    right = lax.ppermute(own, "seq", x_shift(-1))
    own_out = block(jnp.concatenate([own, swapped(own)]))
    far = jnp.concatenate(
        [
            lax.ppermute(left[:half], "seq", x_shift(1)),
            lax.ppermute(right[half:], "seq", x_shift(-1)),
        ]
    )
    near_out = block(jnp.concatenate([left, right, swapped(left), swapped(right)]))
    far_out = block(jnp.concatenate([far, swapped(far)]))

    def paired(out):
        mine, other = jnp.split(out, 2)
        return mine.astype(F32) + swapped(other).astype(F32)

    near = paired(near_out).astype(BF16)
    to_left, to_right = near[:count], near[count:]
    from_right = lax.ppermute(to_left, "seq", x_shift(-1))
    from_left = lax.ppermute(to_right, "seq", x_shift(1))
    from_far = lax.ppermute(paired(far_out).astype(BF16), "seq", x_shift(2))
    return (
        paired(own_out)
        + from_left.astype(F32)
        + from_right.astype(F32)
        + from_far.astype(F32)
    )


def per_device(
    xin,
    zin,
    conv_weight,
    conv_bias,
    xproj_weight,
    dtproj_weight,
    dt_bias,
    a_log,
    skip,
    out_weight,
    resid,
    norm_gain,
    expert_ids,
    gate_weights,
    w_gate,
    w_up,
    w_down,
):
    section, docs, channels = xin.shape
    edge_rows = passed_along(xin[section - (CONV - 1) :], "seq", 1)
    window = jnp.concatenate([edge_rows, xin], axis=0).astype(F32)
    inner_act = jax.nn.silu(conv_inputs(window, conv_weight, conv_bias, section)).astype(BF16)
    inner_f = inner_act.astype(F32)
    projected = jnp.dot(
        inner_act.reshape(section * docs, channels), xproj_weight, preferred_element_type=F32
    )
    projected = summed_over_exp(projected).reshape(section, docs, -1)
    low_rank = projected[..., :RANK].astype(BF16)
    in_state = projected[..., RANK : RANK + STATE]
    out_state = projected[..., RANK + STATE :]
    step_size = jax.nn.softplus(
        jnp.einsum("pbr,rc->pbc", low_rank, dtproj_weight, preferred_element_type=F32) + dt_bias
    )
    decay_rate = -jnp.exp(a_log)
    advance = make_step(decay_rate)
    series = (step_size, in_state, out_state, inner_f)
    zero_state = jnp.zeros((docs, STATE, channels), F32)
    final_local, local_out = lax.scan(advance, zero_state, series)
    incoming = entering(jnp.sum(step_size, axis=0), final_local, decay_rate)
    ignored, ssm_out = lax.scan(advance, incoming, series)
    mixed_in = ((ssm_out + skip * inner_f) * jax.nn.silu(zin.astype(F32))).astype(BF16)
    partial_rows = jnp.dot(
        mixed_in.reshape(section * docs, channels), out_weight, preferred_element_type=F32
    ).astype(BF16)
    exchanged = lax.all_to_all(partial_rows, "exp", split_axis=0, concat_axis=0, tiled=True)
    row_count = resid.shape[0] * resid.shape[1]
    mamba_rows = jnp.sum(exchanged.reshape(-1, row_count, D).astype(F32), axis=0)
    hidden_state = resid.reshape(row_count, D).astype(F32) + mamba_rows
    norm_scale = lax.rsqrt(jnp.mean(hidden_state * hidden_state, axis=-1, keepdims=True) + 1e-05)
    tokens = (hidden_state * norm_scale * norm_gain).astype(BF16)
    capacity = 2 * TOPK * row_count // EXPERTS
    splits = lax.axis_size("exp") // EXPERTS
    route_ids = expert_ids.reshape(row_count, TOPK)
    gate_vals = gate_weights.reshape(row_count, TOPK)
    matches = slot_select(route_ids, capacity)
    chosen = jnp.sum(matches.astype(jnp.int32), axis=2).astype(BF16)
    outgoing = jnp.dot(chosen, tokens, preferred_element_type=F32).astype(BF16)
    arrived = lax.all_to_all(
        jnp.tile(outgoing, (splits, 1)), "exp", split_axis=0, concat_axis=0, tiled=True
    )
    own_rows = experts(arrived, w_gate[0], w_up[0], w_down[0])
    returned = lax.all_to_all(
        own_rows.astype(BF16), "exp", split_axis=0, concat_axis=0, tiled=True
    ).astype(F32)
    summed = jnp.sum(returned.reshape(splits, EXPERTS * capacity, D), axis=0)
    weights = jnp.sum(matches.astype(F32) * gate_vals.astype(F32)[None], axis=2)
    expert_out = jnp.dot(weights.T, summed, precision=lax.Precision.HIGHEST)
    return (hidden_state + expert_out).astype(BF16).reshape(resid.shape)


def solution(mesh):
    placed = (
        P("seq", None, "exp"),
        P("seq", None, "exp"),
        P(None, "exp"),
        P("exp"),
        P("exp", None),
        P(None, "exp"),
        P("exp"),
        P(None, "exp"),
        P("exp"),
        P("exp", None),
        P(("seq", "exp"), None, None),
        P(),
        P(("seq", "exp"), None, None),
        P(("seq", "exp"), None, None),
        P("exp", None, "seq"),
        P("exp", None, "seq"),
        P("exp", "seq", None),
    )
    return jax.shard_map(
        per_device,
        mesh=mesh,
        in_specs=placed,
        out_specs=P(("seq", "exp"), None, None),
        check_vma=False,
    )
```

```python
import jax
import jax.numpy as jnp
from jax import lax
from jax.experimental import pallas as pl
from jax.experimental.pallas import tpu as pltpu
from jax.sharding import PartitionSpec as P

D = 4096
STATE = 16
CONV = 4
RANK = 256
EXPERTS = 8
TOPK = 2
DOCS = 4
SECTION = 64
TOKENS = DOCS * SECTION
LANES = 128
F32 = jnp.float32
BF16 = jnp.bfloat16


def z_shift(by):
    return [(y * 4 + z, y * 4 + (z + by) % 4) for y in range(4) for z in range(4)]


def y_shift(by):
    return [(y * 4 + z, (y + by) % 4 * 4 + z) for y in range(4) for z in range(4)]


def x_shift(by):
    return [(x * 2 + c, (x + by) % 4 * 2 + c) for x in range(4) for c in range(2)]


CORE = [(x * 2 + c, x * 2 + 1 - c) for x in range(4) for c in range(2)]


def passed_along(value, axis, by):
    count = lax.axis_size(axis)
    pairs = [(i, i + by) for i in range(count) if 0 <= i + by < count]
    return lax.ppermute(value, axis, pairs)


def from_others(value, shift):
    return [lax.ppermute(value, "exp", shift(by)) for by in (1, 2, 3)]


def swapped(value):
    return lax.ppermute(value, "seq", CORE)


def document_major(back):
    row = lax.broadcasted_iota(jnp.int32, (TOKENS, TOKENS), 0)
    column = lax.broadcasted_iota(jnp.int32, (TOKENS, TOKENS), 1)
    if back:
        source = (row & (DOCS - 1)) * SECTION + (row >> 2)
    else:
        source = (row & (SECTION - 1)) * DOCS + (row >> 6)
    return jnp.where(column == source, 1.0, 0.0).astype(BF16)


def mixer_in_kernel(xin, edge, conv_weight, conv_bias, xproj, inner, projected, window):
    window[16 - edge.shape[0] : 16, :] = edge[...].astype(F32)
    window[16 : 16 + TOKENS, :] = xin[...].astype(F32)
    blocks = []
    for low in range(0, TOKENS, 64):
        running = jnp.broadcast_to(conv_bias[...], (64, xin.shape[1]))
        for offset in range(CONV):
            tap = window[pl.ds(low + 16 - DOCS * (CONV - 1 - offset), 64), :]
            running = running + conv_weight[offset : offset + 1, :] * tap
        blocks.append(jax.nn.silu(running).astype(BF16))
    by_position = jnp.concatenate(blocks, axis=0)
    ordered = jnp.dot(document_major(False), by_position, preferred_element_type=F32).astype(BF16)
    inner[...] = ordered
    projected[...] = jnp.dot(ordered, xproj[...], preferred_element_type=F32).astype(BF16)


def spread(pairs, target, first):
    lane = lax.broadcasted_iota(jnp.int32, (STATE, LANES), 1)
    entry = lax.broadcasted_iota(jnp.int32, (STATE, LANES), 0)
    mask = jnp.where((lane == first + entry) | (lane == first + STATE + entry), 1.0, 0.0)
    ones = jnp.ones((LANES, LANES), BF16)

    def one(group, carry):
        rows = pairs[pl.ds(pl.multiple_of(group * 16, 16), 16), :].astype(F32)
        wide = jnp.broadcast_to(rows[:, None, :], (16, STATE, LANES)) * mask[None]
        wide = wide.reshape(16 * STATE, LANES).astype(BF16)
        place = pl.ds(pl.multiple_of(group * 16 * STATE, 16 * STATE), 16 * STATE)
        target[place, :] = jnp.dot(wide, ones, preferred_element_type=F32)
        return carry

    lax.fori_loop(0, TOKENS // 16, one, 0)


def four_times(block):
    return jnp.concatenate([block] * 4, axis=1)


def section_kernel(
    p0, p1, p2, p3, dtproj, dt_bias, a_log, inner, step, pairs, packed, taken, entering
):
    total = (p0[...].astype(F32) + p1[...].astype(F32)) + (
        p2[...].astype(F32) + p3[...].astype(F32)
    )
    low_rank = total[:, :RANK].astype(BF16)
    states = total[:, RANK : RANK + 2 * STATE]
    high = states.astype(BF16)
    low = (states - high.astype(F32)).astype(BF16)
    pairs[...] = jnp.concatenate(
        [
            high[:, :STATE],
            low[:, :STATE],
            high[:, STATE:],
            low[:, STATE:],
            jnp.zeros((TOKENS, LANES - 4 * STATE), BF16),
        ],
        axis=1,
    )
    step[...] = jax.nn.softplus(
        jnp.dot(low_rank, dtproj[...], preferred_element_type=F32) + dt_bias[...]
    )
    taken[...] = step[...] * inner[...].astype(F32)
    spread(pairs, entering, 0)
    rate = -jnp.exp(a_log[...])

    def document(doc, carry):
        def eight(group, state):
            first = pl.multiple_of(doc * SECTION + group * 8, 8)
            steps = step[pl.ds(first, 8), :]
            values = taken[pl.ds(first, 8), :]
            for i in range(8):
                into = entering[pl.ds(pl.multiple_of((first + i) * STATE, STATE), STATE), :]
                factor = jnp.exp(steps[i : i + 1] * rate)
                state = factor * state + values[i : i + 1] * four_times(into)
            return state

        state = lax.fori_loop(0, SECTION // 8, eight, jnp.zeros(rate.shape, F32))
        packed[pl.ds(pl.multiple_of(doc * STATE, STATE), STATE), :] = state.astype(BF16)
        return carry

    lax.fori_loop(0, DOCS, document, 0)
    sums = jnp.concatenate(
        [
            jnp.sum(step[doc * SECTION : (doc + 1) * SECTION, :], axis=0, keepdims=True)
            for doc in range(DOCS)
        ],
        axis=0,
    )
    high = sums.astype(BF16).astype(F32)
    both = jnp.concatenate([high, sums - high], axis=0)
    packed[DOCS * STATE : DOCS * STATE + 2 * DOCS, :] = both.astype(BF16)


def mixer_out_kernel(
    place,
    gathered,
    step,
    pairs,
    inner,
    a_log,
    skip,
    zin,
    out_weight,
    rows,
    totals,
    taken,
    entering,
    leaving,
    scanned,
    weight,
    arrived,
):
    copy = pltpu.make_async_copy(out_weight, weight, arrived)
    copy.start()
    sections = gathered.shape[0]
    for section in range(sections - 1):
        both = gathered[section, DOCS * STATE : DOCS * STATE + 2 * DOCS, :].astype(F32)
        totals[8 * section : 8 * section + DOCS, :] = both[:DOCS] + both[DOCS:]
    taken[...] = step[...] * inner[...].astype(F32)
    spread(pairs, entering, 0)
    spread(pairs, leaving, 2 * STATE)
    rate = -jnp.exp(a_log[...])

    def document(doc, carry):
        state = jnp.zeros(rate.shape, F32)
        for section in range(sections - 1):
            total = totals[pl.ds(8 * section + doc, 1), :]
            final = gathered[section, pl.ds(pl.multiple_of(doc * STATE, STATE), STATE), :]
            later = jnp.exp(total * rate) * state + final.astype(F32)
            state = jnp.where(section < place[0], later, state)

        def eight(group, state):
            first = pl.multiple_of(doc * SECTION + group * 8, 8)
            steps = step[pl.ds(first, 8), :]
            values = taken[pl.ds(first, 8), :]
            sums = []
            for i in range(8):
                where = pl.ds(pl.multiple_of((first + i) * STATE, STATE), STATE)
                factor = jnp.exp(steps[i : i + 1] * rate)
                state = factor * state + values[i : i + 1] * four_times(entering[where, :])
                seen = state * four_times(leaving[where, :])
                sums.append(jnp.sum(seen, axis=0, keepdims=True))
            scanned[pl.ds(first, 8), :] = jnp.concatenate(sums, axis=0)
            return state

        lax.fori_loop(0, SECTION // 8, eight, state)
        return carry

    lax.fori_loop(0, DOCS, document, 0)
    gate = jnp.dot(document_major(False), zin[...], preferred_element_type=F32)
    mixed = (scanned[...] + skip[...] * inner[...].astype(F32)) * jax.nn.silu(gate)
    ordered = jnp.dot(
        document_major(True), mixed.astype(BF16), preferred_element_type=F32
    ).astype(BF16)
    copy.wait()
    for low in range(0, D, 1024):
        rows[:, low : low + 1024] = jnp.dot(
            ordered, weight[:, low : low + 1024], preferred_element_type=F32
        ).astype(BF16)


def whole(space=None):
    return pl.BlockSpec(memory_space=pltpu.VMEM if space is None else space)


def mixer_in(xin, edge, conv_weight, conv_bias, xproj):
    channels = xin.shape[1]
    return pl.pallas_call(
        mixer_in_kernel,
        out_shape=(
            jax.ShapeDtypeStruct((TOKENS, channels), BF16),
            jax.ShapeDtypeStruct((TOKENS, xproj.shape[1]), BF16),
        ),
        in_specs=[whole()] * 5,
        out_specs=(whole(), whole()),
        scratch_shapes=[pltpu.VMEM((16 + TOKENS, channels), F32)],
        compiler_params=pltpu.CompilerParams(vmem_limit_bytes=16 << 20),
        name="mixer_in",
    )(xin, edge, conv_weight, conv_bias, xproj)


def section_scan(parts, dtproj, dt_bias, a_log, inner):
    channels = inner.shape[1]
    return pl.pallas_call(
        section_kernel,
        out_shape=(
            jax.ShapeDtypeStruct((TOKENS, channels), F32),
            jax.ShapeDtypeStruct((TOKENS, LANES), BF16),
            jax.ShapeDtypeStruct((DOCS * (STATE + 2), channels), BF16),
        ),
        in_specs=[whole()] * 8,
        out_specs=(whole(),) * 3,
        scratch_shapes=[
            pltpu.VMEM((TOKENS, channels), F32),
            pltpu.VMEM((TOKENS * STATE, LANES), F32),
        ],
        compiler_params=pltpu.CompilerParams(vmem_limit_bytes=16 << 20),
        name="section_scan",
    )(*parts, dtproj, dt_bias, a_log, inner)


def mixer_out(place, gathered, step, pairs, inner, a_log, skip, zin, out_weight):
    channels = inner.shape[1]
    return pl.pallas_call(
        mixer_out_kernel,
        out_shape=jax.ShapeDtypeStruct((TOKENS, D), BF16),
        in_specs=[whole(pltpu.SMEM)] + [whole()] * 7 + [whole(pl.ANY)],
        out_specs=whole(),
        scratch_shapes=[
            pltpu.VMEM((64, channels), F32),
            pltpu.VMEM((TOKENS, channels), F32),
            pltpu.VMEM((TOKENS * STATE, LANES), F32),
            pltpu.VMEM((TOKENS * STATE, LANES), F32),
            pltpu.VMEM((TOKENS, channels), F32),
            pltpu.VMEM(out_weight.shape, BF16),
            pltpu.SemaphoreType.DMA,
        ],
        compiler_params=pltpu.CompilerParams(vmem_limit_bytes=32 << 20),
        name="mixer_out",
    )(place, gathered, step, pairs, inner, a_log, skip, zin, out_weight)


def expert_kernel(count, *refs):
    inputs, (w_gate, w_up, w_down, mine, other, rows, total) = refs[:count], refs[count:]
    block = pl.program_id(0)
    last = pl.num_programs(0) - 1
    size = rows.shape[0]

    @pl.when(block == 0)
    def _():
        low = 0
        for part in inputs:
            rows[low : low + part.shape[0], :] = part[...]
            low += part.shape[0]

    def tile(index, carry):
        place = pl.ds(pl.multiple_of(index * 256, 256), 256)
        these = rows[place, :]
        gate_act = jnp.dot(these, w_gate[...], preferred_element_type=F32)
        up_act = jnp.dot(these, w_up[...], preferred_element_type=F32)
        hidden = (jax.nn.silu(gate_act) * up_act).astype(BF16)
        for low in range(0, D, 1024):
            term = jnp.dot(hidden, w_down[:, low : low + 1024], preferred_element_type=F32)
            before = jnp.where(block == 0, 0.0, total[place, low : low + 1024])
            total[place, low : low + 1024] = before + term
        return carry

    lax.fori_loop(0, size // 256, tile, 0)

    @pl.when(block == last)
    def _():
        mine[...] = total[: size // 2, :].astype(BF16)
        other[...] = total[size // 2 :, :].astype(BF16)


def expert_block(parts, w_gate, w_up, w_down):
    size = sum(part.shape[0] for part in parts)
    units, width = w_down.shape[1], 256

    def once(shape):
        return pl.BlockSpec(shape, lambda i: (0, 0), pipeline_mode=pl.Buffered(1))

    return pl.pallas_call(
        lambda *refs: expert_kernel(len(parts), *refs),
        out_shape=(jax.ShapeDtypeStruct((size // 2, D), BF16),) * 2,
        grid=(units // width,),
        in_specs=[once(part.shape) for part in parts]
        + [pl.BlockSpec((pl.Squeezed(), D, width), lambda i: (0, 0, i))] * 2
        + [pl.BlockSpec((pl.Squeezed(), width, D), lambda i: (0, i, 0))],
        out_specs=(once((size // 2, D)),) * 2,
        scratch_shapes=[pltpu.VMEM((size, D), BF16), pltpu.VMEM((size, D), F32)],
        compiler_params=pltpu.CompilerParams(
            dimension_semantics=("arbitrary",), vmem_limit_bytes=48 << 20
        ),
        cost_estimate=pl.CostEstimate(
            flops=6 * size * D * units,
            bytes_accessed=6 * D * units + 4 * size * D,
            transcendentals=size * units,
        ),
        name=f"experts_{size}",
    )(*parts, w_gate, w_up, w_down)


def slot_select(route_ids, capacity):
    flat_ids = route_ids.reshape(-1)
    onehot = (flat_ids[:, None] == jnp.arange(EXPERTS, dtype=jnp.int32)[None, :]).astype(jnp.int32)
    before = jnp.sum((jnp.cumsum(onehot, axis=0) - onehot) * onehot, axis=1)
    target = flat_ids * capacity + before
    matches = jnp.arange(EXPERTS * capacity, dtype=jnp.int32)[:, None] == target[None, :]
    return matches.reshape(EXPERTS * capacity, route_ids.shape[0], route_ids.shape[1])


def experts(own, w_gate, w_up, w_down):
    half = own.shape[0] // 2
    count = own.shape[0]

    def paired(mine, other):
        return (mine.astype(F32) + swapped(other).astype(F32)).astype(BF16)

    left = lax.ppermute(own, "seq", x_shift(1))
    right = lax.ppermute(own, "seq", x_shift(-1))
    own_mine, own_other = expert_block([own, swapped(own)], w_gate, w_up, w_down)
    left, right, own_mine, own_other = lax.optimization_barrier((left, right, own_mine, own_other))
    far = [
        lax.ppermute(left[:half], "seq", x_shift(1)),
        lax.ppermute(right[half:], "seq", x_shift(-1)),
    ]
    near_parts = [left, right, swapped(left), swapped(right)]
    near_mine, near_other = expert_block(near_parts, w_gate, w_up, w_down)
    own_sum = paired(own_mine, own_other)
    near = paired(near_mine, near_other)
    far = far + [swapped(part) for part in far]
    near, own_sum, *far = lax.optimization_barrier((near, own_sum, *far))
    from_right = lax.ppermute(near[:count], "seq", x_shift(-1))
    from_left = lax.ppermute(near[count:], "seq", x_shift(1))
    far_mine, far_other = expert_block(far, w_gate, w_up, w_down)
    from_far = lax.ppermute(paired(far_mine, far_other), "seq", x_shift(2))
    return (
        own_sum.astype(F32)
        + from_left.astype(F32)
        + from_right.astype(F32)
        + from_far.astype(F32)
    )


def per_device(
    xin,
    zin,
    conv_weight,
    conv_bias,
    xproj_weight,
    dtproj_weight,
    dt_bias,
    a_log,
    skip,
    out_weight,
    resid,
    norm_gain,
    expert_ids,
    gate_weights,
    w_gate,
    w_up,
    w_down,
):
    channels = xin.shape[2]
    xin = xin.reshape(TOKENS, channels)
    edge = passed_along(xin[TOKENS - (CONV - 1) * DOCS :], "seq", 1)
    inner, projected = mixer_in(xin, edge, conv_weight, conv_bias[None], xproj_weight)
    along_z = [projected] + from_others(projected, z_shift)
    projected = sum(part.astype(F32) for part in along_z).astype(BF16)
    parts = [projected] + from_others(projected, y_shift)
    step, pairs, packed = section_scan(parts, dtproj_weight, dt_bias[None], a_log, inner)
    gathered = lax.all_gather(packed, "seq")
    place = lax.axis_index("seq").reshape(1)
    partial_rows = mixer_out(
        place,
        gathered,
        step,
        pairs,
        inner,
        a_log,
        skip[None],
        zin.reshape(TOKENS, channels),
        out_weight,
    )
    exchanged = lax.all_to_all(partial_rows, "exp", split_axis=0, concat_axis=0, tiled=True)
    row_count = resid.shape[0] * resid.shape[1]
    mamba_rows = jnp.sum(exchanged.reshape(-1, row_count, D).astype(F32), axis=0)
    hidden_state = resid.reshape(row_count, D).astype(F32) + mamba_rows
    norm_scale = lax.rsqrt(jnp.mean(hidden_state * hidden_state, axis=-1, keepdims=True) + 1e-05)
    tokens = (hidden_state * norm_scale * norm_gain).astype(BF16)
    capacity = 2 * TOPK * row_count // EXPERTS
    splits = lax.axis_size("exp") // EXPERTS
    route_ids = expert_ids.reshape(row_count, TOPK)
    gate_vals = gate_weights.reshape(row_count, TOPK)
    matches = slot_select(route_ids, capacity)
    chosen = jnp.sum(matches.astype(jnp.int32), axis=2).astype(BF16)
    outgoing = jnp.dot(chosen, tokens, preferred_element_type=F32).astype(BF16)
    arrived = lax.all_to_all(
        jnp.tile(outgoing, (splits, 1)), "exp", split_axis=0, concat_axis=0, tiled=True
    )
    own_rows = experts(arrived, w_gate, w_up, w_down)
    returned = lax.all_to_all(
        own_rows.astype(BF16), "exp", split_axis=0, concat_axis=0, tiled=True
    ).astype(F32)
    summed = jnp.sum(returned.reshape(splits, EXPERTS * capacity, D), axis=0)
    weights = jnp.sum(matches.astype(F32) * gate_vals.astype(F32)[None], axis=2)
    expert_out = jnp.dot(weights.T, summed, precision=lax.Precision.HIGHEST)
    return (hidden_state + expert_out).astype(BF16).reshape(resid.shape)


def solution(mesh):
    placed = (
        P("seq", None, "exp"),
        P("seq", None, "exp"),
        P(None, "exp"),
        P("exp"),
        P("exp", None),
        P(None, "exp"),
        P("exp"),
        P(None, "exp"),
        P("exp"),
        P("exp", None),
        P(("seq", "exp"), None, None),
        P(),
        P(("seq", "exp"), None, None),
        P(("seq", "exp"), None, None),
        P("exp", None, "seq"),
        P("exp", None, "seq"),
        P("exp", "seq", None),
    )
    return jax.shard_map(
        per_device,
        mesh=mesh,
        in_specs=placed,
        out_specs=P(("seq", "exp"), None, None),
        check_vma=False,
    )
```

```python
import jax
import jax.numpy as jnp
from jax import lax
from jax.experimental import pallas as pl
from jax.experimental.pallas import tpu as pltpu
from jax.sharding import PartitionSpec as P

D = 4096
STATE = 16
CONV = 4
RANK = 256
EXPERTS = 8
TOPK = 2
DOCS = 4
SECTION = 64
TOKENS = DOCS * SECTION
LANES = 128
F32 = jnp.float32
BF16 = jnp.bfloat16


def z_shift(by):
    return [(y * 4 + z, y * 4 + (z + by) % 4) for y in range(4) for z in range(4)]


def y_shift(by):
    return [(y * 4 + z, (y + by) % 4 * 4 + z) for y in range(4) for z in range(4)]


def x_shift(by):
    return [(x * 2 + c, (x + by) % 4 * 2 + c) for x in range(4) for c in range(2)]


CORE = [(x * 2 + c, x * 2 + 1 - c) for x in range(4) for c in range(2)]


def passed_along(value, axis, by):
    count = lax.axis_size(axis)
    pairs = [(i, i + by) for i in range(count) if 0 <= i + by < count]
    return lax.ppermute(value, axis, pairs)


def from_others(value, shift):
    return [lax.ppermute(value, "exp", shift(by)) for by in (1, 2, 3)]


def swapped(value):
    return lax.ppermute(value, "seq", CORE)


def document_major(back):
    row = lax.broadcasted_iota(jnp.int32, (TOKENS, TOKENS), 0)
    column = lax.broadcasted_iota(jnp.int32, (TOKENS, TOKENS), 1)
    if back:
        source = (row & (DOCS - 1)) * SECTION + (row >> 2)
    else:
        source = (row & (SECTION - 1)) * DOCS + (row >> 6)
    return jnp.where(column == source, 1.0, 0.0).astype(BF16)


def mixer_in_kernel(xin, edge, conv_weight, conv_bias, xproj, inner, projected, window):
    window[16 - edge.shape[0] : 16, :] = edge[...].astype(F32)
    window[16 : 16 + TOKENS, :] = xin[...].astype(F32)
    blocks = []
    for low in range(0, TOKENS, 64):
        running = jnp.broadcast_to(conv_bias[...], (64, xin.shape[1]))
        for offset in range(CONV):
            tap = window[pl.ds(low + 16 - DOCS * (CONV - 1 - offset), 64), :]
            running = running + conv_weight[offset : offset + 1, :] * tap
        blocks.append(jax.nn.silu(running).astype(BF16))
    by_position = jnp.concatenate(blocks, axis=0)
    ordered = jnp.dot(document_major(False), by_position, preferred_element_type=F32).astype(BF16)
    inner[...] = ordered
    projected[...] = jnp.dot(ordered, xproj[...], preferred_element_type=F32).astype(BF16)


def spread(pairs, target, first):
    lane = lax.broadcasted_iota(jnp.int32, (STATE, LANES), 1)
    entry = lax.broadcasted_iota(jnp.int32, (STATE, LANES), 0)
    mask = jnp.where((lane == first + entry) | (lane == first + STATE + entry), 1.0, 0.0)
    ones = jnp.ones((LANES, LANES), BF16)

    def one(group, carry):
        rows = pairs[pl.ds(pl.multiple_of(group * 16, 16), 16), :].astype(F32)
        wide = jnp.broadcast_to(rows[:, None, :], (16, STATE, LANES)) * mask[None]
        wide = wide.reshape(16 * STATE, LANES).astype(BF16)
        place = pl.ds(pl.multiple_of(group * 16 * STATE, 16 * STATE), 16 * STATE)
        target[place, :] = jnp.dot(wide, ones, preferred_element_type=F32)
        return carry

    lax.fori_loop(0, TOKENS // 16, one, 0)


def four_times(block):
    return jnp.concatenate([block] * 4, axis=1)


def section_kernel(
    p0, p1, p2, p3, dtproj, dt_bias, a_log, inner, step, pairs, packed, taken, entering
):
    total = (p0[...].astype(F32) + p1[...].astype(F32)) + (
        p2[...].astype(F32) + p3[...].astype(F32)
    )
    low_rank = total[:, :RANK].astype(BF16)
    states = total[:, RANK : RANK + 2 * STATE]
    high = states.astype(BF16)
    low = (states - high.astype(F32)).astype(BF16)
    pairs[...] = jnp.concatenate(
        [
            high[:, :STATE],
            low[:, :STATE],
            high[:, STATE:],
            low[:, STATE:],
            jnp.zeros((TOKENS, LANES - 4 * STATE), BF16),
        ],
        axis=1,
    )
    step[...] = jax.nn.softplus(
        jnp.dot(low_rank, dtproj[...], preferred_element_type=F32) + dt_bias[...]
    )
    taken[...] = step[...] * inner[...].astype(F32)
    spread(pairs, entering, 0)
    rate = -jnp.exp(a_log[...])

    def document(doc, carry):
        def eight(group, state):
            first = pl.multiple_of(doc * SECTION + group * 8, 8)
            steps = step[pl.ds(first, 8), :]
            values = taken[pl.ds(first, 8), :]
            for i in range(8):
                into = entering[pl.ds(pl.multiple_of((first + i) * STATE, STATE), STATE), :]
                factor = jnp.exp(steps[i : i + 1] * rate)
                state = factor * state + values[i : i + 1] * four_times(into)
            return state

        state = lax.fori_loop(0, SECTION // 8, eight, jnp.zeros(rate.shape, F32))
        packed[pl.ds(pl.multiple_of(doc * STATE, STATE), STATE), :] = state.astype(BF16)
        return carry

    lax.fori_loop(0, DOCS, document, 0)
    sums = jnp.concatenate(
        [
            jnp.sum(step[doc * SECTION : (doc + 1) * SECTION, :], axis=0, keepdims=True)
            for doc in range(DOCS)
        ],
        axis=0,
    )
    high = sums.astype(BF16).astype(F32)
    both = jnp.concatenate([high, sums - high], axis=0)
    packed[DOCS * STATE : DOCS * STATE + 2 * DOCS, :] = both.astype(BF16)


def mixer_out_kernel(
    place,
    gathered,
    step,
    pairs,
    inner,
    a_log,
    skip,
    zin,
    out_weight,
    rows,
    totals,
    taken,
    entering,
    leaving,
    scanned,
    weight,
    arrived,
):
    copy = pltpu.make_async_copy(out_weight, weight, arrived)
    copy.start()
    sections = gathered.shape[0]
    for section in range(sections - 1):
        both = gathered[section, DOCS * STATE : DOCS * STATE + 2 * DOCS, :].astype(F32)
        totals[8 * section : 8 * section + DOCS, :] = both[:DOCS] + both[DOCS:]
    taken[...] = step[...] * inner[...].astype(F32)
    spread(pairs, entering, 0)
    spread(pairs, leaving, 2 * STATE)
    rate = -jnp.exp(a_log[...])

    def document(doc, carry):
        state = jnp.zeros(rate.shape, F32)
        for section in range(sections - 1):
            total = totals[pl.ds(8 * section + doc, 1), :]
            final = gathered[section, pl.ds(pl.multiple_of(doc * STATE, STATE), STATE), :]
            later = jnp.exp(total * rate) * state + final.astype(F32)
            state = jnp.where(section < place[0], later, state)

        def eight(group, state):
            first = pl.multiple_of(doc * SECTION + group * 8, 8)
            steps = step[pl.ds(first, 8), :]
            values = taken[pl.ds(first, 8), :]
            sums = []
            for i in range(8):
                where = pl.ds(pl.multiple_of((first + i) * STATE, STATE), STATE)
                factor = jnp.exp(steps[i : i + 1] * rate)
                state = factor * state + values[i : i + 1] * four_times(entering[where, :])
                seen = state * four_times(leaving[where, :])
                sums.append(jnp.sum(seen, axis=0, keepdims=True))
            scanned[pl.ds(first, 8), :] = jnp.concatenate(sums, axis=0)
            return state

        lax.fori_loop(0, SECTION // 8, eight, state)
        return carry

    lax.fori_loop(0, DOCS, document, 0)
    gate = jnp.dot(document_major(False), zin[...], preferred_element_type=F32)
    mixed = (scanned[...] + skip[...] * inner[...].astype(F32)) * jax.nn.silu(gate)
    ordered = jnp.dot(
        document_major(True), mixed.astype(BF16), preferred_element_type=F32
    ).astype(BF16)
    copy.wait()
    for low in range(0, D, 1024):
        rows[:, low : low + 1024] = jnp.dot(
            ordered, weight[:, low : low + 1024], preferred_element_type=F32
        ).astype(BF16)


def whole(space=None):
    return pl.BlockSpec(memory_space=pltpu.VMEM if space is None else space)


def mixer_in(xin, edge, conv_weight, conv_bias, xproj):
    channels = xin.shape[1]
    return pl.pallas_call(
        mixer_in_kernel,
        out_shape=(
            jax.ShapeDtypeStruct((TOKENS, channels), BF16),
            jax.ShapeDtypeStruct((TOKENS, xproj.shape[1]), BF16),
        ),
        in_specs=[whole()] * 5,
        out_specs=(whole(), whole()),
        scratch_shapes=[pltpu.VMEM((16 + TOKENS, channels), F32)],
        compiler_params=pltpu.CompilerParams(vmem_limit_bytes=16 << 20),
        name="mixer_in",
    )(xin, edge, conv_weight, conv_bias, xproj)


def section_scan(parts, dtproj, dt_bias, a_log, inner):
    channels = inner.shape[1]
    return pl.pallas_call(
        section_kernel,
        out_shape=(
            jax.ShapeDtypeStruct((TOKENS, channels), F32),
            jax.ShapeDtypeStruct((TOKENS, LANES), BF16),
            jax.ShapeDtypeStruct((DOCS * (STATE + 2), channels), BF16),
        ),
        in_specs=[whole()] * 8,
        out_specs=(whole(),) * 3,
        scratch_shapes=[
            pltpu.VMEM((TOKENS, channels), F32),
            pltpu.VMEM((TOKENS * STATE, LANES), F32),
        ],
        compiler_params=pltpu.CompilerParams(vmem_limit_bytes=16 << 20),
        name="section_scan",
    )(*parts, dtproj, dt_bias, a_log, inner)


def mixer_out(place, gathered, step, pairs, inner, a_log, skip, zin, out_weight):
    channels = inner.shape[1]
    return pl.pallas_call(
        mixer_out_kernel,
        out_shape=jax.ShapeDtypeStruct((TOKENS, D), BF16),
        in_specs=[whole(pltpu.SMEM)] + [whole()] * 7 + [whole(pl.ANY)],
        out_specs=whole(),
        scratch_shapes=[
            pltpu.VMEM((64, channels), F32),
            pltpu.VMEM((TOKENS, channels), F32),
            pltpu.VMEM((TOKENS * STATE, LANES), F32),
            pltpu.VMEM((TOKENS * STATE, LANES), F32),
            pltpu.VMEM((TOKENS, channels), F32),
            pltpu.VMEM(out_weight.shape, BF16),
            pltpu.SemaphoreType.DMA,
        ],
        compiler_params=pltpu.CompilerParams(vmem_limit_bytes=32 << 20),
        name="mixer_out",
    )(place, gathered, step, pairs, inner, a_log, skip, zin, out_weight)


def expert_kernel(count, *refs):
    inputs, (w_gate, w_up, w_down, mine, other, rows, total) = refs[:count], refs[count:]
    block = pl.program_id(0)
    last = pl.num_programs(0) - 1
    size = rows.shape[0]

    @pl.when(block == 0)
    def _():
        low = 0
        for part in inputs:
            rows[low : low + part.shape[0], :] = part[...]
            low += part.shape[0]

    def tile(index, carry):
        place = pl.ds(pl.multiple_of(index * 256, 256), 256)
        these = rows[place, :]
        gate_act = jnp.dot(these, w_gate[...], preferred_element_type=F32)
        up_act = jnp.dot(these, w_up[...], preferred_element_type=F32)
        hidden = (jax.nn.silu(gate_act) * up_act).astype(BF16)
        for low in range(0, D, 1024):
            term = jnp.dot(hidden, w_down[:, low : low + 1024], preferred_element_type=F32)
            before = jnp.where(block == 0, 0.0, total[place, low : low + 1024])
            total[place, low : low + 1024] = before + term
        return carry

    lax.fori_loop(0, size // 256, tile, 0)

    @pl.when(block == last)
    def _():
        mine[...] = total[: size // 2, :].astype(BF16)
        other[...] = total[size // 2 :, :].astype(BF16)


def expert_block(parts, w_gate, w_up, w_down):
    size = sum(part.shape[0] for part in parts)
    units, width = w_down.shape[1], 256

    def once(shape):
        return pl.BlockSpec(shape, lambda i: (0, 0), pipeline_mode=pl.Buffered(1))

    return pl.pallas_call(
        lambda *refs: expert_kernel(len(parts), *refs),
        out_shape=(jax.ShapeDtypeStruct((size // 2, D), BF16),) * 2,
        grid=(units // width,),
        in_specs=[once(part.shape) for part in parts]
        + [pl.BlockSpec((pl.Squeezed(), D, width), lambda i: (0, 0, i))] * 2
        + [pl.BlockSpec((pl.Squeezed(), width, D), lambda i: (0, i, 0))],
        out_specs=(once((size // 2, D)),) * 2,
        scratch_shapes=[pltpu.VMEM((size, D), BF16), pltpu.VMEM((size, D), F32)],
        compiler_params=pltpu.CompilerParams(
            dimension_semantics=("arbitrary",), vmem_limit_bytes=48 << 20
        ),
        cost_estimate=pl.CostEstimate(
            flops=6 * size * D * units,
            bytes_accessed=6 * D * units + 4 * size * D,
            transcendentals=size * units,
        ),
        name=f"experts_{size}",
    )(*parts, w_gate, w_up, w_down)


def slot_select(route_ids, capacity):
    flat_ids = route_ids.reshape(-1)
    onehot = (flat_ids[:, None] == jnp.arange(EXPERTS, dtype=jnp.int32)[None, :]).astype(jnp.int32)
    before = jnp.sum((jnp.cumsum(onehot, axis=0) - onehot) * onehot, axis=1)
    target = flat_ids * capacity + before
    matches = jnp.arange(EXPERTS * capacity, dtype=jnp.int32)[:, None] == target[None, :]
    return matches.reshape(EXPERTS * capacity, route_ids.shape[0], route_ids.shape[1])


def after(values, *others):
    held = lax.optimization_barrier((tuple(values), others))
    return held[0]


def experts(own, w_gate, w_up, w_down):
    count = own.shape[0]
    half = count // 2

    def paired(mine, other):
        return mine.astype(F32) + swapped(other).astype(F32)

    left = lax.ppermute(own, "seq", x_shift(1))
    right = lax.ppermute(own, "seq", x_shift(-1))
    own_out = expert_block([own, swapped(own)], w_gate, w_up, w_down)
    left, right = after((left, right), own_out)
    far = [
        lax.ppermute(left[:half], "seq", x_shift(1)),
        lax.ppermute(right[half:], "seq", x_shift(-1)),
    ]
    near_parts = [left, right, swapped(left), swapped(right)]
    far_out = expert_block(far + [swapped(part) for part in far], w_gate, w_up, w_down)
    far_sum = paired(*far_out).astype(BF16)
    for_right = lax.ppermute(far_sum[:half], "seq", x_shift(1))
    for_left = lax.ppermute(far_sum[half:], "seq", x_shift(-1))
    near_out = expert_block(near_parts, w_gate, w_up, w_down)
    near_out = after(near_out, for_right, for_left)
    near = paired(*near_out)
    to_left = near[:count] + jnp.concatenate([jnp.zeros((half, D), F32), for_left.astype(F32)])
    to_right = near[count:] + jnp.concatenate([for_right.astype(F32), jnp.zeros((half, D), F32)])
    from_right = lax.ppermute(to_left.astype(BF16), "seq", x_shift(-1))
    from_left = lax.ppermute(to_right.astype(BF16), "seq", x_shift(1))
    return paired(*own_out) + from_left.astype(F32) + from_right.astype(F32)


def per_device(
    xin,
    zin,
    conv_weight,
    conv_bias,
    xproj_weight,
    dtproj_weight,
    dt_bias,
    a_log,
    skip,
    out_weight,
    resid,
    norm_gain,
    expert_ids,
    gate_weights,
    w_gate,
    w_up,
    w_down,
):
    channels = xin.shape[2]
    xin = xin.reshape(TOKENS, channels)
    edge = passed_along(xin[TOKENS - (CONV - 1) * DOCS :], "seq", 1)
    inner, projected = mixer_in(xin, edge, conv_weight, conv_bias[None], xproj_weight)
    along_z = [projected] + from_others(projected, z_shift)
    projected = sum(part.astype(F32) for part in along_z).astype(BF16)
    parts = [projected] + from_others(projected, y_shift)
    step, pairs, packed = section_scan(parts, dtproj_weight, dt_bias[None], a_log, inner)
    gathered = lax.all_gather(packed, "seq")
    place = lax.axis_index("seq").reshape(1)
    partial_rows = mixer_out(
        place,
        gathered,
        step,
        pairs,
        inner,
        a_log,
        skip[None],
        zin.reshape(TOKENS, channels),
        out_weight,
    )
    exchanged = lax.all_to_all(partial_rows, "exp", split_axis=0, concat_axis=0, tiled=True)
    row_count = resid.shape[0] * resid.shape[1]
    mamba_rows = jnp.sum(exchanged.reshape(-1, row_count, D).astype(F32), axis=0)
    hidden_state = resid.reshape(row_count, D).astype(F32) + mamba_rows
    norm_scale = lax.rsqrt(jnp.mean(hidden_state * hidden_state, axis=-1, keepdims=True) + 1e-05)
    tokens = (hidden_state * norm_scale * norm_gain).astype(BF16)
    capacity = 2 * TOPK * row_count // EXPERTS
    splits = lax.axis_size("exp") // EXPERTS
    route_ids = expert_ids.reshape(row_count, TOPK)
    gate_vals = gate_weights.reshape(row_count, TOPK)
    matches = slot_select(route_ids, capacity)
    chosen = jnp.sum(matches.astype(jnp.int32), axis=2).astype(BF16)
    outgoing = jnp.dot(chosen, tokens, preferred_element_type=F32).astype(BF16)
    arrived = lax.all_to_all(
        jnp.tile(outgoing, (splits, 1)), "exp", split_axis=0, concat_axis=0, tiled=True
    )
    own_rows = experts(arrived, w_gate, w_up, w_down)
    returned = lax.all_to_all(
        own_rows.astype(BF16), "exp", split_axis=0, concat_axis=0, tiled=True
    ).astype(F32)
    summed = jnp.sum(returned.reshape(splits, EXPERTS * capacity, D), axis=0)
    weights = jnp.sum(matches.astype(F32) * gate_vals.astype(F32)[None], axis=2)
    expert_out = jnp.dot(weights.T, summed, precision=lax.Precision.HIGHEST)
    return (hidden_state + expert_out).astype(BF16).reshape(resid.shape)


def solution(mesh):
    placed = (
        P("seq", None, "exp"),
        P("seq", None, "exp"),
        P(None, "exp"),
        P("exp"),
        P("exp", None),
        P(None, "exp"),
        P("exp"),
        P(None, "exp"),
        P("exp"),
        P("exp", None),
        P(("seq", "exp"), None, None),
        P(),
        P(("seq", "exp"), None, None),
        P(("seq", "exp"), None, None),
        P("exp", None, "seq"),
        P("exp", None, "seq"),
        P("exp", "seq", None),
    )
    return jax.shard_map(
        per_device,
        mesh=mesh,
        in_specs=placed,
        out_specs=P(("seq", "exp"), None, None),
        check_vma=False,
    )
```

```python
import jax
import jax.numpy as jnp
from jax import lax
from jax.experimental import pallas as pl
from jax.experimental.pallas import tpu as pltpu
from jax.sharding import PartitionSpec as P

D = 4096
STATE = 16
CONV = 4
RANK = 256
EXPERTS = 8
TOPK = 2
DOCS = 4
SECTION = 64
TOKENS = DOCS * SECTION
LANES = 128
F32 = jnp.float32
BF16 = jnp.bfloat16


def z_shift(by):
    return [(y * 4 + z, y * 4 + (z + by) % 4) for y in range(4) for z in range(4)]


def y_shift(by):
    return [(y * 4 + z, (y + by) % 4 * 4 + z) for y in range(4) for z in range(4)]


def x_shift(by):
    return [(x * 2 + c, (x + by) % 4 * 2 + c) for x in range(4) for c in range(2)]


def x_onward(by):
    return [(x * 2 + c, (x + by) * 2 + c) for x in range(4 - by) for c in range(2)]


CORE = [(x * 2 + c, x * 2 + 1 - c) for x in range(4) for c in range(2)]


def passed_along(value, axis, by):
    count = lax.axis_size(axis)
    pairs = [(i, i + by) for i in range(count) if 0 <= i + by < count]
    return lax.ppermute(value, axis, pairs)


def from_others(value, shift):
    return [lax.ppermute(value, "exp", shift(by)) for by in (1, 2, 3)]


def swapped(value):
    return lax.ppermute(value, "seq", CORE)


def document_major(back):
    row = lax.broadcasted_iota(jnp.int32, (TOKENS, TOKENS), 0)
    column = lax.broadcasted_iota(jnp.int32, (TOKENS, TOKENS), 1)
    if back:
        source = (row & (DOCS - 1)) * SECTION + (row >> 2)
    else:
        source = (row & (SECTION - 1)) * DOCS + (row >> 6)
    return jnp.where(column == source, 1.0, 0.0).astype(BF16)


def mixer_in_kernel(xin, edge, conv_weight, conv_bias, xproj, inner, projected, window):
    window[16 - edge.shape[0] : 16, :] = edge[...].astype(F32)
    window[16 : 16 + TOKENS, :] = xin[...].astype(F32)
    blocks = []
    for low in range(0, TOKENS, 64):
        running = jnp.broadcast_to(conv_bias[...], (64, xin.shape[1]))
        for offset in range(CONV):
            tap = window[pl.ds(low + 16 - DOCS * (CONV - 1 - offset), 64), :]
            running = running + conv_weight[offset : offset + 1, :] * tap
        blocks.append(jax.nn.silu(running).astype(BF16))
    by_position = jnp.concatenate(blocks, axis=0)
    ordered = jnp.dot(document_major(False), by_position, preferred_element_type=F32).astype(BF16)
    inner[...] = ordered
    projected[...] = lax.dot_general(
        xproj[...], ordered, (((1,), (1,)), ((), ())), preferred_element_type=F32
    ).astype(BF16)


def spread(pairs, target, first):
    lane = lax.broadcasted_iota(jnp.int32, (STATE, LANES), 1)
    entry = lax.broadcasted_iota(jnp.int32, (STATE, LANES), 0)
    mask = jnp.where((lane == first + entry) | (lane == first + STATE + entry), 1.0, 0.0)
    ones = jnp.ones((LANES, LANES), BF16)

    def one(group, carry):
        rows = pairs[pl.ds(pl.multiple_of(group * 16, 16), 16), :].astype(F32)
        wide = jnp.broadcast_to(rows[:, None, :], (16, STATE, LANES)) * mask[None]
        wide = wide.reshape(16 * STATE, LANES).astype(BF16)
        place = pl.ds(pl.multiple_of(group * 16 * STATE, 16 * STATE), 16 * STATE)
        target[place, :] = jnp.dot(wide, ones, preferred_element_type=F32)
        return carry

    lax.fori_loop(0, TOKENS // 16, one, 0)


def four_times(block):
    return jnp.concatenate([block] * 4, axis=1)


def section_kernel(
    p0, p1, p2, p3, dtproj, dt_bias, a_log, inner, step, pairs, packed, taken, entering
):
    total = (p0[...].astype(F32) + p1[...].astype(F32)) + (
        p2[...].astype(F32) + p3[...].astype(F32)
    )
    low_rank = total[:RANK].astype(BF16)
    states = total[RANK : RANK + 2 * STATE].T
    high = states.astype(BF16)
    low = (states - high.astype(F32)).astype(BF16)
    pairs[...] = jnp.concatenate(
        [
            high[:, :STATE],
            low[:, :STATE],
            high[:, STATE:],
            low[:, STATE:],
            jnp.zeros((TOKENS, LANES - 4 * STATE), BF16),
        ],
        axis=1,
    )
    step[...] = jax.nn.softplus(
        lax.dot_general(
            low_rank, dtproj[...], (((0,), (0,)), ((), ())), preferred_element_type=F32
        )
        + dt_bias[...]
    )
    taken[...] = step[...] * inner[...].astype(F32)
    spread(pairs, entering, 0)
    rate = -jnp.exp(a_log[...])

    def document(doc, carry):
        def eight(group, state):
            first = pl.multiple_of(doc * SECTION + group * 8, 8)
            steps = step[pl.ds(first, 8), :]
            values = taken[pl.ds(first, 8), :]
            for i in range(8):
                into = entering[pl.ds(pl.multiple_of((first + i) * STATE, STATE), STATE), :]
                factor = jnp.exp(steps[i : i + 1] * rate)
                state = factor * state + values[i : i + 1] * four_times(into)
            return state

        state = lax.fori_loop(0, SECTION // 8, eight, jnp.zeros(rate.shape, F32))
        packed[pl.ds(pl.multiple_of(doc * STATE, STATE), STATE), :] = state.astype(BF16)
        return carry

    lax.fori_loop(0, DOCS, document, 0)
    sums = jnp.concatenate(
        [
            jnp.sum(step[doc * SECTION : (doc + 1) * SECTION, :], axis=0, keepdims=True)
            for doc in range(DOCS)
        ],
        axis=0,
    )
    high = sums.astype(BF16).astype(F32)
    both = jnp.concatenate([high, sums - high], axis=0)
    packed[DOCS * STATE : DOCS * STATE + 2 * DOCS, :] = both.astype(BF16)


def mixer_out_kernel(
    core,
    *refs,
):
    earlier, refs = refs[:7], refs[7:]
    (
        step,
        pairs,
        inner,
        a_log,
        skip,
        zin,
        out_weight,
        rows,
        totals,
        finals,
        taken,
        entering,
        leaving,
        scanned,
        weight,
        arrived,
    ) = refs
    copy = pltpu.make_async_copy(out_weight, weight, arrived)
    copy.start()
    first = core[0] == 0
    partner = earlier[3][...].astype(F32)
    order = [jnp.where(first, 0.0, partner)]
    for by in (1, 2, 3):
        mine, theirs = earlier[by - 1][...].astype(F32), earlier[3 + by][...].astype(F32)
        order = [jnp.where(first, mine, theirs), jnp.where(first, theirs, mine)] + order
    for index, packed in enumerate(order):
        both = packed[DOCS * STATE :]
        totals[8 * index : 8 * index + DOCS, :] = both[:DOCS] + both[DOCS:]
        finals[index] = packed[: DOCS * STATE]
    taken[...] = step[...] * inner[...].astype(F32)
    spread(pairs, entering, 0)
    spread(pairs, leaving, 2 * STATE)
    rate = -jnp.exp(a_log[...])

    def document(doc, carry):
        state = jnp.zeros(rate.shape, F32)
        for index in range(len(order)):
            total = totals[pl.ds(8 * index + doc, 1), :]
            final = finals[index, pl.ds(pl.multiple_of(doc * STATE, STATE), STATE), :]
            state = jnp.exp(total * rate) * state + final

        def eight(group, state):
            first = pl.multiple_of(doc * SECTION + group * 8, 8)
            steps = step[pl.ds(first, 8), :]
            values = taken[pl.ds(first, 8), :]
            sums = []
            for i in range(8):
                where = pl.ds(pl.multiple_of((first + i) * STATE, STATE), STATE)
                factor = jnp.exp(steps[i : i + 1] * rate)
                state = factor * state + values[i : i + 1] * four_times(entering[where, :])
                seen = state * four_times(leaving[where, :])
                sums.append(jnp.sum(seen, axis=0, keepdims=True))
            scanned[pl.ds(first, 8), :] = jnp.concatenate(sums, axis=0)
            return state

        lax.fori_loop(0, SECTION // 8, eight, state)
        return carry

    lax.fori_loop(0, DOCS, document, 0)
    gate = jnp.dot(document_major(False), zin[...], preferred_element_type=F32)
    mixed = (scanned[...] + skip[...] * inner[...].astype(F32)) * jax.nn.silu(gate)
    ordered = jnp.dot(
        document_major(True), mixed.astype(BF16), preferred_element_type=F32
    ).astype(BF16)
    copy.wait()
    for low in range(0, D, 1024):
        rows[:, low : low + 1024] = jnp.dot(
            ordered, weight[:, low : low + 1024], preferred_element_type=F32
        ).astype(BF16)


def whole(space=None):
    return pl.BlockSpec(memory_space=pltpu.VMEM if space is None else space)


def mixer_in(xin, edge, conv_weight, conv_bias, xproj):
    channels = xin.shape[1]
    return pl.pallas_call(
        mixer_in_kernel,
        out_shape=(
            jax.ShapeDtypeStruct((TOKENS, channels), BF16),
            jax.ShapeDtypeStruct((xproj.shape[0], TOKENS), BF16),
        ),
        in_specs=[whole()] * 5,
        out_specs=(whole(), whole()),
        scratch_shapes=[pltpu.VMEM((16 + TOKENS, channels), F32)],
        compiler_params=pltpu.CompilerParams(vmem_limit_bytes=16 << 20),
        name="mixer_in",
    )(xin, edge, conv_weight, conv_bias, xproj)


def section_scan(parts, dtproj, dt_bias, a_log, inner):
    channels = inner.shape[1]
    return pl.pallas_call(
        section_kernel,
        out_shape=(
            jax.ShapeDtypeStruct((TOKENS, channels), F32),
            jax.ShapeDtypeStruct((TOKENS, LANES), BF16),
            jax.ShapeDtypeStruct((DOCS * (STATE + 2), channels), BF16),
        ),
        in_specs=[whole()] * 8,
        out_specs=(whole(),) * 3,
        scratch_shapes=[
            pltpu.VMEM((TOKENS, channels), F32),
            pltpu.VMEM((TOKENS * STATE, LANES), F32),
        ],
        compiler_params=pltpu.CompilerParams(vmem_limit_bytes=16 << 20),
        name="section_scan",
    )(*parts, dtproj, dt_bias, a_log, inner)


def mixer_out(core, earlier, step, pairs, inner, a_log, skip, zin, out_weight):
    channels = inner.shape[1]
    return pl.pallas_call(
        mixer_out_kernel,
        out_shape=jax.ShapeDtypeStruct((TOKENS, D), BF16),
        in_specs=[whole(pltpu.SMEM)] + [whole()] * 13 + [whole(pl.ANY)],
        out_specs=whole(),
        scratch_shapes=[
            pltpu.VMEM((64, channels), F32),
            pltpu.VMEM((7, DOCS * STATE, channels), F32),
            pltpu.VMEM((TOKENS, channels), F32),
            pltpu.VMEM((TOKENS * STATE, LANES), F32),
            pltpu.VMEM((TOKENS * STATE, LANES), F32),
            pltpu.VMEM((TOKENS, channels), F32),
            pltpu.VMEM(out_weight.shape, BF16),
            pltpu.SemaphoreType.DMA,
        ],
        compiler_params=pltpu.CompilerParams(vmem_limit_bytes=32 << 20),
        name="mixer_out",
    )(core, *earlier, step, pairs, inner, a_log, skip, zin, out_weight)


def expert_kernel(count, *refs):
    inputs, (w_gate, w_up, w_down, mine, other, rows, total) = refs[:count], refs[count:]
    block = pl.program_id(0)
    last = pl.num_programs(0) - 1
    size = rows.shape[0]

    @pl.when(block == 0)
    def _():
        low = 0
        for part in inputs:
            rows[low : low + part.shape[0], :] = part[...]
            low += part.shape[0]

    def tile(index, carry):
        place = pl.ds(pl.multiple_of(index * 256, 256), 256)
        these = rows[place, :]
        gate_act = jnp.dot(these, w_gate[...], preferred_element_type=F32)
        up_act = jnp.dot(these, w_up[...], preferred_element_type=F32)
        hidden = (jax.nn.silu(gate_act) * up_act).astype(BF16)
        for low in range(0, D, 1024):
            term = jnp.dot(hidden, w_down[:, low : low + 1024], preferred_element_type=F32)
            before = jnp.where(block == 0, 0.0, total[place, low : low + 1024])
            total[place, low : low + 1024] = before + term
        return carry

    lax.fori_loop(0, size // 256, tile, 0)

    @pl.when(block == last)
    def _():
        mine[...] = total[: size // 2, :].astype(BF16)
        other[...] = total[size // 2 :, :].astype(BF16)


def expert_block(parts, w_gate, w_up, w_down):
    size = sum(part.shape[0] for part in parts)
    units, width = w_down.shape[1], 256

    def once(shape):
        return pl.BlockSpec(shape, lambda i: (0, 0), pipeline_mode=pl.Buffered(1))

    return pl.pallas_call(
        lambda *refs: expert_kernel(len(parts), *refs),
        out_shape=(jax.ShapeDtypeStruct((size // 2, D), BF16),) * 2,
        grid=(units // width,),
        in_specs=[once(part.shape) for part in parts]
        + [pl.BlockSpec((pl.Squeezed(), D, width), lambda i: (0, 0, i))] * 2
        + [pl.BlockSpec((pl.Squeezed(), width, D), lambda i: (0, i, 0))],
        out_specs=(once((size // 2, D)),) * 2,
        scratch_shapes=[pltpu.VMEM((size, D), BF16), pltpu.VMEM((size, D), F32)],
        compiler_params=pltpu.CompilerParams(
            dimension_semantics=("arbitrary",), vmem_limit_bytes=48 << 20
        ),
        cost_estimate=pl.CostEstimate(
            flops=6 * size * D * units,
            bytes_accessed=6 * D * units + 4 * size * D,
            transcendentals=size * units,
        ),
        name=f"experts_{size}",
    )(*parts, w_gate, w_up, w_down)


def slot_select(route_ids, capacity):
    flat_ids = route_ids.reshape(-1)
    onehot = (flat_ids[:, None] == jnp.arange(EXPERTS, dtype=jnp.int32)[None, :]).astype(jnp.int32)
    before = jnp.sum((jnp.cumsum(onehot, axis=0) - onehot) * onehot, axis=1)
    target = flat_ids * capacity + before
    matches = jnp.arange(EXPERTS * capacity, dtype=jnp.int32)[:, None] == target[None, :]
    return matches.reshape(EXPERTS * capacity, route_ids.shape[0], route_ids.shape[1])


def after(values, *others):
    held = lax.optimization_barrier((tuple(values), others))
    return held[0]


def experts(own, w_gate, w_up, w_down):
    count = own.shape[0]
    half = count // 2

    def paired(mine, other):
        return mine.astype(F32) + swapped(other).astype(F32)

    left = lax.ppermute(own, "seq", x_shift(1))
    right = lax.ppermute(own, "seq", x_shift(-1))
    own_out = expert_block([own, swapped(own)], w_gate, w_up, w_down)
    left, right = after((left, right), own_out)
    far = [
        lax.ppermute(left[:half], "seq", x_shift(1)),
        lax.ppermute(right[half:], "seq", x_shift(-1)),
    ]
    left_out = expert_block([left, swapped(left)], w_gate, w_up, w_down)
    far = list(after(far, left_out))
    far_out = expert_block(far + [swapped(part) for part in far], w_gate, w_up, w_down)
    left_out = after(left_out, far_out)
    far_sum = paired(*far_out).astype(BF16)
    for_right = lax.ppermute(far_sum[:half], "seq", x_shift(1))
    for_left = lax.ppermute(far_sum[half:], "seq", x_shift(-1))
    right_out = expert_block([right, swapped(right)], w_gate, w_up, w_down)
    right_out = after(right_out, for_right, for_left)
    nothing = jnp.zeros((half, D), F32)
    to_left = paired(*left_out) + jnp.concatenate([nothing, for_left.astype(F32)])
    to_right = paired(*right_out) + jnp.concatenate([for_right.astype(F32), nothing])
    from_right = lax.ppermute(to_left.astype(BF16), "seq", x_shift(-1))
    from_left = lax.ppermute(to_right.astype(BF16), "seq", x_shift(1))
    return paired(*own_out) + from_left.astype(F32) + from_right.astype(F32)


def per_device(
    xin,
    zin,
    conv_weight,
    conv_bias,
    xproj_weight,
    dtproj_weight,
    dt_bias,
    a_log,
    skip,
    out_weight,
    resid,
    norm_gain,
    expert_ids,
    gate_weights,
    w_gate,
    w_up,
    w_down,
):
    channels = xin.shape[2]
    xin = xin.reshape(TOKENS, channels)
    edge = passed_along(xin[TOKENS - (CONV - 1) * DOCS :], "seq", 1)
    inner, projected = mixer_in(xin, edge, conv_weight, conv_bias[None], xproj_weight.T)
    along_z = [projected] + from_others(projected, z_shift)
    projected = sum(part.astype(F32) for part in along_z).astype(BF16)
    parts = [projected] + from_others(projected, y_shift)
    step, pairs, packed = section_scan(parts, dtproj_weight, dt_bias[None], a_log, inner)
    columns = [lax.ppermute(packed, "seq", x_onward(by)) for by in (1, 2, 3)]
    partial_rows = mixer_out(
        (lax.axis_index("seq") % 2).reshape(1),
        columns + [swapped(packed)] + [swapped(column) for column in columns],
        step,
        pairs,
        inner,
        a_log,
        skip[None],
        zin.reshape(TOKENS, channels),
        out_weight,
    )
    exchanged = lax.all_to_all(partial_rows, "exp", split_axis=0, concat_axis=0, tiled=True)
    row_count = resid.shape[0] * resid.shape[1]
    mamba_rows = jnp.sum(exchanged.reshape(-1, row_count, D).astype(F32), axis=0)
    hidden_state = resid.reshape(row_count, D).astype(F32) + mamba_rows
    norm_scale = lax.rsqrt(jnp.mean(hidden_state * hidden_state, axis=-1, keepdims=True) + 1e-05)
    tokens = (hidden_state * norm_scale * norm_gain).astype(BF16)
    capacity = 2 * TOPK * row_count // EXPERTS
    splits = lax.axis_size("exp") // EXPERTS
    route_ids = expert_ids.reshape(row_count, TOPK)
    gate_vals = gate_weights.reshape(row_count, TOPK)
    matches = slot_select(route_ids, capacity)
    chosen = jnp.sum(matches.astype(jnp.int32), axis=2).astype(BF16)
    outgoing = jnp.dot(chosen, tokens, preferred_element_type=F32).astype(BF16)
    arrived = lax.all_to_all(
        jnp.tile(outgoing, (splits, 1)), "exp", split_axis=0, concat_axis=0, tiled=True
    )
    own_rows = experts(arrived, w_gate, w_up, w_down)
    returned = lax.all_to_all(
        own_rows.astype(BF16), "exp", split_axis=0, concat_axis=0, tiled=True
    ).astype(F32)
    summed = jnp.sum(returned.reshape(splits, EXPERTS * capacity, D), axis=0)
    weights = jnp.sum(matches.astype(F32) * gate_vals.astype(F32)[None], axis=2)
    expert_out = jnp.dot(weights.T, summed, precision=lax.Precision.HIGHEST)
    return (hidden_state + expert_out).astype(BF16).reshape(resid.shape)


def solution(mesh):
    placed = (
        P("seq", None, "exp"),
        P("seq", None, "exp"),
        P(None, "exp"),
        P("exp"),
        P("exp", None),
        P(None, "exp"),
        P("exp"),
        P(None, "exp"),
        P("exp"),
        P("exp", None),
        P(("seq", "exp"), None, None),
        P(),
        P(("seq", "exp"), None, None),
        P(("seq", "exp"), None, None),
        P("exp", None, "seq"),
        P("exp", None, "seq"),
        P("exp", "seq", None),
    )
    return jax.shard_map(
        per_device,
        mesh=mesh,
        in_specs=placed,
        out_specs=P(("seq", "exp"), None, None),
        check_vma=False,
    )
```

```python
import jax
import jax.numpy as jnp
from jax import lax
from jax.experimental import pallas as pl
from jax.experimental.pallas import tpu as pltpu
from jax.sharding import PartitionSpec as P

D = 4096
STATE = 16
CONV = 4
RANK = 256
EXPERTS = 8
TOPK = 2
DOCS = 4
SECTION = 64
TOKENS = DOCS * SECTION
LANES = 128
F32 = jnp.float32
BF16 = jnp.bfloat16


def z_shift(by):
    return [(y * 4 + z, y * 4 + (z + by) % 4) for y in range(4) for z in range(4)]


def y_shift(by):
    return [(y * 4 + z, (y + by) % 4 * 4 + z) for y in range(4) for z in range(4)]


def x_shift(by):
    return [(x * 2 + c, (x + by) % 4 * 2 + c) for x in range(4) for c in range(2)]


def x_onward(by):
    return [(x * 2 + c, (x + by) * 2 + c) for x in range(4 - by) for c in range(2)]


CORE = [(x * 2 + c, x * 2 + 1 - c) for x in range(4) for c in range(2)]


def passed_along(value, axis, by):
    count = lax.axis_size(axis)
    pairs = [(i, i + by) for i in range(count) if 0 <= i + by < count]
    return lax.ppermute(value, axis, pairs)


def from_others(value, shift):
    return [lax.ppermute(value, "exp", shift(by)) for by in (1, 2, 3)]


def swapped(value):
    return lax.ppermute(value, "seq", CORE)


def document_major(back):
    row = lax.broadcasted_iota(jnp.int32, (TOKENS, TOKENS), 0)
    column = lax.broadcasted_iota(jnp.int32, (TOKENS, TOKENS), 1)
    if back:
        source = (row & (DOCS - 1)) * SECTION + (row >> 2)
    else:
        source = (row & (SECTION - 1)) * DOCS + (row >> 6)
    return jnp.where(column == source, 1.0, 0.0).astype(BF16)


def fetched(sources, targets, arrived):
    copies = [
        pltpu.make_async_copy(source, target, arrived.at[index])
        for index, (source, target) in enumerate(zip(sources, targets))
    ]
    for copy in copies:
        copy.start()
    return copies


def mixer_in_kernel(xin, edge, *refs):
    sources, (inner, projected, window, *targets, arrived) = refs[:3], refs[3:]
    copies = fetched(sources, targets, arrived)
    conv_weight, conv_bias, xproj = targets
    window[16 - edge.shape[0] : 16, :] = edge[...].astype(F32)
    window[16 : 16 + TOKENS, :] = xin[...].astype(F32)
    copies[0].wait()
    copies[1].wait()
    blocks = []
    for low in range(0, TOKENS, 64):
        running = jnp.broadcast_to(conv_bias[...], (64, xin.shape[1]))
        for offset in range(CONV):
            tap = window[pl.ds(low + 16 - DOCS * (CONV - 1 - offset), 64), :]
            running = running + conv_weight[offset : offset + 1, :] * tap
        blocks.append(jax.nn.silu(running).astype(BF16))
    by_position = jnp.concatenate(blocks, axis=0)
    ordered = jnp.dot(document_major(False), by_position, preferred_element_type=F32).astype(BF16)
    inner[...] = ordered
    copies[2].wait()
    projected[...] = lax.dot_general(
        xproj[...], ordered, (((1,), (1,)), ((), ())), preferred_element_type=F32
    ).astype(BF16)


def columns_from(states, doc, group):
    block = states[:, pl.ds(pl.multiple_of((doc >> 1) * LANES, LANES), LANES)]
    offset = (doc & 1) * SECTION + group * 8
    return pltpu.roll(block, (LANES - offset) & (LANES - 1), 1)


def in_all_lanes(turned, index):
    column = jnp.broadcast_to(turned[:, index : index + 1], (turned.shape[0], LANES))
    return jnp.concatenate([column] * 4, axis=1)


def section_kernel(p0, p1, p2, p3, inner, *refs):
    sources, (step, states, packed, taken, *targets, arrived) = refs[:3], refs[3:]
    copies = fetched(sources, targets, arrived)
    dtproj, dt_bias, a_log = targets
    total = (p0[...].astype(F32) + p1[...].astype(F32)) + (
        p2[...].astype(F32) + p3[...].astype(F32)
    )
    low_rank = total[:RANK].astype(BF16)
    states[...] = total[RANK : RANK + 2 * STATE]
    for copy in copies:
        copy.wait()
    step[...] = jax.nn.softplus(
        lax.dot_general(
            low_rank, dtproj[...], (((0,), (0,)), ((), ())), preferred_element_type=F32
        )
        + dt_bias[...]
    )
    taken[...] = step[...] * inner[...].astype(F32)
    rate = -jnp.exp(a_log[...])

    def document(doc, carry):
        def eight(group, state):
            first = pl.multiple_of(doc * SECTION + group * 8, 8)
            steps = step[pl.ds(first, 8), :]
            values = taken[pl.ds(first, 8), :]
            entering = columns_from(states, doc, group)[:STATE]
            for i in range(8):
                factor = jnp.exp(steps[i : i + 1] * rate)
                state = factor * state + values[i : i + 1] * in_all_lanes(entering, i)
            return state

        state = lax.fori_loop(0, SECTION // 8, eight, jnp.zeros(rate.shape, F32), unroll=8)
        packed[pl.ds(pl.multiple_of(doc * STATE, STATE), STATE), :] = state.astype(BF16)
        return carry

    lax.fori_loop(0, DOCS, document, 0)
    sums = jnp.concatenate(
        [
            jnp.sum(step[doc * SECTION : (doc + 1) * SECTION, :], axis=0, keepdims=True)
            for doc in range(DOCS)
        ],
        axis=0,
    )
    high = sums.astype(BF16).astype(F32)
    both = jnp.concatenate([high, sums - high], axis=0)
    packed[DOCS * STATE : DOCS * STATE + 2 * DOCS, :] = both.astype(BF16)


def mixer_out_kernel(
    core,
    *refs,
):
    earlier, refs = refs[:7], refs[7:]
    (
        step,
        states,
        inner,
        a_log,
        skip,
        zin,
        out_weight,
        rows,
        totals,
        finals,
        taken,
        scanned,
        weight,
        arrived,
    ) = refs
    copy = pltpu.make_async_copy(out_weight, weight, arrived)
    copy.start()
    first = core[0] == 0
    partner = earlier[3][...].astype(F32)
    order = [jnp.where(first, 0.0, partner)]
    for by in (1, 2, 3):
        mine, theirs = earlier[by - 1][...].astype(F32), earlier[3 + by][...].astype(F32)
        order = [jnp.where(first, mine, theirs), jnp.where(first, theirs, mine)] + order
    for index, packed in enumerate(order):
        both = packed[DOCS * STATE :]
        totals[8 * index : 8 * index + DOCS, :] = both[:DOCS] + both[DOCS:]
        finals[index] = packed[: DOCS * STATE]
    taken[...] = step[...] * inner[...].astype(F32)
    rate = -jnp.exp(a_log[...])

    def document(doc, carry):
        state = jnp.zeros(rate.shape, F32)
        for index in range(len(order)):
            total = totals[pl.ds(8 * index + doc, 1), :]
            final = finals[index, pl.ds(pl.multiple_of(doc * STATE, STATE), STATE), :]
            state = jnp.exp(total * rate) * state + final

        def eight(group, state):
            first = pl.multiple_of(doc * SECTION + group * 8, 8)
            steps = step[pl.ds(first, 8), :]
            values = taken[pl.ds(first, 8), :]
            turned = columns_from(states, doc, group)
            sums = []
            for i in range(8):
                factor = jnp.exp(steps[i : i + 1] * rate)
                state = factor * state + values[i : i + 1] * in_all_lanes(turned[:STATE], i)
                seen = state * in_all_lanes(turned[STATE:], i)
                sums.append(jnp.sum(seen, axis=0, keepdims=True))
            scanned[pl.ds(first, 8), :] = jnp.concatenate(sums, axis=0)
            return state

        lax.fori_loop(0, SECTION // 8, eight, state, unroll=2)
        return carry

    lax.fori_loop(0, DOCS, document, 0)
    gate = jnp.dot(document_major(False), zin[...], preferred_element_type=F32)
    mixed = (scanned[...] + skip[...] * inner[...].astype(F32)) * jax.nn.silu(gate)
    ordered = jnp.dot(
        document_major(True), mixed.astype(BF16), preferred_element_type=F32
    ).astype(BF16)
    copy.wait()
    for low in range(0, D, 1024):
        rows[:, low : low + 1024] = jnp.dot(
            ordered, weight[:, low : low + 1024], preferred_element_type=F32
        ).astype(BF16)


def in_hbm(*values):
    return [pltpu.with_memory_space_constraint(value, pltpu.HBM) for value in values]


def whole(space=None):
    return pl.BlockSpec(memory_space=pltpu.VMEM if space is None else space)


def mixer_in(xin, edge, conv_weight, conv_bias, xproj):
    channels = xin.shape[1]
    return pl.pallas_call(
        mixer_in_kernel,
        out_shape=(
            jax.ShapeDtypeStruct((TOKENS, channels), BF16),
            jax.ShapeDtypeStruct((xproj.shape[0], TOKENS), BF16),
        ),
        in_specs=[whole()] * 2 + [whole(pltpu.HBM)] * 3,
        out_specs=(whole(), whole()),
        scratch_shapes=[
            pltpu.VMEM((16 + TOKENS, channels), F32),
            pltpu.VMEM(conv_weight.shape, F32),
            pltpu.VMEM(conv_bias.shape, F32),
            pltpu.VMEM(xproj.shape, BF16),
            pltpu.SemaphoreType.DMA((3,)),
        ],
        compiler_params=pltpu.CompilerParams(vmem_limit_bytes=16 << 20),
        name="mixer_in",
    )(xin, edge, *in_hbm(conv_weight, conv_bias, xproj))


def section_scan(parts, dtproj, dt_bias, a_log, inner):
    channels = inner.shape[1]
    return pl.pallas_call(
        section_kernel,
        out_shape=(
            jax.ShapeDtypeStruct((TOKENS, channels), F32),
            jax.ShapeDtypeStruct((2 * STATE, TOKENS), F32),
            jax.ShapeDtypeStruct((DOCS * (STATE + 2), channels), BF16),
        ),
        in_specs=[whole()] * 5 + [whole(pltpu.HBM)] * 3,
        out_specs=(whole(),) * 3,
        scratch_shapes=[
            pltpu.VMEM((TOKENS, channels), F32),
            pltpu.VMEM(dtproj.shape, BF16),
            pltpu.VMEM(dt_bias.shape, F32),
            pltpu.VMEM(a_log.shape, F32),
            pltpu.SemaphoreType.DMA((3,)),
        ],
        compiler_params=pltpu.CompilerParams(vmem_limit_bytes=16 << 20),
        name="section_scan",
    )(*parts, inner, *in_hbm(dtproj, dt_bias, a_log))


def mixer_out(core, earlier, step, states, inner, a_log, skip, zin, out_weight):
    channels = inner.shape[1]
    return pl.pallas_call(
        mixer_out_kernel,
        out_shape=jax.ShapeDtypeStruct((TOKENS, D), BF16),
        in_specs=[whole(pltpu.SMEM)] + [whole()] * 13 + [whole(pltpu.HBM)],
        out_specs=whole(),
        scratch_shapes=[
            pltpu.VMEM((64, channels), F32),
            pltpu.VMEM((7, DOCS * STATE, channels), F32),
            pltpu.VMEM((TOKENS, channels), F32),
            pltpu.VMEM((TOKENS, channels), F32),
            pltpu.VMEM(out_weight.shape, BF16),
            pltpu.SemaphoreType.DMA,
        ],
        compiler_params=pltpu.CompilerParams(vmem_limit_bytes=32 << 20),
        name="mixer_out",
    )(core, *earlier, step, states, inner, a_log, skip, zin, *in_hbm(out_weight))


def expert_kernel(count, *refs):
    inputs, (w_gate, w_up, w_down, mine, other, rows, total) = refs[:count], refs[count:]
    size = rows.shape[0]
    low = 0
    for part in inputs:
        rows[low : low + part.shape[0], :] = part[...]
        low += part.shape[0]

    def units(block, carry):
        place = pl.ds(pl.multiple_of(block * 256, 256), 256)
        gate_act = jnp.dot(rows[...], w_gate[0, :, place], preferred_element_type=F32)
        up_act = jnp.dot(rows[...], w_up[0, :, place], preferred_element_type=F32)
        hidden = (jax.nn.silu(gate_act) * up_act).astype(BF16)
        for low in range(0, D, 1024):
            term = jnp.dot(
                hidden, w_down[0, place, low : low + 1024], preferred_element_type=F32
            )
            before = jnp.where(block == 0, 0.0, total[:, low : low + 1024])
            total[:, low : low + 1024] = before + term
        return carry

    lax.fori_loop(0, w_down.shape[1] // 256, units, 0)
    mine[...] = total[: size // 2, :].astype(BF16)
    other[...] = total[size // 2 :, :].astype(BF16)


def expert_block(parts, w_gate, w_up, w_down):
    size = sum(part.shape[0] for part in parts)
    units = w_down.shape[1]
    return pl.pallas_call(
        lambda *refs: expert_kernel(len(parts), *refs),
        out_shape=(jax.ShapeDtypeStruct((size // 2, D), BF16),) * 2,
        in_specs=[whole()] * (len(parts) + 3),
        out_specs=(whole(),) * 2,
        scratch_shapes=[pltpu.VMEM((size, D), BF16), pltpu.VMEM((size, D), F32)],
        compiler_params=pltpu.CompilerParams(vmem_limit_bytes=12 << 20),
        cost_estimate=pl.CostEstimate(
            flops=6 * size * D * units,
            bytes_accessed=4 * size * D,
            transcendentals=size * units,
        ),
        name=f"experts_{size}",
    )(*parts, w_gate, w_up, w_down)


def slot_select(route_ids, capacity):
    flat_ids = route_ids.reshape(-1)
    onehot = (flat_ids[:, None] == jnp.arange(EXPERTS, dtype=jnp.int32)[None, :]).astype(jnp.int32)
    before = jnp.sum((jnp.cumsum(onehot, axis=0) - onehot) * onehot, axis=1)
    target = flat_ids * capacity + before
    matches = jnp.arange(EXPERTS * capacity, dtype=jnp.int32)[:, None] == target[None, :]
    return matches.reshape(EXPERTS * capacity, route_ids.shape[0], route_ids.shape[1])


def after(values, *others):
    held = lax.optimization_barrier((tuple(values), others))
    return held[0]


def experts(own, w_gate, w_up, w_down):
    count = own.shape[0]
    half = count // 2

    def paired(mine, other):
        return mine.astype(F32) + swapped(other).astype(F32)

    w_gate, w_up, w_down = [
        pltpu.with_memory_space_constraint(w, pltpu.VMEM) for w in (w_gate, w_up, w_down)
    ]
    left = lax.ppermute(own, "seq", x_shift(1))
    right = lax.ppermute(own, "seq", x_shift(-1))
    own_out = expert_block([own, swapped(own)], w_gate, w_up, w_down)
    left, right = after((left, right), own_out)
    far = [
        lax.ppermute(left[:half], "seq", x_shift(1)),
        lax.ppermute(right[half:], "seq", x_shift(-1)),
    ]
    left_out = expert_block([left, swapped(left)], w_gate, w_up, w_down)
    far = list(after(far, left_out))
    far_out = expert_block(far + [swapped(part) for part in far], w_gate, w_up, w_down)
    left_out = after(left_out, far_out)
    far_sum = paired(*far_out).astype(BF16)
    for_right = lax.ppermute(far_sum[:half], "seq", x_shift(1))
    for_left = lax.ppermute(far_sum[half:], "seq", x_shift(-1))
    right_out = expert_block([right, swapped(right)], w_gate, w_up, w_down)
    right_out = after(right_out, for_right, for_left)
    nothing = jnp.zeros((half, D), F32)
    to_left = paired(*left_out) + jnp.concatenate([nothing, for_left.astype(F32)])
    to_right = paired(*right_out) + jnp.concatenate([for_right.astype(F32), nothing])
    from_right = lax.ppermute(to_left.astype(BF16), "seq", x_shift(-1))
    from_left = lax.ppermute(to_right.astype(BF16), "seq", x_shift(1))
    return paired(*own_out) + from_left.astype(F32) + from_right.astype(F32)


def per_device(
    xin,
    zin,
    conv_weight,
    conv_bias,
    xproj_weight,
    dtproj_weight,
    dt_bias,
    a_log,
    skip,
    out_weight,
    resid,
    norm_gain,
    expert_ids,
    gate_weights,
    w_gate,
    w_up,
    w_down,
):
    channels = xin.shape[2]
    xin = xin.reshape(TOKENS, channels)
    edge = passed_along(xin[TOKENS - (CONV - 1) * DOCS :], "seq", 1)
    inner, projected = mixer_in(xin, edge, conv_weight, conv_bias[None], xproj_weight.T)
    along_z = [projected] + from_others(projected, z_shift)
    projected = sum(part.astype(F32) for part in along_z).astype(BF16)
    parts = [projected] + from_others(projected, y_shift)
    step, states, packed = section_scan(parts, dtproj_weight, dt_bias[None], a_log, inner)
    columns = [lax.ppermute(packed, "seq", x_onward(by)) for by in (1, 2, 3)]
    partial_rows = mixer_out(
        (lax.axis_index("seq") % 2).reshape(1),
        columns + [swapped(packed)] + [swapped(column) for column in columns],
        step,
        states,
        inner,
        a_log,
        skip[None],
        zin.reshape(TOKENS, channels),
        out_weight,
    )
    exchanged = lax.all_to_all(partial_rows, "exp", split_axis=0, concat_axis=0, tiled=True)
    row_count = resid.shape[0] * resid.shape[1]
    mamba_rows = jnp.sum(exchanged.reshape(-1, row_count, D).astype(F32), axis=0)
    hidden_state = resid.reshape(row_count, D).astype(F32) + mamba_rows
    norm_scale = lax.rsqrt(jnp.mean(hidden_state * hidden_state, axis=-1, keepdims=True) + 1e-05)
    tokens = (hidden_state * norm_scale * norm_gain).astype(BF16)
    capacity = 2 * TOPK * row_count // EXPERTS
    splits = lax.axis_size("exp") // EXPERTS
    route_ids = expert_ids.reshape(row_count, TOPK)
    gate_vals = gate_weights.reshape(row_count, TOPK)
    matches = slot_select(route_ids, capacity)
    chosen = jnp.sum(matches.astype(jnp.int32), axis=2).astype(BF16)
    outgoing = jnp.dot(chosen, tokens, preferred_element_type=F32).astype(BF16)
    arrived = lax.all_to_all(
        jnp.tile(outgoing, (splits, 1)), "exp", split_axis=0, concat_axis=0, tiled=True
    )
    own_rows = experts(arrived, w_gate, w_up, w_down)
    returned = lax.all_to_all(
        own_rows.astype(BF16), "exp", split_axis=0, concat_axis=0, tiled=True
    ).astype(F32)
    summed = jnp.sum(returned.reshape(splits, EXPERTS * capacity, D), axis=0)
    weights = jnp.sum(matches.astype(F32) * gate_vals.astype(F32)[None], axis=2)
    expert_out = jnp.dot(weights.T, summed, precision=lax.Precision.HIGHEST)
    return (hidden_state + expert_out).astype(BF16).reshape(resid.shape)


def solution(mesh):
    placed = (
        P("seq", None, "exp"),
        P("seq", None, "exp"),
        P(None, "exp"),
        P("exp"),
        P("exp", None),
        P(None, "exp"),
        P("exp"),
        P(None, "exp"),
        P("exp"),
        P("exp", None),
        P(("seq", "exp"), None, None),
        P(),
        P(("seq", "exp"), None, None),
        P(("seq", "exp"), None, None),
        P("exp", None, "seq"),
        P("exp", None, "seq"),
        P("exp", "seq", None),
    )
    return jax.shard_map(
        per_device,
        mesh=mesh,
        in_specs=placed,
        out_specs=P(("seq", "exp"), None, None),
        check_vma=False,
    )
```

```python
import jax
import jax.numpy as jnp
from jax import lax
from jax.experimental import pallas as pl
from jax.experimental.pallas import tpu as pltpu
from jax.sharding import PartitionSpec as P

D = 4096
STATE = 16
CONV = 4
RANK = 256
EXPERTS = 8
TOPK = 2
DOCS = 4
SECTION = 64
TOKENS = DOCS * SECTION
LANES = 128
F32 = jnp.float32
BF16 = jnp.bfloat16


def z_shift(by):
    return [(y * 4 + z, y * 4 + (z + by) % 4) for y in range(4) for z in range(4)]


def y_shift(by):
    return [(y * 4 + z, (y + by) % 4 * 4 + z) for y in range(4) for z in range(4)]


def x_shift(by):
    return [(x * 2 + c, (x + by) % 4 * 2 + c) for x in range(4) for c in range(2)]


def x_onward(by):
    return [(x * 2 + c, (x + by) * 2 + c) for x in range(4 - by) for c in range(2)]


CORE = [(x * 2 + c, x * 2 + 1 - c) for x in range(4) for c in range(2)]


def passed_along(value, axis, by):
    count = lax.axis_size(axis)
    pairs = [(i, i + by) for i in range(count) if 0 <= i + by < count]
    return lax.ppermute(value, axis, pairs)


def from_others(value, shift):
    return [lax.ppermute(value, "exp", shift(by)) for by in (1, 2, 3)]


def swapped(value):
    return lax.ppermute(value, "seq", CORE)


def document_major(back):
    row = lax.broadcasted_iota(jnp.int32, (TOKENS, TOKENS), 0)
    column = lax.broadcasted_iota(jnp.int32, (TOKENS, TOKENS), 1)
    if back:
        source = (row & (DOCS - 1)) * SECTION + (row >> 2)
    else:
        source = (row & (SECTION - 1)) * DOCS + (row >> 6)
    return jnp.where(column == source, 1.0, 0.0).astype(BF16)


def fetched(sources, targets, arrived):
    copies = [
        pltpu.make_async_copy(source, target, arrived.at[index])
        for index, (source, target) in enumerate(zip(sources, targets))
    ]
    for copy in copies:
        copy.start()
    return copies


def mixer_in_kernel(xin, edge, *refs):
    sources, (inner, projected, window, *targets, arrived) = refs[:3], refs[3:]
    copies = fetched(sources, targets, arrived)
    conv_weight, conv_bias, xproj = targets
    window[16 - edge.shape[0] : 16, :] = edge[...].astype(F32)
    window[16 : 16 + TOKENS, :] = xin[...].astype(F32)
    copies[0].wait()
    copies[1].wait()
    blocks = []
    for low in range(0, TOKENS, 64):
        running = jnp.broadcast_to(conv_bias[...], (64, xin.shape[1]))
        for offset in range(CONV):
            tap = window[pl.ds(low + 16 - DOCS * (CONV - 1 - offset), 64), :]
            running = running + conv_weight[offset : offset + 1, :] * tap
        blocks.append(jax.nn.silu(running).astype(BF16))
    by_position = jnp.concatenate(blocks, axis=0)
    ordered = jnp.dot(document_major(False), by_position, preferred_element_type=F32).astype(BF16)
    inner[...] = ordered
    copies[2].wait()
    projected[...] = lax.dot_general(
        xproj[...], ordered, (((1,), (1,)), ((), ())), preferred_element_type=F32
    ).astype(BF16)


def columns_from(states, doc, group):
    block = states[:, pl.ds(pl.multiple_of((doc >> 1) * LANES, LANES), LANES)]
    offset = (doc & 1) * SECTION + group * 8
    return pltpu.roll(block, (LANES - offset) & (LANES - 1), 1)


def in_all_lanes(turned, index):
    column = jnp.broadcast_to(turned[:, index : index + 1], (turned.shape[0], LANES))
    return jnp.concatenate([column] * 4, axis=1)


def section_kernel(p0, p1, p2, p3, inner, *refs):
    sources, (step, states, packed, taken, *targets, arrived) = refs[:3], refs[3:]
    copies = fetched(sources, targets, arrived)
    dtproj, dt_bias, a_log = targets
    total = (p0[...].astype(F32) + p1[...].astype(F32)) + (
        p2[...].astype(F32) + p3[...].astype(F32)
    )
    low_rank = total[:RANK].astype(BF16)
    states[...] = total[RANK : RANK + 2 * STATE]
    for copy in copies:
        copy.wait()
    step[...] = jax.nn.softplus(
        lax.dot_general(
            low_rank, dtproj[...], (((0,), (0,)), ((), ())), preferred_element_type=F32
        )
        + dt_bias[...]
    )
    taken[...] = step[...] * inner[...].astype(F32)
    rate = -jnp.exp(a_log[...])

    def document(doc, carry):
        def eight(group, state):
            first = pl.multiple_of(doc * SECTION + group * 8, 8)
            steps = step[pl.ds(first, 8), :]
            values = taken[pl.ds(first, 8), :]
            entering = columns_from(states, doc, group)[:STATE]
            for i in range(8):
                factor = jnp.exp(steps[i : i + 1] * rate)
                state = factor * state + values[i : i + 1] * in_all_lanes(entering, i)
            return state

        state = lax.fori_loop(0, SECTION // 8, eight, jnp.zeros(rate.shape, F32), unroll=8)
        packed[pl.ds(pl.multiple_of(doc * STATE, STATE), STATE), :] = state.astype(BF16)
        return carry

    lax.fori_loop(0, DOCS, document, 0)
    sums = jnp.concatenate(
        [
            jnp.sum(step[doc * SECTION : (doc + 1) * SECTION, :], axis=0, keepdims=True)
            for doc in range(DOCS)
        ],
        axis=0,
    )
    high = sums.astype(BF16).astype(F32)
    both = jnp.concatenate([high, sums - high], axis=0)
    packed[DOCS * STATE : DOCS * STATE + 2 * DOCS, :] = both.astype(BF16)


def mixer_out_kernel(
    core,
    *refs,
):
    earlier, refs = refs[:7], refs[7:]
    (
        step,
        states,
        inner,
        a_log,
        skip,
        zin,
        out_weight,
        rows,
        totals,
        finals,
        taken,
        scanned,
        weight,
        arrived,
    ) = refs
    copy = pltpu.make_async_copy(out_weight, weight, arrived)
    copy.start()
    first = core[0] == 0
    partner = earlier[3][...].astype(F32)
    order = [jnp.where(first, 0.0, partner)]
    for by in (1, 2, 3):
        mine, theirs = earlier[by - 1][...].astype(F32), earlier[3 + by][...].astype(F32)
        order = [jnp.where(first, mine, theirs), jnp.where(first, theirs, mine)] + order
    for index, packed in enumerate(order):
        both = packed[DOCS * STATE :]
        totals[8 * index : 8 * index + DOCS, :] = both[:DOCS] + both[DOCS:]
        finals[index] = packed[: DOCS * STATE]
    taken[...] = step[...] * inner[...].astype(F32)
    rate = -jnp.exp(a_log[...])

    def document(doc, carry):
        state = jnp.zeros(rate.shape, F32)
        for index in range(len(order)):
            total = totals[pl.ds(8 * index + doc, 1), :]
            final = finals[index, pl.ds(pl.multiple_of(doc * STATE, STATE), STATE), :]
            state = jnp.exp(total * rate) * state + final

        def eight(group, state):
            first = pl.multiple_of(doc * SECTION + group * 8, 8)
            steps = step[pl.ds(first, 8), :]
            values = taken[pl.ds(first, 8), :]
            turned = columns_from(states, doc, group)
            sums = []
            for i in range(8):
                factor = jnp.exp(steps[i : i + 1] * rate)
                state = factor * state + values[i : i + 1] * in_all_lanes(turned[:STATE], i)
                seen = state * in_all_lanes(turned[STATE:], i)
                sums.append(jnp.sum(seen, axis=0, keepdims=True))
            scanned[pl.ds(first, 8), :] = jnp.concatenate(sums, axis=0)
            return state

        lax.fori_loop(0, SECTION // 8, eight, state, unroll=2)
        return carry

    lax.fori_loop(0, DOCS, document, 0)
    gate = jnp.dot(document_major(False), zin[...], preferred_element_type=F32)
    mixed = (scanned[...] + skip[...] * inner[...].astype(F32)) * jax.nn.silu(gate)
    ordered = jnp.dot(
        document_major(True), mixed.astype(BF16), preferred_element_type=F32
    ).astype(BF16)
    copy.wait()
    for low in range(0, D, 1024):
        rows[:, low : low + 1024] = jnp.dot(
            ordered, weight[:, low : low + 1024], preferred_element_type=F32
        ).astype(BF16)


def in_hbm(*values):
    return [pltpu.with_memory_space_constraint(value, pltpu.HBM) for value in values]


def whole(space=None):
    return pl.BlockSpec(memory_space=pltpu.VMEM if space is None else space)


def mixer_in(xin, edge, conv_weight, conv_bias, xproj):
    channels = xin.shape[1]
    return pl.pallas_call(
        mixer_in_kernel,
        out_shape=(
            jax.ShapeDtypeStruct((TOKENS, channels), BF16),
            jax.ShapeDtypeStruct((xproj.shape[0], TOKENS), BF16),
        ),
        in_specs=[whole()] * 2 + [whole(pltpu.HBM)] * 3,
        out_specs=(whole(), whole()),
        scratch_shapes=[
            pltpu.VMEM((16 + TOKENS, channels), F32),
            pltpu.VMEM(conv_weight.shape, F32),
            pltpu.VMEM(conv_bias.shape, F32),
            pltpu.VMEM(xproj.shape, BF16),
            pltpu.SemaphoreType.DMA((3,)),
        ],
        compiler_params=pltpu.CompilerParams(vmem_limit_bytes=16 << 20),
        name="mixer_in",
    )(xin, edge, *in_hbm(conv_weight, conv_bias, xproj))


def section_scan(parts, dtproj, dt_bias, a_log, inner):
    channels = inner.shape[1]
    return pl.pallas_call(
        section_kernel,
        out_shape=(
            jax.ShapeDtypeStruct((TOKENS, channels), F32),
            jax.ShapeDtypeStruct((2 * STATE, TOKENS), F32),
            jax.ShapeDtypeStruct((DOCS * (STATE + 2), channels), BF16),
        ),
        in_specs=[whole()] * 5 + [whole(pltpu.HBM)] * 3,
        out_specs=(whole(),) * 3,
        scratch_shapes=[
            pltpu.VMEM((TOKENS, channels), F32),
            pltpu.VMEM(dtproj.shape, BF16),
            pltpu.VMEM(dt_bias.shape, F32),
            pltpu.VMEM(a_log.shape, F32),
            pltpu.SemaphoreType.DMA((3,)),
        ],
        compiler_params=pltpu.CompilerParams(vmem_limit_bytes=16 << 20),
        name="section_scan",
    )(*parts, inner, *in_hbm(dtproj, dt_bias, a_log))


def mixer_out(core, earlier, step, states, inner, a_log, skip, zin, out_weight):
    channels = inner.shape[1]
    return pl.pallas_call(
        mixer_out_kernel,
        out_shape=jax.ShapeDtypeStruct((TOKENS, D), BF16),
        in_specs=[whole(pltpu.SMEM)] + [whole()] * 13 + [whole(pltpu.HBM)],
        out_specs=whole(),
        scratch_shapes=[
            pltpu.VMEM((64, channels), F32),
            pltpu.VMEM((7, DOCS * STATE, channels), F32),
            pltpu.VMEM((TOKENS, channels), F32),
            pltpu.VMEM((TOKENS, channels), F32),
            pltpu.VMEM(out_weight.shape, BF16),
            pltpu.SemaphoreType.DMA,
        ],
        compiler_params=pltpu.CompilerParams(vmem_limit_bytes=32 << 20),
        name="mixer_out",
    )(core, *earlier, step, states, inner, a_log, skip, zin, *in_hbm(out_weight))


def expert_kernel(count, *refs):
    inputs, (w_gate, w_up, w_down, mine, other, rows, total) = refs[:count], refs[count:]
    size = rows.shape[0]
    low = 0
    for part in inputs:
        rows[low : low + part.shape[0], :] = part[...]
        low += part.shape[0]

    def units(block, carry):
        place = pl.ds(pl.multiple_of(block * 256, 256), 256)
        gate_act = jnp.dot(rows[...], w_gate[0, :, place], preferred_element_type=F32)
        up_act = jnp.dot(rows[...], w_up[0, :, place], preferred_element_type=F32)
        hidden = (jax.nn.silu(gate_act) * up_act).astype(BF16)
        for low in range(0, D, 1024):
            term = jnp.dot(
                hidden, w_down[0, place, low : low + 1024], preferred_element_type=F32
            )
            before = jnp.where(block == 0, 0.0, total[:, low : low + 1024])
            total[:, low : low + 1024] = before + term
        return carry

    lax.fori_loop(0, w_down.shape[1] // 256, units, 0)
    mine[...] = total[: size // 2, :].astype(BF16)
    other[...] = total[size // 2 :, :].astype(BF16)


def expert_block(parts, w_gate, w_up, w_down):
    size = sum(part.shape[0] for part in parts)
    units = w_down.shape[1]
    return pl.pallas_call(
        lambda *refs: expert_kernel(len(parts), *refs),
        out_shape=(jax.ShapeDtypeStruct((size // 2, D), BF16),) * 2,
        in_specs=[whole()] * (len(parts) + 3),
        out_specs=(whole(),) * 2,
        scratch_shapes=[pltpu.VMEM((size, D), BF16), pltpu.VMEM((size, D), F32)],
        compiler_params=pltpu.CompilerParams(vmem_limit_bytes=12 << 20),
        cost_estimate=pl.CostEstimate(
            flops=6 * size * D * units,
            bytes_accessed=4 * size * D,
            transcendentals=size * units,
        ),
        name=f"experts_{size}",
    )(*parts, w_gate, w_up, w_down)


def slot_select(route_ids, capacity):
    flat_ids = route_ids.reshape(-1)
    onehot = (flat_ids[:, None] == jnp.arange(EXPERTS, dtype=jnp.int32)[None, :]).astype(jnp.int32)
    before = jnp.sum((jnp.cumsum(onehot, axis=0) - onehot) * onehot, axis=1)
    target = flat_ids * capacity + before
    matches = jnp.arange(EXPERTS * capacity, dtype=jnp.int32)[:, None] == target[None, :]
    return matches.reshape(EXPERTS * capacity, route_ids.shape[0], route_ids.shape[1])


def after(values, *others):
    held = lax.optimization_barrier((tuple(values), others))
    return held[0]


def experts(own, w_gate, w_up, w_down):
    count = own.shape[0]
    half = count // 2

    def paired(mine, other):
        return mine.astype(F32) + swapped(other).astype(F32)

    w_gate, w_up, w_down = [
        pltpu.with_memory_space_constraint(w, pltpu.VMEM) for w in (w_gate, w_up, w_down)
    ]
    left = lax.ppermute(own, "seq", x_shift(1))
    right = lax.ppermute(own, "seq", x_shift(-1))
    own_out = expert_block([own, swapped(own)], w_gate, w_up, w_down)
    left, right = after((left, right), own_out)
    far = [
        lax.ppermute(left[:half], "seq", x_shift(1)),
        lax.ppermute(right[half:], "seq", x_shift(-1)),
    ]
    left_out = expert_block([left, swapped(left)], w_gate, w_up, w_down)
    right_out = expert_block([right, swapped(right)], w_gate, w_up, w_down)
    far, left_out, right_out = lax.optimization_barrier((far, left_out, right_out))
    left_sum, right_sum = paired(*left_out), paired(*right_out)
    from_right = lax.ppermute(left_sum[:half].astype(BF16), "seq", x_shift(-1))
    from_left = lax.ppermute(right_sum[half:].astype(BF16), "seq", x_shift(1))
    far_out = expert_block(far + [swapped(part) for part in far], w_gate, w_up, w_down)
    far_out = after(far_out, from_right, from_left)
    far_sum = paired(*far_out).astype(BF16)
    for_right = lax.ppermute(far_sum[:half], "seq", x_shift(1))
    for_left = lax.ppermute(far_sum[half:], "seq", x_shift(-1))
    to_left = left_sum[half:] + for_left.astype(F32)
    to_right = right_sum[:half] + for_right.astype(F32)
    then_right = lax.ppermute(to_left.astype(BF16), "seq", x_shift(-1))
    then_left = lax.ppermute(to_right.astype(BF16), "seq", x_shift(1))
    return (
        paired(*own_out)
        + jnp.concatenate([from_right, then_right]).astype(F32)
        + jnp.concatenate([then_left, from_left]).astype(F32)
    )


def per_device(
    xin,
    zin,
    conv_weight,
    conv_bias,
    xproj_weight,
    dtproj_weight,
    dt_bias,
    a_log,
    skip,
    out_weight,
    resid,
    norm_gain,
    expert_ids,
    gate_weights,
    w_gate,
    w_up,
    w_down,
):
    channels = xin.shape[2]
    xin = xin.reshape(TOKENS, channels)
    edge = passed_along(xin[TOKENS - (CONV - 1) * DOCS :], "seq", 1)
    inner, projected = mixer_in(xin, edge, conv_weight, conv_bias[None], xproj_weight.T)
    along_z = [projected] + from_others(projected, z_shift)
    projected = sum(part.astype(F32) for part in along_z).astype(BF16)
    parts = [projected] + from_others(projected, y_shift)
    step, states, packed = section_scan(parts, dtproj_weight, dt_bias[None], a_log, inner)
    columns = [lax.ppermute(packed, "seq", x_onward(by)) for by in (1, 2, 3)]
    partial_rows = mixer_out(
        (lax.axis_index("seq") % 2).reshape(1),
        columns + [swapped(packed)] + [swapped(column) for column in columns],
        step,
        states,
        inner,
        a_log,
        skip[None],
        zin.reshape(TOKENS, channels),
        out_weight,
    )
    exchanged = lax.all_to_all(partial_rows, "exp", split_axis=0, concat_axis=0, tiled=True)
    row_count = resid.shape[0] * resid.shape[1]
    mamba_rows = jnp.sum(exchanged.reshape(-1, row_count, D).astype(F32), axis=0)
    hidden_state = resid.reshape(row_count, D).astype(F32) + mamba_rows
    norm_scale = lax.rsqrt(jnp.mean(hidden_state * hidden_state, axis=-1, keepdims=True) + 1e-05)
    tokens = (hidden_state * norm_scale * norm_gain).astype(BF16)
    capacity = 2 * TOPK * row_count // EXPERTS
    splits = lax.axis_size("exp") // EXPERTS
    route_ids = expert_ids.reshape(row_count, TOPK)
    gate_vals = gate_weights.reshape(row_count, TOPK)
    matches = slot_select(route_ids, capacity)
    chosen = jnp.sum(matches.astype(jnp.int32), axis=2).astype(BF16)
    outgoing = jnp.dot(chosen, tokens, preferred_element_type=F32).astype(BF16)
    arrived = lax.all_to_all(
        jnp.tile(outgoing, (splits, 1)), "exp", split_axis=0, concat_axis=0, tiled=True
    )
    own_rows = experts(arrived, w_gate, w_up, w_down)
    returned = lax.all_to_all(
        own_rows.astype(BF16), "exp", split_axis=0, concat_axis=0, tiled=True
    ).astype(F32)
    summed = jnp.sum(returned.reshape(splits, EXPERTS * capacity, D), axis=0)
    weights = jnp.sum(matches.astype(F32) * gate_vals.astype(F32)[None], axis=2)
    expert_out = jnp.dot(weights.T, summed, precision=lax.Precision.HIGHEST)
    return (hidden_state + expert_out).astype(BF16).reshape(resid.shape)


def solution(mesh):
    placed = (
        P("seq", None, "exp"),
        P("seq", None, "exp"),
        P(None, "exp"),
        P("exp"),
        P("exp", None),
        P(None, "exp"),
        P("exp"),
        P(None, "exp"),
        P("exp"),
        P("exp", None),
        P(("seq", "exp"), None, None),
        P(),
        P(("seq", "exp"), None, None),
        P(("seq", "exp"), None, None),
        P("exp", None, "seq"),
        P("exp", None, "seq"),
        P("exp", "seq", None),
    )
    return jax.shard_map(
        per_device,
        mesh=mesh,
        in_specs=placed,
        out_specs=P(("seq", "exp"), None, None),
        check_vma=False,
    )
```

```python
import jax
import jax.numpy as jnp
from jax import lax
from jax.experimental import pallas as pl
from jax.experimental.pallas import tpu as pltpu
from jax.sharding import PartitionSpec as P

D = 4096
STATE = 16
CONV = 4
RANK = 256
EXPERTS = 8
TOPK = 2
DOCS = 4
SECTION = 64
TOKENS = DOCS * SECTION
LANES = 128
F32 = jnp.float32
BF16 = jnp.bfloat16


def z_shift(by):
    return [(y * 4 + z, y * 4 + (z + by) % 4) for y in range(4) for z in range(4)]


def y_shift(by):
    return [(y * 4 + z, (y + by) % 4 * 4 + z) for y in range(4) for z in range(4)]


def x_shift(by):
    return [(x * 2 + c, (x + by) % 4 * 2 + c) for x in range(4) for c in range(2)]


CORE = [(x * 2 + c, x * 2 + 1 - c) for x in range(4) for c in range(2)]


def passed_along(value, axis, by):
    count = lax.axis_size(axis)
    pairs = [(i, i + by) for i in range(count) if 0 <= i + by < count]
    return lax.ppermute(value, axis, pairs)


def from_others(value, shift):
    return [lax.ppermute(value, "exp", shift(by)) for by in (1, 2, 3)]


def swapped(value):
    return lax.ppermute(value, "seq", CORE)


def document_major(back):
    row = lax.broadcasted_iota(jnp.int32, (TOKENS, TOKENS), 0)
    column = lax.broadcasted_iota(jnp.int32, (TOKENS, TOKENS), 1)
    if back:
        source = (row & (DOCS - 1)) * SECTION + (row >> 2)
    else:
        source = (row & (SECTION - 1)) * DOCS + (row >> 6)
    return jnp.where(column == source, 1.0, 0.0).astype(BF16)


def fetched(sources, targets, arrived):
    copies = [
        pltpu.make_async_copy(source, target, arrived.at[index])
        for index, (source, target) in enumerate(zip(sources, targets))
    ]
    for copy in copies:
        copy.start()
    return copies


def mixer_in_kernel(xin, edge, *refs):
    sources, (inner, projected, window, *targets, arrived) = refs[:3], refs[3:]
    copies = fetched(sources, targets, arrived)
    conv_weight, conv_bias, xproj = targets
    window[16 - edge.shape[0] : 16, :] = edge[...].astype(F32)
    window[16 : 16 + TOKENS, :] = xin[...].astype(F32)
    copies[0].wait()
    copies[1].wait()
    blocks = []
    for low in range(0, TOKENS, 64):
        running = jnp.broadcast_to(conv_bias[...], (64, xin.shape[1]))
        for offset in range(CONV):
            tap = window[pl.ds(low + 16 - DOCS * (CONV - 1 - offset), 64), :]
            running = running + conv_weight[offset : offset + 1, :] * tap
        blocks.append(jax.nn.silu(running).astype(BF16))
    by_position = jnp.concatenate(blocks, axis=0)
    ordered = jnp.dot(document_major(False), by_position, preferred_element_type=F32).astype(BF16)
    inner[...] = ordered
    copies[2].wait()
    projected[...] = lax.dot_general(
        xproj[...], ordered, (((1,), (1,)), ((), ())), preferred_element_type=F32
    ).astype(BF16)


def columns_from(states, doc, group):
    block = states[:, pl.ds(pl.multiple_of((doc >> 1) * LANES, LANES), LANES)]
    offset = (doc & 1) * SECTION + group * 8
    return pltpu.roll(block, (LANES - offset) & (LANES - 1), 1)


def in_all_lanes(turned, index):
    column = jnp.broadcast_to(turned[:, index : index + 1], (turned.shape[0], LANES))
    return jnp.concatenate([column] * 4, axis=1)


def section_kernel(p0, p1, p2, p3, inner, *refs):
    sources, (step, states, packed, taken, *targets, arrived) = refs[:3], refs[3:]
    copies = fetched(sources, targets, arrived)
    dtproj, dt_bias, a_log = targets
    total = (p0[...].astype(F32) + p1[...].astype(F32)) + (
        p2[...].astype(F32) + p3[...].astype(F32)
    )
    low_rank = total[:RANK].astype(BF16)
    states[...] = total[RANK : RANK + 2 * STATE]
    for copy in copies:
        copy.wait()
    step[...] = jax.nn.softplus(
        lax.dot_general(
            low_rank, dtproj[...], (((0,), (0,)), ((), ())), preferred_element_type=F32
        )
        + dt_bias[...]
    )
    taken[...] = step[...] * inner[...].astype(F32)
    rate = -jnp.exp(a_log[...])

    def document(doc, carry):
        def eight(group, state):
            first = pl.multiple_of(doc * SECTION + group * 8, 8)
            steps = step[pl.ds(first, 8), :]
            values = taken[pl.ds(first, 8), :]
            entering = columns_from(states, doc, group)[:STATE]
            for i in range(8):
                factor = jnp.exp(steps[i : i + 1] * rate)
                state = factor * state + values[i : i + 1] * in_all_lanes(entering, i)
            return state

        state = lax.fori_loop(0, SECTION // 8, eight, jnp.zeros(rate.shape, F32), unroll=8)
        packed[pl.ds(pl.multiple_of(doc * STATE, STATE), STATE), :] = state.astype(BF16)
        return carry

    lax.fori_loop(0, DOCS, document, 0)
    sums = jnp.concatenate(
        [
            jnp.sum(step[doc * SECTION : (doc + 1) * SECTION, :], axis=0, keepdims=True)
            for doc in range(DOCS)
        ],
        axis=0,
    )
    high = sums.astype(BF16).astype(F32)
    both = jnp.concatenate([high, sums - high], axis=0)
    packed[DOCS * STATE : DOCS * STATE + 2 * DOCS, :] = both.astype(BF16)


def mixer_out_kernel(
    section,
    *refs,
):
    earlier, refs = refs[:7], refs[7:]
    (
        step,
        states,
        inner,
        a_log,
        skip,
        zin,
        out_weight,
        rows,
        totals,
        finals,
        taken,
        scanned,
        weight,
        finished,
        arrived,
        left,
    ) = refs
    copy = pltpu.make_async_copy(out_weight, weight, arrived)
    copy.start()
    first = section[0] % 2 == 0
    partner = earlier[3][...].astype(F32)
    order = [jnp.where(first, 0.0, partner)]
    for by in (1, 2, 3):
        before = section[0] >= 2 * by
        mine = jnp.where(before, earlier[by - 1][...].astype(F32), 0.0)
        theirs = jnp.where(before, earlier[3 + by][...].astype(F32), 0.0)
        order = [jnp.where(first, mine, theirs), jnp.where(first, theirs, mine)] + order
    for index, packed in enumerate(order):
        both = packed[DOCS * STATE :]
        totals[8 * index : 8 * index + DOCS, :] = both[:DOCS] + both[DOCS:]
        finals[index] = packed[: DOCS * STATE]
    taken[...] = step[...] * inner[...].astype(F32)
    rate = -jnp.exp(a_log[...])

    def document(doc, carry):
        state = jnp.zeros(rate.shape, F32)
        for index in range(len(order)):
            total = totals[pl.ds(8 * index + doc, 1), :]
            final = finals[index, pl.ds(pl.multiple_of(doc * STATE, STATE), STATE), :]
            state = jnp.exp(total * rate) * state + final

        def eight(group, state):
            first = pl.multiple_of(doc * SECTION + group * 8, 8)
            steps = step[pl.ds(first, 8), :]
            values = taken[pl.ds(first, 8), :]
            turned = columns_from(states, doc, group)
            sums = []
            for i in range(8):
                factor = jnp.exp(steps[i : i + 1] * rate)
                state = factor * state + values[i : i + 1] * in_all_lanes(turned[:STATE], i)
                seen = state * in_all_lanes(turned[STATE:], i)
                sums.append(jnp.sum(seen, axis=0, keepdims=True))
            scanned[pl.ds(first, 8), :] = jnp.concatenate(sums, axis=0)
            return state

        lax.fori_loop(0, SECTION // 8, eight, state, unroll=2)
        return carry

    lax.fori_loop(0, DOCS, document, 0)
    gate = jnp.dot(document_major(False), zin[...], preferred_element_type=F32)
    mixed = (scanned[...] + skip[...] * inner[...].astype(F32)) * jax.nn.silu(gate)
    ordered = jnp.dot(
        document_major(True), mixed.astype(BF16), preferred_element_type=F32
    ).astype(BF16)
    copy.wait()
    leaving = []
    for index, low in enumerate(range(0, D, 1024)):
        finished[index] = jnp.dot(
            ordered, weight[:, low : low + 1024], preferred_element_type=F32
        ).astype(BF16)
        leaving.append(
            pltpu.make_async_copy(
                finished.at[index], rows.at[:, pl.ds(low, 1024)], left.at[index]
            )
        )
        leaving[-1].start()
    for copy in leaving:
        copy.wait()


def in_hbm(*values):
    return [pltpu.with_memory_space_constraint(value, pltpu.HBM) for value in values]


def whole(space=None):
    return pl.BlockSpec(memory_space=pltpu.VMEM if space is None else space)


def mixer_in(xin, edge, conv_weight, conv_bias, xproj):
    channels = xin.shape[1]
    return pl.pallas_call(
        mixer_in_kernel,
        out_shape=(
            jax.ShapeDtypeStruct((TOKENS, channels), BF16),
            jax.ShapeDtypeStruct((xproj.shape[0], TOKENS), BF16),
        ),
        in_specs=[whole()] * 2 + [whole(pltpu.HBM)] * 3,
        out_specs=(whole(), whole()),
        scratch_shapes=[
            pltpu.VMEM((16 + TOKENS, channels), F32),
            pltpu.VMEM(conv_weight.shape, F32),
            pltpu.VMEM(conv_bias.shape, F32),
            pltpu.VMEM(xproj.shape, BF16),
            pltpu.SemaphoreType.DMA((3,)),
        ],
        compiler_params=pltpu.CompilerParams(vmem_limit_bytes=16 << 20),
        name="mixer_in",
    )(xin, edge, *in_hbm(conv_weight, conv_bias, xproj))


def section_scan(parts, dtproj, dt_bias, a_log, inner):
    channels = inner.shape[1]
    return pl.pallas_call(
        section_kernel,
        out_shape=(
            jax.ShapeDtypeStruct((TOKENS, channels), F32),
            jax.ShapeDtypeStruct((2 * STATE, TOKENS), F32),
            jax.ShapeDtypeStruct((DOCS * (STATE + 2), channels), BF16),
        ),
        in_specs=[whole()] * 5 + [whole(pltpu.HBM)] * 3,
        out_specs=(whole(),) * 3,
        scratch_shapes=[
            pltpu.VMEM((TOKENS, channels), F32),
            pltpu.VMEM(dtproj.shape, BF16),
            pltpu.VMEM(dt_bias.shape, F32),
            pltpu.VMEM(a_log.shape, F32),
            pltpu.SemaphoreType.DMA((3,)),
        ],
        compiler_params=pltpu.CompilerParams(vmem_limit_bytes=16 << 20),
        name="section_scan",
    )(*parts, inner, *in_hbm(dtproj, dt_bias, a_log))


def mixer_out(section, earlier, step, states, inner, a_log, skip, zin, out_weight):
    channels = inner.shape[1]
    return pl.pallas_call(
        mixer_out_kernel,
        out_shape=jax.ShapeDtypeStruct((TOKENS, D), BF16),
        in_specs=[whole(pltpu.SMEM)] + [whole()] * 13 + [whole(pltpu.HBM)],
        out_specs=whole(pltpu.HBM),
        scratch_shapes=[
            pltpu.VMEM((64, channels), F32),
            pltpu.VMEM((7, DOCS * STATE, channels), F32),
            pltpu.VMEM((TOKENS, channels), F32),
            pltpu.VMEM((TOKENS, channels), F32),
            pltpu.VMEM(out_weight.shape, BF16),
            pltpu.VMEM((D // 1024, TOKENS, 1024), BF16),
            pltpu.SemaphoreType.DMA,
            pltpu.SemaphoreType.DMA((D // 1024,)),
        ],
        compiler_params=pltpu.CompilerParams(vmem_limit_bytes=32 << 20),
        name="mixer_out",
    )(section, *earlier, step, states, inner, a_log, skip, zin, *in_hbm(out_weight))


def expert_kernel(count, *refs):
    inputs, (w_gate, w_up, w_down, mine, other, rows, total) = refs[:count], refs[count:]
    size = rows.shape[0]
    low = 0
    for part in inputs:
        rows[low : low + part.shape[0], :] = part[...]
        low += part.shape[0]

    def units(block, carry):
        place = pl.ds(pl.multiple_of(block * 256, 256), 256)
        gate_act = jnp.dot(rows[...], w_gate[0, :, place], preferred_element_type=F32)
        up_act = jnp.dot(rows[...], w_up[0, :, place], preferred_element_type=F32)
        hidden = (jax.nn.silu(gate_act) * up_act).astype(BF16)
        for low in range(0, D, 1024):
            term = jnp.dot(
                hidden, w_down[0, place, low : low + 1024], preferred_element_type=F32
            )
            before = jnp.where(block == 0, 0.0, total[:, low : low + 1024])
            total[:, low : low + 1024] = before + term
        return carry

    lax.fori_loop(0, w_down.shape[1] // 256, units, 0)
    mine[...] = total[: size // 2, :].astype(BF16)
    other[...] = total[size // 2 :, :].astype(BF16)


def expert_block(parts, w_gate, w_up, w_down):
    size = sum(part.shape[0] for part in parts)
    units = w_down.shape[1]
    return pl.pallas_call(
        lambda *refs: expert_kernel(len(parts), *refs),
        out_shape=(jax.ShapeDtypeStruct((size // 2, D), BF16),) * 2,
        in_specs=[whole()] * (len(parts) + 3),
        out_specs=(whole(),) * 2,
        scratch_shapes=[pltpu.VMEM((size, D), BF16), pltpu.VMEM((size, D), F32)],
        compiler_params=pltpu.CompilerParams(vmem_limit_bytes=12 << 20),
        cost_estimate=pl.CostEstimate(
            flops=6 * size * D * units,
            bytes_accessed=4 * size * D,
            transcendentals=size * units,
        ),
        name=f"experts_{size}",
    )(*parts, w_gate, w_up, w_down)


def slot_select(route_ids, capacity):
    flat_ids = route_ids.reshape(-1)
    onehot = (flat_ids[:, None] == jnp.arange(EXPERTS, dtype=jnp.int32)[None, :]).astype(jnp.int32)
    before = jnp.sum((jnp.cumsum(onehot, axis=0) - onehot) * onehot, axis=1)
    target = flat_ids * capacity + before
    matches = jnp.arange(EXPERTS * capacity, dtype=jnp.int32)[:, None] == target[None, :]
    return matches.reshape(EXPERTS * capacity, route_ids.shape[0], route_ids.shape[1])


def after(values, *others):
    held = lax.optimization_barrier((tuple(values), others))
    return held[0]


def experts(own, w_gate, w_up, w_down):
    count = own.shape[0]
    half = count // 2

    def paired(mine, other):
        return mine.astype(F32) + swapped(other).astype(F32)

    w_gate, w_up, w_down = [
        pltpu.with_memory_space_constraint(w, pltpu.VMEM) for w in (w_gate, w_up, w_down)
    ]
    left = lax.ppermute(own, "seq", x_shift(1))
    right = lax.ppermute(own, "seq", x_shift(-1))
    own_out = expert_block([own, swapped(own)], w_gate, w_up, w_down)
    left, right = after((left, right), own_out)
    far = [
        lax.ppermute(left[:half], "seq", x_shift(1)),
        lax.ppermute(right[half:], "seq", x_shift(-1)),
    ]
    left_out = expert_block([left, swapped(left)], w_gate, w_up, w_down)
    right_out = expert_block([right, swapped(right)], w_gate, w_up, w_down)
    far, left_out, right_out = lax.optimization_barrier((far, left_out, right_out))
    left_sum, right_sum = paired(*left_out), paired(*right_out)
    from_right = lax.ppermute(left_sum[:half].astype(BF16), "seq", x_shift(-1))
    from_left = lax.ppermute(right_sum[half:].astype(BF16), "seq", x_shift(1))
    far_out = expert_block(far + [swapped(part) for part in far], w_gate, w_up, w_down)
    far_out = after(far_out, from_right, from_left)
    far_sum = paired(*far_out).astype(BF16)
    for_right = lax.ppermute(far_sum[:half], "seq", x_shift(1))
    for_left = lax.ppermute(far_sum[half:], "seq", x_shift(-1))
    own_sum = paired(*own_out)
    to_left = left_sum[half:] + for_left.astype(F32)
    to_right = right_sum[:half] + for_right.astype(F32)
    first_half = own_sum[:half] + from_right.astype(F32)
    second_half = own_sum[half:] + from_left.astype(F32)
    first_half, second_half = lax.optimization_barrier((first_half, second_half))
    then_right = lax.ppermute(to_left.astype(BF16), "seq", x_shift(-1))
    then_left = lax.ppermute(to_right.astype(BF16), "seq", x_shift(1))
    return jnp.concatenate(
        [first_half + then_left.astype(F32), second_half + then_right.astype(F32)]
    )


def per_device(
    xin,
    zin,
    conv_weight,
    conv_bias,
    xproj_weight,
    dtproj_weight,
    dt_bias,
    a_log,
    skip,
    out_weight,
    resid,
    norm_gain,
    expert_ids,
    gate_weights,
    w_gate,
    w_up,
    w_down,
):
    channels = xin.shape[2]
    xin = xin.reshape(TOKENS, channels)
    edge = passed_along(xin[TOKENS - (CONV - 1) * DOCS :], "seq", 1)
    inner, projected = mixer_in(xin, edge, conv_weight, conv_bias[None], xproj_weight.T)
    along_z = [projected] + from_others(projected, z_shift)
    projected = sum(part.astype(F32) for part in along_z).astype(BF16)
    parts = [projected] + from_others(projected, y_shift)
    step, states, packed = section_scan(parts, dtproj_weight, dt_bias[None], a_log, inner)
    columns = [lax.ppermute(packed, "seq", x_shift(by)) for by in (1, 2, 3)]
    partial_rows = mixer_out(
        lax.axis_index("seq").reshape(1),
        columns + [swapped(packed)] + [swapped(column) for column in columns],
        step,
        states,
        inner,
        a_log,
        skip[None],
        zin.reshape(TOKENS, channels),
        out_weight,
    )
    exchanged = lax.all_to_all(partial_rows, "exp", split_axis=0, concat_axis=0, tiled=True)
    row_count = resid.shape[0] * resid.shape[1]
    mamba_rows = jnp.sum(exchanged.reshape(-1, row_count, D).astype(F32), axis=0)
    hidden_state = resid.reshape(row_count, D).astype(F32) + mamba_rows
    norm_scale = lax.rsqrt(jnp.mean(hidden_state * hidden_state, axis=-1, keepdims=True) + 1e-05)
    tokens = (hidden_state * norm_scale * norm_gain).astype(BF16)
    capacity = 2 * TOPK * row_count // EXPERTS
    splits = lax.axis_size("exp") // EXPERTS
    route_ids = expert_ids.reshape(row_count, TOPK)
    gate_vals = gate_weights.reshape(row_count, TOPK)
    matches = slot_select(route_ids, capacity)
    chosen = jnp.sum(matches.astype(jnp.int32), axis=2).astype(BF16)
    outgoing = jnp.dot(chosen, tokens, preferred_element_type=F32).astype(BF16)
    arrived = lax.all_to_all(
        jnp.tile(outgoing, (splits, 1)), "exp", split_axis=0, concat_axis=0, tiled=True
    )
    own_rows = experts(arrived, w_gate, w_up, w_down)
    returned = lax.all_to_all(
        own_rows.astype(BF16), "exp", split_axis=0, concat_axis=0, tiled=True
    ).astype(F32)
    summed = jnp.sum(returned.reshape(splits, EXPERTS * capacity, D), axis=0)
    weights = jnp.sum(matches.astype(F32) * gate_vals.astype(F32)[None], axis=2)
    expert_out = jnp.dot(weights.T, summed, precision=lax.Precision.HIGHEST)
    return (hidden_state + expert_out).astype(BF16).reshape(resid.shape)


def solution(mesh):
    placed = (
        P("seq", None, "exp"),
        P("seq", None, "exp"),
        P(None, "exp"),
        P("exp"),
        P("exp", None),
        P(None, "exp"),
        P("exp"),
        P(None, "exp"),
        P("exp"),
        P("exp", None),
        P(("seq", "exp"), None, None),
        P(),
        P(("seq", "exp"), None, None),
        P(("seq", "exp"), None, None),
        P("exp", None, "seq"),
        P("exp", None, "seq"),
        P("exp", "seq", None),
    )
    return jax.shard_map(
        per_device,
        mesh=mesh,
        in_specs=placed,
        out_specs=P(("seq", "exp"), None, None),
        check_vma=False,
    )
```

```python
import jax
import jax.numpy as jnp
from jax import lax
from jax.experimental import pallas as pl
from jax.experimental.pallas import tpu as pltpu
from jax.sharding import PartitionSpec as P

D = 4096
STATE = 16
CONV = 4
RANK = 256
EXPERTS = 8
TOPK = 2
DOCS = 4
SECTION = 64
TOKENS = DOCS * SECTION
LANES = 128
F32 = jnp.float32
BF16 = jnp.bfloat16


def z_shift(by):
    return [(y * 4 + z, y * 4 + (z + by) % 4) for y in range(4) for z in range(4)]


def y_shift(by):
    return [(y * 4 + z, (y + by) % 4 * 4 + z) for y in range(4) for z in range(4)]


def x_shift(by):
    return [(x * 2 + c, (x + by) % 4 * 2 + c) for x in range(4) for c in range(2)]


CORE = [(x * 2 + c, x * 2 + 1 - c) for x in range(4) for c in range(2)]


def passed_along(value, axis, by):
    count = lax.axis_size(axis)
    pairs = [(i, i + by) for i in range(count) if 0 <= i + by < count]
    return lax.ppermute(value, axis, pairs)


def from_others(value, shift):
    return [lax.ppermute(value, "exp", shift(by)) for by in (1, 2, 3)]


def swapped(value):
    return lax.ppermute(value, "seq", CORE)


def document_major(back):
    row = lax.broadcasted_iota(jnp.int32, (TOKENS, TOKENS), 0)
    column = lax.broadcasted_iota(jnp.int32, (TOKENS, TOKENS), 1)
    if back:
        source = (row & (DOCS - 1)) * SECTION + (row >> 2)
    else:
        source = (row & (SECTION - 1)) * DOCS + (row >> 6)
    return jnp.where(column == source, 1.0, 0.0).astype(BF16)


def fetched(sources, targets, arrived):
    copies = [
        pltpu.make_async_copy(source, target, arrived.at[index])
        for index, (source, target) in enumerate(zip(sources, targets))
    ]
    for copy in copies:
        copy.start()
    return copies


def mixer_in_kernel(edge, *refs):
    sources, (inner, projected, window, acted, *targets, arrived) = refs[:4], refs[4:]
    copies = fetched(sources, targets, arrived)
    xin, conv_weight, conv_bias, xproj = targets
    window[: CONV - 1] = edge[...].astype(F32)
    for copy in copies[:3]:
        copy.wait()
    window[CONV - 1 :] = xin[...].astype(F32)
    running = jnp.broadcast_to(conv_bias[...][None], acted.shape)
    for offset in range(CONV):
        running = running + conv_weight[offset : offset + 1, :][None] * window[
            offset : offset + SECTION
        ]
    acted[...] = jax.nn.silu(running)
    ordered = jnp.concatenate([acted[:, doc, :] for doc in range(DOCS)], axis=0).astype(BF16)
    inner[...] = ordered
    copies[3].wait()
    projected[...] = lax.dot_general(
        xproj[...], ordered, (((1,), (1,)), ((), ())), preferred_element_type=F32
    ).astype(BF16)


def columns_from(states, doc, group):
    block = states[:, pl.ds(pl.multiple_of((doc >> 1) * LANES, LANES), LANES)]
    offset = (doc & 1) * SECTION + group * 8
    return pltpu.roll(block, (LANES - offset) & (LANES - 1), 1)


def in_all_lanes(turned, index):
    column = jnp.broadcast_to(turned[:, index : index + 1], (turned.shape[0], LANES))
    return jnp.concatenate([column] * 4, axis=1)


def section_kernel(p0, p1, p2, p3, inner, *refs):
    sources, (step, states, packed, taken, *targets, arrived) = refs[:3], refs[3:]
    copies = fetched(sources, targets, arrived)
    dtproj, dt_bias, a_log = targets
    total = (p0[...].astype(F32) + p1[...].astype(F32)) + (
        p2[...].astype(F32) + p3[...].astype(F32)
    )
    low_rank = total[:RANK].astype(BF16)
    states[...] = total[RANK : RANK + 2 * STATE]
    for copy in copies:
        copy.wait()
    step[...] = jax.nn.softplus(
        lax.dot_general(
            low_rank, dtproj[...], (((0,), (0,)), ((), ())), preferred_element_type=F32
        )
        + dt_bias[...]
    )
    taken[...] = step[...] * inner[...].astype(F32)
    rate = -jnp.exp(a_log[...])

    def document(doc, carry):
        def eight(group, state):
            first = pl.multiple_of(doc * SECTION + group * 8, 8)
            steps = step[pl.ds(first, 8), :]
            values = taken[pl.ds(first, 8), :]
            entering = columns_from(states, doc, group)[:STATE]
            for i in range(8):
                factor = jnp.exp(steps[i : i + 1] * rate)
                state = factor * state + values[i : i + 1] * in_all_lanes(entering, i)
            return state

        state = lax.fori_loop(0, SECTION // 8, eight, jnp.zeros(rate.shape, F32), unroll=8)
        packed[pl.ds(pl.multiple_of(doc * STATE, STATE), STATE), :] = state.astype(BF16)
        return carry

    lax.fori_loop(0, DOCS, document, 0)
    sums = jnp.concatenate(
        [
            jnp.sum(step[doc * SECTION : (doc + 1) * SECTION, :], axis=0, keepdims=True)
            for doc in range(DOCS)
        ],
        axis=0,
    )
    high = sums.astype(BF16).astype(F32)
    both = jnp.concatenate([high, sums - high], axis=0)
    packed[DOCS * STATE : DOCS * STATE + 2 * DOCS, :] = both.astype(BF16)


def mixer_out_kernel(
    section,
    *refs,
):
    earlier, refs = refs[:7], refs[7:]
    (
        step,
        states,
        inner,
        a_log,
        skip,
        zin,
        out_weight,
        rows,
        totals,
        finals,
        taken,
        scanned,
        weight,
        finished,
        arrived,
        left,
    ) = refs
    copy = pltpu.make_async_copy(out_weight, weight, arrived)
    copy.start()
    first = section[0] % 2 == 0
    partner = earlier[3][...].astype(F32)
    order = [jnp.where(first, 0.0, partner)]
    for by in (1, 2, 3):
        before = section[0] >= 2 * by
        mine = jnp.where(before, earlier[by - 1][...].astype(F32), 0.0)
        theirs = jnp.where(before, earlier[3 + by][...].astype(F32), 0.0)
        order = [jnp.where(first, mine, theirs), jnp.where(first, theirs, mine)] + order
    for index, packed in enumerate(order):
        both = packed[DOCS * STATE :]
        totals[8 * index : 8 * index + DOCS, :] = both[:DOCS] + both[DOCS:]
        finals[index] = packed[: DOCS * STATE]
    taken[...] = step[...] * inner[...].astype(F32)
    rate = -jnp.exp(a_log[...])

    def document(doc, carry):
        state = jnp.zeros(rate.shape, F32)
        for index in range(len(order)):
            total = totals[pl.ds(8 * index + doc, 1), :]
            final = finals[index, pl.ds(pl.multiple_of(doc * STATE, STATE), STATE), :]
            state = jnp.exp(total * rate) * state + final

        def eight(group, state):
            first = pl.multiple_of(doc * SECTION + group * 8, 8)
            steps = step[pl.ds(first, 8), :]
            values = taken[pl.ds(first, 8), :]
            turned = columns_from(states, doc, group)
            sums = []
            for i in range(8):
                factor = jnp.exp(steps[i : i + 1] * rate)
                state = factor * state + values[i : i + 1] * in_all_lanes(turned[:STATE], i)
                seen = state * in_all_lanes(turned[STATE:], i)
                sums.append(jnp.sum(seen, axis=0, keepdims=True))
            scanned[pl.ds(first, 8), :] = jnp.concatenate(sums, axis=0)
            return state

        lax.fori_loop(0, SECTION // 8, eight, state, unroll=2)
        return carry

    lax.fori_loop(0, DOCS, document, 0)
    gate = jnp.dot(document_major(False), zin[...], preferred_element_type=F32)
    mixed = (scanned[...] + skip[...] * inner[...].astype(F32)) * jax.nn.silu(gate)
    ordered = jnp.dot(
        document_major(True), mixed.astype(BF16), preferred_element_type=F32
    ).astype(BF16)
    copy.wait()
    leaving = []
    for index, low in enumerate(range(0, D, 1024)):
        finished[index] = jnp.dot(
            ordered, weight[:, low : low + 1024], preferred_element_type=F32
        ).astype(BF16)
        leaving.append(
            pltpu.make_async_copy(
                finished.at[index], rows.at[:, pl.ds(low, 1024)], left.at[index]
            )
        )
        leaving[-1].start()
    for copy in leaving:
        copy.wait()


def in_hbm(*values):
    return [pltpu.with_memory_space_constraint(value, pltpu.HBM) for value in values]


def whole(space=None):
    return pl.BlockSpec(memory_space=pltpu.VMEM if space is None else space)


def mixer_in(xin, edge, conv_weight, conv_bias, xproj):
    channels = xin.shape[2]
    return pl.pallas_call(
        mixer_in_kernel,
        out_shape=(
            jax.ShapeDtypeStruct((TOKENS, channels), BF16),
            jax.ShapeDtypeStruct((xproj.shape[0], TOKENS), BF16),
        ),
        in_specs=[whole()] + [whole(pltpu.HBM)] * 4,
        out_specs=(whole(), whole()),
        scratch_shapes=[
            pltpu.VMEM((CONV - 1 + SECTION, DOCS, channels), F32),
            pltpu.VMEM((SECTION, DOCS, channels), F32),
            pltpu.VMEM(xin.shape, BF16),
            pltpu.VMEM(conv_weight.shape, F32),
            pltpu.VMEM(conv_bias.shape, F32),
            pltpu.VMEM(xproj.shape, BF16),
            pltpu.SemaphoreType.DMA((4,)),
        ],
        compiler_params=pltpu.CompilerParams(vmem_limit_bytes=16 << 20),
        name="mixer_in",
    )(edge, *in_hbm(xin, conv_weight, conv_bias, xproj))


def section_scan(parts, dtproj, dt_bias, a_log, inner):
    channels = inner.shape[1]
    return pl.pallas_call(
        section_kernel,
        out_shape=(
            jax.ShapeDtypeStruct((TOKENS, channels), F32),
            jax.ShapeDtypeStruct((2 * STATE, TOKENS), F32),
            jax.ShapeDtypeStruct((DOCS * (STATE + 2), channels), BF16),
        ),
        in_specs=[whole()] * 5 + [whole(pltpu.HBM)] * 3,
        out_specs=(whole(),) * 3,
        scratch_shapes=[
            pltpu.VMEM((TOKENS, channels), F32),
            pltpu.VMEM(dtproj.shape, BF16),
            pltpu.VMEM(dt_bias.shape, F32),
            pltpu.VMEM(a_log.shape, F32),
            pltpu.SemaphoreType.DMA((3,)),
        ],
        compiler_params=pltpu.CompilerParams(vmem_limit_bytes=16 << 20),
        name="section_scan",
    )(*parts, inner, *in_hbm(dtproj, dt_bias, a_log))


def mixer_out(section, earlier, step, states, inner, a_log, skip, zin, out_weight):
    channels = inner.shape[1]
    return pl.pallas_call(
        mixer_out_kernel,
        out_shape=jax.ShapeDtypeStruct((TOKENS, D), BF16),
        in_specs=[whole(pltpu.SMEM)] + [whole()] * 13 + [whole(pltpu.HBM)],
        out_specs=whole(pltpu.HBM),
        scratch_shapes=[
            pltpu.VMEM((64, channels), F32),
            pltpu.VMEM((7, DOCS * STATE, channels), F32),
            pltpu.VMEM((TOKENS, channels), F32),
            pltpu.VMEM((TOKENS, channels), F32),
            pltpu.VMEM(out_weight.shape, BF16),
            pltpu.VMEM((D // 1024, TOKENS, 1024), BF16),
            pltpu.SemaphoreType.DMA,
            pltpu.SemaphoreType.DMA((D // 1024,)),
        ],
        compiler_params=pltpu.CompilerParams(vmem_limit_bytes=32 << 20),
        name="mixer_out",
    )(section, *earlier, step, states, inner, a_log, skip, zin, *in_hbm(out_weight))


def expert_kernel(count, *refs):
    inputs, (w_gate, w_up, w_down, mine, other, rows, total) = refs[:count], refs[count:]
    size = rows.shape[0]
    low = 0
    for part in inputs:
        rows[low : low + part.shape[0], :] = part[...]
        low += part.shape[0]

    def units(block, carry):
        place = pl.ds(pl.multiple_of(block * 256, 256), 256)
        gate_act = jnp.dot(rows[...], w_gate[0, :, place], preferred_element_type=F32)
        up_act = jnp.dot(rows[...], w_up[0, :, place], preferred_element_type=F32)
        hidden = (jax.nn.silu(gate_act) * up_act).astype(BF16)
        for low in range(0, D, 1024):
            term = jnp.dot(
                hidden, w_down[0, place, low : low + 1024], preferred_element_type=F32
            )
            before = jnp.where(block == 0, 0.0, total[:, low : low + 1024])
            total[:, low : low + 1024] = before + term
        return carry

    lax.fori_loop(0, w_down.shape[1] // 256, units, 0)
    mine[...] = total[: size // 2, :].astype(BF16)
    other[...] = total[size // 2 :, :].astype(BF16)


def expert_block(parts, w_gate, w_up, w_down):
    size = sum(part.shape[0] for part in parts)
    units = w_down.shape[1]
    return pl.pallas_call(
        lambda *refs: expert_kernel(len(parts), *refs),
        out_shape=(jax.ShapeDtypeStruct((size // 2, D), BF16),) * 2,
        in_specs=[whole()] * (len(parts) + 3),
        out_specs=(whole(),) * 2,
        scratch_shapes=[pltpu.VMEM((size, D), BF16), pltpu.VMEM((size, D), F32)],
        compiler_params=pltpu.CompilerParams(vmem_limit_bytes=12 << 20),
        cost_estimate=pl.CostEstimate(
            flops=6 * size * D * units,
            bytes_accessed=4 * size * D,
            transcendentals=size * units,
        ),
        name=f"experts_{size}",
    )(*parts, w_gate, w_up, w_down)


def slot_select(route_ids, capacity):
    flat_ids = route_ids.reshape(-1)
    onehot = (flat_ids[:, None] == jnp.arange(EXPERTS, dtype=jnp.int32)[None, :]).astype(jnp.int32)
    before = jnp.sum((jnp.cumsum(onehot, axis=0) - onehot) * onehot, axis=1)
    target = flat_ids * capacity + before
    matches = jnp.arange(EXPERTS * capacity, dtype=jnp.int32)[:, None] == target[None, :]
    return matches.reshape(EXPERTS * capacity, route_ids.shape[0], route_ids.shape[1])


def after(values, *others):
    held = lax.optimization_barrier((tuple(values), others))
    return held[0]


def experts(own, w_gate, w_up, w_down):
    count = own.shape[0]
    half = count // 2

    def paired(mine, other):
        return mine.astype(F32) + swapped(other).astype(F32)

    w_gate, w_up, w_down = [
        pltpu.with_memory_space_constraint(w, pltpu.VMEM) for w in (w_gate, w_up, w_down)
    ]
    left = lax.ppermute(own, "seq", x_shift(1))
    right = lax.ppermute(own, "seq", x_shift(-1))
    own_out = expert_block([own, swapped(own)], w_gate, w_up, w_down)
    left, right = after((left, right), own_out)
    far = [
        lax.ppermute(left[:half], "seq", x_shift(1)),
        lax.ppermute(right[half:], "seq", x_shift(-1)),
    ]
    left_out = expert_block([left, swapped(left)], w_gate, w_up, w_down)
    right_out = expert_block([right, swapped(right)], w_gate, w_up, w_down)
    far, left_out, right_out = lax.optimization_barrier((far, left_out, right_out))
    left_sum, right_sum = paired(*left_out), paired(*right_out)
    from_right = lax.ppermute(left_sum[:half].astype(BF16), "seq", x_shift(-1))
    from_left = lax.ppermute(right_sum[half:].astype(BF16), "seq", x_shift(1))
    far_out = expert_block(far + [swapped(part) for part in far], w_gate, w_up, w_down)
    far_out = after(far_out, from_right, from_left)
    far_sum = paired(*far_out).astype(BF16)
    for_right = lax.ppermute(far_sum[:half], "seq", x_shift(1))
    for_left = lax.ppermute(far_sum[half:], "seq", x_shift(-1))
    own_sum = paired(*own_out)
    to_left = left_sum[half:] + for_left.astype(F32)
    to_right = right_sum[:half] + for_right.astype(F32)
    first_half = own_sum[:half] + from_right.astype(F32)
    second_half = own_sum[half:] + from_left.astype(F32)
    first_half, second_half = lax.optimization_barrier((first_half, second_half))
    then_right = lax.ppermute(to_left.astype(BF16), "seq", x_shift(-1))
    then_left = lax.ppermute(to_right.astype(BF16), "seq", x_shift(1))
    return jnp.concatenate(
        [first_half + then_left.astype(F32), second_half + then_right.astype(F32)]
    )


def per_device(
    xin,
    zin,
    conv_weight,
    conv_bias,
    xproj_weight,
    dtproj_weight,
    dt_bias,
    a_log,
    skip,
    out_weight,
    resid,
    norm_gain,
    expert_ids,
    gate_weights,
    w_gate,
    w_up,
    w_down,
):
    channels = xin.shape[2]
    edge = passed_along(xin[SECTION - (CONV - 1) :], "seq", 1)
    inner, projected = mixer_in(xin, edge, conv_weight, conv_bias[None], xproj_weight.T)
    along_z = [projected] + from_others(projected, z_shift)
    projected = sum(part.astype(F32) for part in along_z).astype(BF16)
    parts = [projected] + from_others(projected, y_shift)
    step, states, packed = section_scan(parts, dtproj_weight, dt_bias[None], a_log, inner)
    columns = [lax.ppermute(packed, "seq", x_shift(by)) for by in (1, 2, 3)]
    partial_rows = mixer_out(
        lax.axis_index("seq").reshape(1),
        columns + [swapped(packed)] + [swapped(column) for column in columns],
        step,
        states,
        inner,
        a_log,
        skip[None],
        zin.reshape(TOKENS, channels),
        out_weight,
    )
    exchanged = lax.all_to_all(partial_rows, "exp", split_axis=0, concat_axis=0, tiled=True)
    row_count = resid.shape[0] * resid.shape[1]
    mamba_rows = jnp.sum(exchanged.reshape(-1, row_count, D).astype(F32), axis=0)
    hidden_state = resid.reshape(row_count, D).astype(F32) + mamba_rows
    norm_scale = lax.rsqrt(jnp.mean(hidden_state * hidden_state, axis=-1, keepdims=True) + 1e-05)
    tokens = (hidden_state * norm_scale * norm_gain).astype(BF16)
    capacity = 2 * TOPK * row_count // EXPERTS
    splits = lax.axis_size("exp") // EXPERTS
    route_ids = expert_ids.reshape(row_count, TOPK)
    gate_vals = gate_weights.reshape(row_count, TOPK)
    matches = slot_select(route_ids, capacity)
    chosen = jnp.sum(matches.astype(jnp.int32), axis=2).astype(BF16)
    outgoing = jnp.dot(chosen, tokens, preferred_element_type=F32).astype(BF16)
    arrived = lax.all_to_all(
        jnp.tile(outgoing, (splits, 1)), "exp", split_axis=0, concat_axis=0, tiled=True
    )
    own_rows = experts(arrived, w_gate, w_up, w_down)
    returned = lax.all_to_all(
        own_rows.astype(BF16), "exp", split_axis=0, concat_axis=0, tiled=True
    ).astype(F32)
    summed = jnp.sum(returned.reshape(splits, EXPERTS * capacity, D), axis=0)
    weights = jnp.sum(matches.astype(F32) * gate_vals.astype(F32)[None], axis=2)
    weights = weights.reshape((-1,) + resid.shape[:2])
    expert_out = jnp.einsum("qab,qd->abd", weights, summed, precision=lax.Precision.HIGHEST)
    return (hidden_state.reshape(resid.shape) + expert_out).astype(BF16)


def solution(mesh):
    placed = (
        P("seq", None, "exp"),
        P("seq", None, "exp"),
        P(None, "exp"),
        P("exp"),
        P("exp", None),
        P(None, "exp"),
        P("exp"),
        P(None, "exp"),
        P("exp"),
        P("exp", None),
        P(("seq", "exp"), None, None),
        P(),
        P(("seq", "exp"), None, None),
        P(("seq", "exp"), None, None),
        P("exp", None, "seq"),
        P("exp", None, "seq"),
        P("exp", "seq", None),
    )
    return jax.shard_map(
        per_device,
        mesh=mesh,
        in_specs=placed,
        out_specs=P(("seq", "exp"), None, None),
        check_vma=False,
    )
```

```python
import jax
import jax.numpy as jnp
from jax import lax
from jax.experimental import pallas as pl
from jax.experimental.pallas import tpu as pltpu
from jax.sharding import PartitionSpec as P

D = 4096
STATE = 16
CONV = 4
RANK = 256
EXPERTS = 8
TOPK = 2
DOCS = 4
SECTION = 64
TOKENS = DOCS * SECTION
LANES = 128
F32 = jnp.float32
BF16 = jnp.bfloat16


def z_shift(by):
    return [(y * 4 + z, y * 4 + (z + by) % 4) for y in range(4) for z in range(4)]


def y_shift(by):
    return [(y * 4 + z, (y + by) % 4 * 4 + z) for y in range(4) for z in range(4)]


def x_shift(by):
    return [(x * 2 + c, (x + by) % 4 * 2 + c) for x in range(4) for c in range(2)]


CORE = [(x * 2 + c, x * 2 + 1 - c) for x in range(4) for c in range(2)]


def passed_along(value, axis, by):
    count = lax.axis_size(axis)
    pairs = [(i, i + by) for i in range(count) if 0 <= i + by < count]
    return lax.ppermute(value, axis, pairs)


def from_others(value, shift):
    return [lax.ppermute(value, "exp", shift(by)) for by in (1, 2, 3)]


def swapped(value):
    return lax.ppermute(value, "seq", CORE)


def document_major(back):
    row = lax.broadcasted_iota(jnp.int32, (TOKENS, TOKENS), 0)
    column = lax.broadcasted_iota(jnp.int32, (TOKENS, TOKENS), 1)
    if back:
        source = (row & (DOCS - 1)) * SECTION + (row >> 2)
    else:
        source = (row & (SECTION - 1)) * DOCS + (row >> 6)
    return jnp.where(column == source, 1.0, 0.0).astype(BF16)


def fetched(sources, targets, arrived):
    copies = [
        pltpu.make_async_copy(source, target, arrived.at[index])
        for index, (source, target) in enumerate(zip(sources, targets))
    ]
    for copy in copies:
        copy.start()
    return copies


def mixer_in_kernel(xin, edge, *refs):
    sources, (inner, projected, window, *targets, arrived) = refs[:3], refs[3:]
    copies = fetched(sources, targets, arrived)
    conv_weight, conv_bias, xproj = targets
    window[16 - edge.shape[0] : 16, :] = edge[...].astype(F32)
    window[16 : 16 + TOKENS, :] = xin[...].astype(F32)
    copies[0].wait()
    copies[1].wait()
    blocks = []
    for low in range(0, TOKENS, 64):
        running = jnp.broadcast_to(conv_bias[...], (64, xin.shape[1]))
        for offset in range(CONV):
            tap = window[pl.ds(low + 16 - DOCS * (CONV - 1 - offset), 64), :]
            running = running + conv_weight[offset : offset + 1, :] * tap
        blocks.append(jax.nn.silu(running).astype(BF16))
    by_position = jnp.concatenate(blocks, axis=0)
    ordered = jnp.dot(document_major(False), by_position, preferred_element_type=F32).astype(BF16)
    inner[...] = ordered
    copies[2].wait()
    projected[...] = lax.dot_general(
        xproj[...], ordered, (((1,), (1,)), ((), ())), preferred_element_type=F32
    ).astype(BF16)


def columns_from(states, doc, group):
    block = states[:, pl.ds(pl.multiple_of((doc >> 1) * LANES, LANES), LANES)]
    offset = (doc & 1) * SECTION + group * 8
    return pltpu.roll(block, (LANES - offset) & (LANES - 1), 1)


def in_all_lanes(turned, index):
    column = jnp.broadcast_to(turned[:, index : index + 1], (turned.shape[0], LANES))
    return jnp.concatenate([column] * 4, axis=1)


def section_kernel(p0, p1, p2, p3, inner, *refs):
    sources, (step, states, packed, taken, *targets, arrived) = refs[:3], refs[3:]
    copies = fetched(sources, targets, arrived)
    dtproj, dt_bias, a_log = targets
    total = (p0[...].astype(F32) + p1[...].astype(F32)) + (
        p2[...].astype(F32) + p3[...].astype(F32)
    )
    low_rank = total[:RANK].astype(BF16)
    states[...] = total[RANK : RANK + 2 * STATE]
    for copy in copies:
        copy.wait()
    step[...] = jax.nn.softplus(
        lax.dot_general(
            low_rank, dtproj[...], (((0,), (0,)), ((), ())), preferred_element_type=F32
        )
        + dt_bias[...]
    )
    taken[...] = step[...] * inner[...].astype(F32)
    rate = -jnp.exp(a_log[...])

    def document(doc, carry):
        def eight(group, state):
            first = pl.multiple_of(doc * SECTION + group * 8, 8)
            steps = step[pl.ds(first, 8), :]
            values = taken[pl.ds(first, 8), :]
            entering = columns_from(states, doc, group)[:STATE]
            for i in range(8):
                factor = jnp.exp(steps[i : i + 1] * rate)
                state = factor * state + values[i : i + 1] * in_all_lanes(entering, i)
            return state

        state = lax.fori_loop(0, SECTION // 8, eight, jnp.zeros(rate.shape, F32), unroll=8)
        packed[pl.ds(pl.multiple_of(doc * STATE, STATE), STATE), :] = state.astype(BF16)
        return carry

    lax.fori_loop(0, DOCS, document, 0)
    sums = jnp.concatenate(
        [
            jnp.sum(step[doc * SECTION : (doc + 1) * SECTION, :], axis=0, keepdims=True)
            for doc in range(DOCS)
        ],
        axis=0,
    )
    high = sums.astype(BF16).astype(F32)
    both = jnp.concatenate([high, sums - high], axis=0)
    packed[DOCS * STATE : DOCS * STATE + 2 * DOCS, :] = both.astype(BF16)


def mixer_out_kernel(
    section,
    *refs,
):
    earlier, refs = refs[:7], refs[7:]
    (
        step,
        states,
        inner,
        a_log,
        skip,
        zin,
        out_weight,
        rows,
        totals,
        finals,
        taken,
        scanned,
        weight,
        finished,
        arrived,
        left,
    ) = refs
    copy = pltpu.make_async_copy(out_weight, weight, arrived)
    copy.start()
    first = section[0] % 2 == 0
    partner = earlier[3][...].astype(F32)
    order = [jnp.where(first, 0.0, partner)]
    for by in (1, 2, 3):
        before = section[0] >= 2 * by
        mine = jnp.where(before, earlier[by - 1][...].astype(F32), 0.0)
        theirs = jnp.where(before, earlier[3 + by][...].astype(F32), 0.0)
        order = [jnp.where(first, mine, theirs), jnp.where(first, theirs, mine)] + order
    for index, packed in enumerate(order):
        both = packed[DOCS * STATE :]
        totals[8 * index : 8 * index + DOCS, :] = both[:DOCS] + both[DOCS:]
        finals[index] = packed[: DOCS * STATE]
    taken[...] = step[...] * inner[...].astype(F32)
    rate = -jnp.exp(a_log[...])

    def document(doc, carry):
        state = jnp.zeros(rate.shape, F32)
        for index in range(len(order)):
            total = totals[pl.ds(8 * index + doc, 1), :]
            final = finals[index, pl.ds(pl.multiple_of(doc * STATE, STATE), STATE), :]
            state = jnp.exp(total * rate) * state + final

        def eight(group, state):
            first = pl.multiple_of(doc * SECTION + group * 8, 8)
            steps = step[pl.ds(first, 8), :]
            values = taken[pl.ds(first, 8), :]
            turned = columns_from(states, doc, group)
            sums = []
            for i in range(8):
                factor = jnp.exp(steps[i : i + 1] * rate)
                state = factor * state + values[i : i + 1] * in_all_lanes(turned[:STATE], i)
                seen = state * in_all_lanes(turned[STATE:], i)
                sums.append(jnp.sum(seen, axis=0, keepdims=True))
            scanned[pl.ds(first, 8), :] = jnp.concatenate(sums, axis=0)
            return state

        lax.fori_loop(0, SECTION // 8, eight, state, unroll=2)
        return carry

    lax.fori_loop(0, DOCS, document, 0)
    gate = jnp.dot(document_major(False), zin[...], preferred_element_type=F32)
    mixed = (scanned[...] + skip[...] * inner[...].astype(F32)) * jax.nn.silu(gate)
    ordered = jnp.dot(
        document_major(True), mixed.astype(BF16), preferred_element_type=F32
    ).astype(BF16)
    copy.wait()
    leaving = []
    for index, low in enumerate(range(0, D, 1024)):
        finished[index] = jnp.dot(
            ordered, weight[:, low : low + 1024], preferred_element_type=F32
        ).astype(BF16)
        leaving.append(
            pltpu.make_async_copy(
                finished.at[index], rows.at[:, pl.ds(low, 1024)], left.at[index]
            )
        )
        leaving[-1].start()
    for copy in leaving:
        copy.wait()


def in_hbm(*values):
    return [pltpu.with_memory_space_constraint(value, pltpu.HBM) for value in values]


def whole(space=None):
    return pl.BlockSpec(memory_space=pltpu.VMEM if space is None else space)


def mixer_in(xin, edge, conv_weight, conv_bias, xproj):
    channels = xin.shape[1]
    return pl.pallas_call(
        mixer_in_kernel,
        out_shape=(
            jax.ShapeDtypeStruct((TOKENS, channels), BF16),
            jax.ShapeDtypeStruct((xproj.shape[0], TOKENS), BF16),
        ),
        in_specs=[whole()] * 2 + [whole(pltpu.HBM)] * 3,
        out_specs=(whole(), whole()),
        scratch_shapes=[
            pltpu.VMEM((16 + TOKENS, channels), F32),
            pltpu.VMEM(conv_weight.shape, F32),
            pltpu.VMEM(conv_bias.shape, F32),
            pltpu.VMEM(xproj.shape, BF16),
            pltpu.SemaphoreType.DMA((3,)),
        ],
        compiler_params=pltpu.CompilerParams(vmem_limit_bytes=16 << 20),
        name="mixer_in",
    )(xin, edge, *in_hbm(conv_weight, conv_bias, xproj))


def section_scan(parts, dtproj, dt_bias, a_log, inner):
    channels = inner.shape[1]
    return pl.pallas_call(
        section_kernel,
        out_shape=(
            jax.ShapeDtypeStruct((TOKENS, channels), F32),
            jax.ShapeDtypeStruct((2 * STATE, TOKENS), F32),
            jax.ShapeDtypeStruct((DOCS * (STATE + 2), channels), BF16),
        ),
        in_specs=[whole()] * 5 + [whole(pltpu.HBM)] * 3,
        out_specs=(whole(),) * 3,
        scratch_shapes=[
            pltpu.VMEM((TOKENS, channels), F32),
            pltpu.VMEM(dtproj.shape, BF16),
            pltpu.VMEM(dt_bias.shape, F32),
            pltpu.VMEM(a_log.shape, F32),
            pltpu.SemaphoreType.DMA((3,)),
        ],
        compiler_params=pltpu.CompilerParams(vmem_limit_bytes=16 << 20),
        name="section_scan",
    )(*parts, inner, *in_hbm(dtproj, dt_bias, a_log))


def mixer_out(section, earlier, step, states, inner, a_log, skip, zin, out_weight):
    channels = inner.shape[1]
    return pl.pallas_call(
        mixer_out_kernel,
        out_shape=jax.ShapeDtypeStruct((TOKENS, D), BF16),
        in_specs=[whole(pltpu.SMEM)] + [whole()] * 13 + [whole(pltpu.HBM)],
        out_specs=whole(pltpu.HBM),
        scratch_shapes=[
            pltpu.VMEM((64, channels), F32),
            pltpu.VMEM((7, DOCS * STATE, channels), F32),
            pltpu.VMEM((TOKENS, channels), F32),
            pltpu.VMEM((TOKENS, channels), F32),
            pltpu.VMEM(out_weight.shape, BF16),
            pltpu.VMEM((D // 1024, TOKENS, 1024), BF16),
            pltpu.SemaphoreType.DMA,
            pltpu.SemaphoreType.DMA((D // 1024,)),
        ],
        compiler_params=pltpu.CompilerParams(vmem_limit_bytes=32 << 20),
        name="mixer_out",
    )(section, *earlier, step, states, inner, a_log, skip, zin, *in_hbm(out_weight))


def expert_kernel(count, *refs):
    inputs, (w_gate, w_up, w_down, mine, other, rows, total) = refs[:count], refs[count:]
    size = rows.shape[0]
    low = 0
    for part in inputs:
        rows[low : low + part.shape[0], :] = part[...]
        low += part.shape[0]

    def units(block, carry):
        place = pl.ds(pl.multiple_of(block * 256, 256), 256)
        gate_act = jnp.dot(rows[...], w_gate[0, :, place], preferred_element_type=F32)
        up_act = jnp.dot(rows[...], w_up[0, :, place], preferred_element_type=F32)
        hidden = (jax.nn.silu(gate_act) * up_act).astype(BF16)
        for low in range(0, D, 1024):
            term = jnp.dot(
                hidden, w_down[0, place, low : low + 1024], preferred_element_type=F32
            )
            before = jnp.where(block == 0, 0.0, total[:, low : low + 1024])
            total[:, low : low + 1024] = before + term
        return carry

    lax.fori_loop(0, w_down.shape[1] // 256, units, 0)
    mine[...] = total[: size // 2, :].astype(BF16)
    other[...] = total[size // 2 :, :].astype(BF16)


def expert_block(parts, w_gate, w_up, w_down):
    size = sum(part.shape[0] for part in parts)
    units = w_down.shape[1]
    return pl.pallas_call(
        lambda *refs: expert_kernel(len(parts), *refs),
        out_shape=(jax.ShapeDtypeStruct((size // 2, D), BF16),) * 2,
        in_specs=[whole()] * (len(parts) + 3),
        out_specs=(whole(),) * 2,
        scratch_shapes=[pltpu.VMEM((size, D), BF16), pltpu.VMEM((size, D), F32)],
        compiler_params=pltpu.CompilerParams(vmem_limit_bytes=12 << 20),
        cost_estimate=pl.CostEstimate(
            flops=6 * size * D * units,
            bytes_accessed=4 * size * D,
            transcendentals=size * units,
        ),
        name=f"experts_{size}",
    )(*parts, w_gate, w_up, w_down)


def slot_select(route_ids, capacity):
    flat_ids = route_ids.reshape(-1)
    onehot = (flat_ids[:, None] == jnp.arange(EXPERTS, dtype=jnp.int32)[None, :]).astype(jnp.int32)
    before = jnp.sum((jnp.cumsum(onehot, axis=0) - onehot) * onehot, axis=1)
    target = flat_ids * capacity + before
    matches = jnp.arange(EXPERTS * capacity, dtype=jnp.int32)[:, None] == target[None, :]
    return matches.reshape(EXPERTS * capacity, route_ids.shape[0], route_ids.shape[1])


def after(values, *others):
    held = lax.optimization_barrier((tuple(values), others))
    return held[0]


def experts(own, w_gate, w_up, w_down):
    count = own.shape[0]
    half = count // 2

    def paired(mine, other):
        return mine.astype(F32) + swapped(other).astype(F32)

    w_gate, w_up, w_down = [
        pltpu.with_memory_space_constraint(w, pltpu.VMEM) for w in (w_gate, w_up, w_down)
    ]
    left = lax.ppermute(own, "seq", x_shift(1))
    right = lax.ppermute(own, "seq", x_shift(-1))
    own_out = expert_block([own, swapped(own)], w_gate, w_up, w_down)
    left, right = after((left, right), own_out)
    far = [
        lax.ppermute(left[:half], "seq", x_shift(1)),
        lax.ppermute(right[half:], "seq", x_shift(-1)),
    ]
    left_out = expert_block([left, swapped(left)], w_gate, w_up, w_down)
    right_out = expert_block([right, swapped(right)], w_gate, w_up, w_down)
    far, left_out, right_out = lax.optimization_barrier((far, left_out, right_out))
    left_sum, right_sum = paired(*left_out), paired(*right_out)
    from_right = lax.ppermute(left_sum[:half].astype(BF16), "seq", x_shift(-1))
    from_left = lax.ppermute(right_sum[half:].astype(BF16), "seq", x_shift(1))
    far_out = expert_block(far + [swapped(part) for part in far], w_gate, w_up, w_down)
    far_out = after(far_out, from_right, from_left)
    far_sum = paired(*far_out).astype(BF16)
    for_right = lax.ppermute(far_sum[:half], "seq", x_shift(1))
    for_left = lax.ppermute(far_sum[half:], "seq", x_shift(-1))
    own_sum = paired(*own_out)
    to_left = left_sum[half:] + for_left.astype(F32)
    to_right = right_sum[:half] + for_right.astype(F32)
    (own_sum,) = after((own_sum,), to_left, to_right)
    first_half = own_sum[:half] + from_right.astype(F32)
    second_half = own_sum[half:] + from_left.astype(F32)
    first_half, second_half = lax.optimization_barrier((first_half, second_half))
    then_right = lax.ppermute(to_left.astype(BF16), "seq", x_shift(-1))
    then_left = lax.ppermute(to_right.astype(BF16), "seq", x_shift(1))
    return jnp.concatenate(
        [first_half + then_left.astype(F32), second_half + then_right.astype(F32)]
    )


def per_device(
    xin,
    zin,
    conv_weight,
    conv_bias,
    xproj_weight,
    dtproj_weight,
    dt_bias,
    a_log,
    skip,
    out_weight,
    resid,
    norm_gain,
    expert_ids,
    gate_weights,
    w_gate,
    w_up,
    w_down,
):
    channels = xin.shape[2]
    xin = xin.reshape(TOKENS, channels)
    edge = passed_along(xin[TOKENS - (CONV - 1) * DOCS :], "seq", 1)
    inner, projected = mixer_in(xin, edge, conv_weight, conv_bias[None], xproj_weight.T)
    along_z = [projected] + from_others(projected, z_shift)
    projected = sum(part.astype(F32) for part in along_z).astype(BF16)
    parts = [projected] + from_others(projected, y_shift)
    step, states, packed = section_scan(parts, dtproj_weight, dt_bias[None], a_log, inner)
    columns = [lax.ppermute(packed, "seq", x_shift(by)) for by in (1, 2, 3)]
    partial_rows = mixer_out(
        lax.axis_index("seq").reshape(1),
        columns + [swapped(packed)] + [swapped(column) for column in columns],
        step,
        states,
        inner,
        a_log,
        skip[None],
        zin.reshape(TOKENS, channels),
        out_weight,
    )
    exchanged = lax.all_to_all(partial_rows, "exp", split_axis=0, concat_axis=0, tiled=True)
    row_count = resid.shape[0] * resid.shape[1]
    mamba_rows = jnp.sum(exchanged.reshape(-1, row_count, D).astype(F32), axis=0)
    hidden_state = resid.reshape(row_count, D).astype(F32) + mamba_rows
    norm_scale = lax.rsqrt(jnp.mean(hidden_state * hidden_state, axis=-1, keepdims=True) + 1e-05)
    tokens = (hidden_state * norm_scale * norm_gain).astype(BF16)
    capacity = 2 * TOPK * row_count // EXPERTS
    splits = lax.axis_size("exp") // EXPERTS
    route_ids = expert_ids.reshape(row_count, TOPK)
    gate_vals = gate_weights.reshape(row_count, TOPK)
    matches = slot_select(route_ids, capacity)
    chosen = jnp.sum(matches.astype(jnp.int32), axis=2).astype(BF16)
    outgoing = jnp.dot(chosen, tokens, preferred_element_type=F32).astype(BF16)
    arrived = lax.all_to_all(
        jnp.tile(outgoing, (splits, 1)), "exp", split_axis=0, concat_axis=0, tiled=True
    )
    own_rows = experts(arrived, w_gate, w_up, w_down)
    returned = lax.all_to_all(
        own_rows.astype(BF16), "exp", split_axis=0, concat_axis=0, tiled=True
    ).astype(F32)
    summed = jnp.sum(returned.reshape(splits, EXPERTS * capacity, D), axis=0)
    weights = jnp.sum(matches.astype(F32) * gate_vals.astype(F32)[None], axis=2)
    weights = weights.reshape((-1,) + resid.shape[:2])
    expert_out = jnp.einsum("qab,qd->abd", weights, summed, precision=lax.Precision.HIGHEST)
    return (hidden_state.reshape(resid.shape) + expert_out).astype(BF16)


def solution(mesh):
    placed = (
        P("seq", None, "exp"),
        P("seq", None, "exp"),
        P(None, "exp"),
        P("exp"),
        P("exp", None),
        P(None, "exp"),
        P("exp"),
        P(None, "exp"),
        P("exp"),
        P("exp", None),
        P(("seq", "exp"), None, None),
        P(),
        P(("seq", "exp"), None, None),
        P(("seq", "exp"), None, None),
        P("exp", None, "seq"),
        P("exp", None, "seq"),
        P("exp", "seq", None),
    )
    return jax.shard_map(
        per_device,
        mesh=mesh,
        in_specs=placed,
        out_specs=P(("seq", "exp"), None, None),
        check_vma=False,
    )
```

```python
import jax
import jax.numpy as jnp
from jax import lax
from jax.experimental import pallas as pl
from jax.experimental.pallas import tpu as pltpu
from jax.sharding import PartitionSpec as P

D = 4096
STATE = 16
CONV = 4
RANK = 256
EXPERTS = 8
TOPK = 2
DOCS = 4
SECTION = 64
TOKENS = DOCS * SECTION
LANES = 128
F32 = jnp.float32
BF16 = jnp.bfloat16


def z_shift(by):
    return [(y * 4 + z, y * 4 + (z + by) % 4) for y in range(4) for z in range(4)]


def y_shift(by):
    return [(y * 4 + z, (y + by) % 4 * 4 + z) for y in range(4) for z in range(4)]


def x_shift(by):
    return [(x * 2 + c, (x + by) % 4 * 2 + c) for x in range(4) for c in range(2)]


CORE = [(x * 2 + c, x * 2 + 1 - c) for x in range(4) for c in range(2)]


def passed_along(value, axis, by):
    count = lax.axis_size(axis)
    pairs = [(i, i + by) for i in range(count) if 0 <= i + by < count]
    return lax.ppermute(value, axis, pairs)


def from_others(value, shift):
    return [lax.ppermute(value, "exp", shift(by)) for by in (1, 2, 3)]


def swapped(value):
    return lax.ppermute(value, "seq", CORE)


def document_major(back):
    row = lax.broadcasted_iota(jnp.int32, (TOKENS, TOKENS), 0)
    column = lax.broadcasted_iota(jnp.int32, (TOKENS, TOKENS), 1)
    if back:
        source = (row & (DOCS - 1)) * SECTION + (row >> 2)
    else:
        source = (row & (SECTION - 1)) * DOCS + (row >> 6)
    return jnp.where(column == source, 1.0, 0.0).astype(BF16)


def fetched(sources, targets, arrived):
    copies = [
        pltpu.make_async_copy(source, target, arrived.at[index])
        for index, (source, target) in enumerate(zip(sources, targets))
    ]
    for copy in copies:
        copy.start()
    return copies


def mixer_in_kernel(xin, edge, *refs):
    sources, (inner, projected, window, *targets, arrived) = refs[:3], refs[3:]
    copies = fetched(sources, targets, arrived)
    conv_weight, conv_bias, xproj = targets
    window[16 - edge.shape[0] : 16, :] = edge[...].astype(F32)
    window[16 : 16 + TOKENS, :] = xin[...].astype(F32)
    copies[0].wait()
    copies[1].wait()
    blocks = []
    for low in range(0, TOKENS, 64):
        running = jnp.broadcast_to(conv_bias[...], (64, xin.shape[1]))
        for offset in range(CONV):
            tap = window[pl.ds(low + 16 - DOCS * (CONV - 1 - offset), 64), :]
            running = running + conv_weight[offset : offset + 1, :] * tap
        blocks.append(jax.nn.silu(running).astype(BF16))
    by_position = jnp.concatenate(blocks, axis=0)
    ordered = jnp.dot(document_major(False), by_position, preferred_element_type=F32).astype(BF16)
    inner[...] = ordered
    copies[2].wait()
    projected[...] = lax.dot_general(
        xproj[...], ordered, (((1,), (1,)), ((), ())), preferred_element_type=F32
    ).astype(BF16)


def columns_from(states, doc, group):
    block = states[:, pl.ds(pl.multiple_of((doc >> 1) * LANES, LANES), LANES)]
    offset = (doc & 1) * SECTION + group * 8
    return pltpu.roll(block, (LANES - offset) & (LANES - 1), 1)


def in_all_lanes(turned, index):
    column = jnp.broadcast_to(turned[:, index : index + 1], (turned.shape[0], LANES))
    return jnp.concatenate([column] * 4, axis=1)


def section_kernel(p0, p1, p2, p3, inner, *refs):
    sources, (step, states, packed, taken, *targets, arrived) = refs[:3], refs[3:]
    copies = fetched(sources, targets, arrived)
    dtproj, dt_bias, a_log = targets
    total = (p0[...].astype(F32) + p1[...].astype(F32)) + (
        p2[...].astype(F32) + p3[...].astype(F32)
    )
    low_rank = total[:RANK].astype(BF16)
    states[...] = total[RANK : RANK + 2 * STATE]
    for copy in copies:
        copy.wait()
    step[...] = jax.nn.softplus(
        lax.dot_general(
            low_rank, dtproj[...], (((0,), (0,)), ((), ())), preferred_element_type=F32
        )
        + dt_bias[...]
    )
    taken[...] = step[...] * inner[...].astype(F32)
    rate = -jnp.exp(a_log[...])

    def document(doc, carry):
        def eight(group, state):
            first = pl.multiple_of(doc * SECTION + group * 8, 8)
            steps = step[pl.ds(first, 8), :]
            values = taken[pl.ds(first, 8), :]
            entering = columns_from(states, doc, group)[:STATE]
            for i in range(8):
                factor = jnp.exp(steps[i : i + 1] * rate)
                state = factor * state + values[i : i + 1] * in_all_lanes(entering, i)
            return state

        state = lax.fori_loop(0, SECTION // 8, eight, jnp.zeros(rate.shape, F32), unroll=8)
        packed[pl.ds(pl.multiple_of(doc * STATE, STATE), STATE), :] = state.astype(BF16)
        return carry

    lax.fori_loop(0, DOCS, document, 0)
    sums = jnp.concatenate(
        [
            jnp.sum(step[doc * SECTION : (doc + 1) * SECTION, :], axis=0, keepdims=True)
            for doc in range(DOCS)
        ],
        axis=0,
    )
    high = sums.astype(BF16).astype(F32)
    both = jnp.concatenate([high, sums - high], axis=0)
    packed[DOCS * STATE : DOCS * STATE + 2 * DOCS, :] = both.astype(BF16)


def mixer_out_kernel(
    section,
    *refs,
):
    earlier, refs = refs[:7], refs[7:]
    (
        step,
        states,
        inner,
        a_log,
        skip,
        zin,
        out_weight,
        rows,
        totals,
        finals,
        taken,
        scanned,
        weight,
        finished,
        arrived,
        left,
    ) = refs
    copy = pltpu.make_async_copy(out_weight, weight, arrived)
    copy.start()
    first = section[0] % 2 == 0
    partner = earlier[3][...].astype(F32)
    order = [jnp.where(first, 0.0, partner)]
    for by in (1, 2, 3):
        before = section[0] >= 2 * by
        mine = jnp.where(before, earlier[by - 1][...].astype(F32), 0.0)
        theirs = jnp.where(before, earlier[3 + by][...].astype(F32), 0.0)
        order = [jnp.where(first, mine, theirs), jnp.where(first, theirs, mine)] + order
    for index, packed in enumerate(order):
        both = packed[DOCS * STATE :]
        totals[8 * index : 8 * index + DOCS, :] = both[:DOCS] + both[DOCS:]
        finals[index] = packed[: DOCS * STATE]
    taken[...] = step[...] * inner[...].astype(F32)
    rate = -jnp.exp(a_log[...])

    def document(doc, carry):
        state = jnp.zeros(rate.shape, F32)
        for index in range(len(order)):
            total = totals[pl.ds(8 * index + doc, 1), :]
            final = finals[index, pl.ds(pl.multiple_of(doc * STATE, STATE), STATE), :]
            state = jnp.exp(total * rate) * state + final

        def eight(group, state):
            first = pl.multiple_of(doc * SECTION + group * 8, 8)
            steps = step[pl.ds(first, 8), :]
            values = taken[pl.ds(first, 8), :]
            turned = columns_from(states, doc, group)
            sums = []
            for i in range(8):
                factor = jnp.exp(steps[i : i + 1] * rate)
                state = factor * state + values[i : i + 1] * in_all_lanes(turned[:STATE], i)
                seen = state * in_all_lanes(turned[STATE:], i)
                sums.append(jnp.sum(seen, axis=0, keepdims=True))
            scanned[pl.ds(first, 8), :] = jnp.concatenate(sums, axis=0)
            return state

        lax.fori_loop(0, SECTION // 8, eight, state, unroll=2)
        return carry

    lax.fori_loop(0, DOCS, document, 0)
    gate = jnp.dot(document_major(False), zin[...], preferred_element_type=F32)
    mixed = (scanned[...] + skip[...] * inner[...].astype(F32)) * jax.nn.silu(gate)
    ordered = jnp.dot(
        document_major(True), mixed.astype(BF16), preferred_element_type=F32
    ).astype(BF16)
    copy.wait()
    leaving = []
    for index, low in enumerate(range(0, D, 1024)):
        finished[index] = jnp.dot(
            ordered, weight[:, low : low + 1024], preferred_element_type=F32
        ).astype(BF16)
        leaving.append(
            pltpu.make_async_copy(
                finished.at[index], rows.at[:, pl.ds(low, 1024)], left.at[index]
            )
        )
        leaving[-1].start()
    for copy in leaving:
        copy.wait()


def in_hbm(*values):
    return [pltpu.with_memory_space_constraint(value, pltpu.HBM) for value in values]


def whole(space=None):
    return pl.BlockSpec(memory_space=pltpu.VMEM if space is None else space)


def mixer_in(xin, edge, conv_weight, conv_bias, xproj):
    channels = xin.shape[1]
    return pl.pallas_call(
        mixer_in_kernel,
        out_shape=(
            jax.ShapeDtypeStruct((TOKENS, channels), BF16),
            jax.ShapeDtypeStruct((xproj.shape[0], TOKENS), BF16),
        ),
        in_specs=[whole()] * 2 + [whole(pltpu.HBM)] * 3,
        out_specs=(whole(), whole()),
        scratch_shapes=[
            pltpu.VMEM((16 + TOKENS, channels), F32),
            pltpu.VMEM(conv_weight.shape, F32),
            pltpu.VMEM(conv_bias.shape, F32),
            pltpu.VMEM(xproj.shape, BF16),
            pltpu.SemaphoreType.DMA((3,)),
        ],
        compiler_params=pltpu.CompilerParams(vmem_limit_bytes=16 << 20),
        name="mixer_in",
    )(xin, edge, *in_hbm(conv_weight, conv_bias, xproj))


def section_scan(parts, dtproj, dt_bias, a_log, inner):
    channels = inner.shape[1]
    return pl.pallas_call(
        section_kernel,
        out_shape=(
            jax.ShapeDtypeStruct((TOKENS, channels), F32),
            jax.ShapeDtypeStruct((2 * STATE, TOKENS), F32),
            jax.ShapeDtypeStruct((DOCS * (STATE + 2), channels), BF16),
        ),
        in_specs=[whole()] * 5 + [whole(pltpu.HBM)] * 3,
        out_specs=(whole(),) * 3,
        scratch_shapes=[
            pltpu.VMEM((TOKENS, channels), F32),
            pltpu.VMEM(dtproj.shape, BF16),
            pltpu.VMEM(dt_bias.shape, F32),
            pltpu.VMEM(a_log.shape, F32),
            pltpu.SemaphoreType.DMA((3,)),
        ],
        compiler_params=pltpu.CompilerParams(vmem_limit_bytes=16 << 20),
        name="section_scan",
    )(*parts, inner, *in_hbm(dtproj, dt_bias, a_log))


def mixer_out(section, earlier, step, states, inner, a_log, skip, zin, out_weight):
    channels = inner.shape[1]
    return pl.pallas_call(
        mixer_out_kernel,
        out_shape=jax.ShapeDtypeStruct((TOKENS, D), BF16),
        in_specs=[whole(pltpu.SMEM)] + [whole()] * 13 + [whole(pltpu.HBM)],
        out_specs=whole(pltpu.HBM),
        scratch_shapes=[
            pltpu.VMEM((64, channels), F32),
            pltpu.VMEM((7, DOCS * STATE, channels), F32),
            pltpu.VMEM((TOKENS, channels), F32),
            pltpu.VMEM((TOKENS, channels), F32),
            pltpu.VMEM(out_weight.shape, BF16),
            pltpu.VMEM((D // 1024, TOKENS, 1024), BF16),
            pltpu.SemaphoreType.DMA,
            pltpu.SemaphoreType.DMA((D // 1024,)),
        ],
        compiler_params=pltpu.CompilerParams(vmem_limit_bytes=32 << 20),
        name="mixer_out",
    )(section, *earlier, step, states, inner, a_log, skip, zin, *in_hbm(out_weight))


def expert_kernel(count, *refs):
    inputs, (w_gate, w_up, w_down, mine, other, rows, total) = refs[:count], refs[count:]
    size = rows.shape[0]
    low = 0
    for part in inputs:
        rows[low : low + part.shape[0], :] = part[...]
        low += part.shape[0]

    def units(block, carry):
        place = pl.ds(pl.multiple_of(block * 256, 256), 256)
        gate_act = jnp.dot(rows[...], w_gate[0, :, place], preferred_element_type=F32)
        up_act = jnp.dot(rows[...], w_up[0, :, place], preferred_element_type=F32)
        hidden = (jax.nn.silu(gate_act) * up_act).astype(BF16)
        for low in range(0, D, 1024):
            term = jnp.dot(
                hidden, w_down[0, place, low : low + 1024], preferred_element_type=F32
            )
            before = jnp.where(block == 0, 0.0, total[:, low : low + 1024])
            total[:, low : low + 1024] = before + term
        return carry

    lax.fori_loop(0, w_down.shape[1] // 256, units, 0)
    mine[...] = total[: size // 2, :].astype(BF16)
    other[...] = total[size // 2 :, :].astype(BF16)


def expert_block(parts, w_gate, w_up, w_down):
    size = sum(part.shape[0] for part in parts)
    units = w_down.shape[1]
    return pl.pallas_call(
        lambda *refs: expert_kernel(len(parts), *refs),
        out_shape=(jax.ShapeDtypeStruct((size // 2, D), BF16),) * 2,
        in_specs=[whole()] * (len(parts) + 3),
        out_specs=(whole(),) * 2,
        scratch_shapes=[pltpu.VMEM((size, D), BF16), pltpu.VMEM((size, D), F32)],
        compiler_params=pltpu.CompilerParams(vmem_limit_bytes=12 << 20),
        cost_estimate=pl.CostEstimate(
            flops=6 * size * D * units,
            bytes_accessed=4 * size * D,
            transcendentals=size * units,
        ),
        name=f"experts_{size}",
    )(*parts, w_gate, w_up, w_down)


def slot_select(route_ids, capacity):
    flat_ids = route_ids.reshape(-1)
    onehot = (flat_ids[:, None] == jnp.arange(EXPERTS, dtype=jnp.int32)[None, :]).astype(jnp.int32)
    before = jnp.sum((jnp.cumsum(onehot, axis=0) - onehot) * onehot, axis=1)
    target = flat_ids * capacity + before
    matches = jnp.arange(EXPERTS * capacity, dtype=jnp.int32)[:, None] == target[None, :]
    return matches.reshape(EXPERTS * capacity, route_ids.shape[0], route_ids.shape[1])


def after(values, *others):
    held = lax.optimization_barrier((tuple(values), others))
    return held[0]


def experts(own, w_gate, w_up, w_down):
    count = own.shape[0]
    half = count // 2

    def paired(mine, other):
        return mine.astype(F32) + swapped(other).astype(F32)

    w_gate, w_up, w_down = [
        pltpu.with_memory_space_constraint(w, pltpu.VMEM) for w in (w_gate, w_up, w_down)
    ]
    left = lax.ppermute(own, "seq", x_shift(1))
    right = lax.ppermute(own, "seq", x_shift(-1))
    own_out = expert_block([own, swapped(own)], w_gate, w_up, w_down)
    own_sum = paired(*own_out)
    left, right = after((left, right), own_sum)
    far = [
        lax.ppermute(left[:half], "seq", x_shift(1)),
        lax.ppermute(right[half:], "seq", x_shift(-1)),
    ]
    left_out = expert_block([left, swapped(left)], w_gate, w_up, w_down)
    right_out = expert_block([right, swapped(right)], w_gate, w_up, w_down)
    far, left_out, right_out = lax.optimization_barrier((far, left_out, right_out))
    left_sum, right_sum = paired(*left_out), paired(*right_out)
    from_right = lax.ppermute(left_sum[:half].astype(BF16), "seq", x_shift(-1))
    from_left = lax.ppermute(right_sum[half:].astype(BF16), "seq", x_shift(1))
    far_out = expert_block(far + [swapped(part) for part in far], w_gate, w_up, w_down)
    far_out = after(far_out, from_right, from_left)
    far_sum = paired(*far_out).astype(BF16)
    for_right = lax.ppermute(far_sum[:half], "seq", x_shift(1))
    for_left = lax.ppermute(far_sum[half:], "seq", x_shift(-1))
    to_left = left_sum[half:] + for_left.astype(F32)
    to_right = right_sum[:half] + for_right.astype(F32)
    (own_sum,) = after((own_sum,), to_left, to_right)
    first_half = own_sum[:half] + from_right.astype(F32)
    second_half = own_sum[half:] + from_left.astype(F32)
    first_half, second_half = lax.optimization_barrier((first_half, second_half))
    then_right = lax.ppermute(to_left.astype(BF16), "seq", x_shift(-1))
    then_left = lax.ppermute(to_right.astype(BF16), "seq", x_shift(1))
    return jnp.concatenate(
        [first_half + then_left.astype(F32), second_half + then_right.astype(F32)]
    )


def per_device(
    xin,
    zin,
    conv_weight,
    conv_bias,
    xproj_weight,
    dtproj_weight,
    dt_bias,
    a_log,
    skip,
    out_weight,
    resid,
    norm_gain,
    expert_ids,
    gate_weights,
    w_gate,
    w_up,
    w_down,
):
    channels = xin.shape[2]
    xin = xin.reshape(TOKENS, channels)
    edge = passed_along(xin[TOKENS - (CONV - 1) * DOCS :], "seq", 1)
    inner, projected = mixer_in(xin, edge, conv_weight, conv_bias[None], xproj_weight.T)
    along_z = [projected] + from_others(projected, z_shift)
    projected = sum(part.astype(F32) for part in along_z).astype(BF16)
    parts = [projected] + from_others(projected, y_shift)
    step, states, packed = section_scan(parts, dtproj_weight, dt_bias[None], a_log, inner)
    columns = [lax.ppermute(packed, "seq", x_shift(by)) for by in (1, 2, 3)]
    partial_rows = mixer_out(
        lax.axis_index("seq").reshape(1),
        columns + [swapped(packed)] + [swapped(column) for column in columns],
        step,
        states,
        inner,
        a_log,
        skip[None],
        zin.reshape(TOKENS, channels),
        out_weight,
    )
    exchanged = lax.all_to_all(partial_rows, "exp", split_axis=0, concat_axis=0, tiled=True)
    row_count = resid.shape[0] * resid.shape[1]
    mamba_rows = jnp.sum(exchanged.reshape(-1, row_count, D).astype(F32), axis=0)
    hidden_state = resid.reshape(row_count, D).astype(F32) + mamba_rows
    norm_scale = lax.rsqrt(jnp.mean(hidden_state * hidden_state, axis=-1, keepdims=True) + 1e-05)
    tokens = (hidden_state * norm_scale * norm_gain).astype(BF16)
    capacity = 2 * TOPK * row_count // EXPERTS
    splits = lax.axis_size("exp") // EXPERTS
    route_ids = expert_ids.reshape(row_count, TOPK)
    gate_vals = gate_weights.reshape(row_count, TOPK)
    matches = slot_select(route_ids, capacity)
    chosen = jnp.sum(matches.astype(jnp.int32), axis=2).astype(BF16)
    outgoing = jnp.dot(chosen, tokens, preferred_element_type=F32).astype(BF16)
    arrived = lax.all_to_all(
        jnp.tile(outgoing, (splits, 1)), "exp", split_axis=0, concat_axis=0, tiled=True
    )
    own_rows = experts(arrived, w_gate, w_up, w_down)
    returned = lax.all_to_all(
        own_rows.astype(BF16), "exp", split_axis=0, concat_axis=0, tiled=True
    ).astype(F32)
    summed = jnp.sum(returned.reshape(splits, EXPERTS * capacity, D), axis=0)
    weights = jnp.sum(matches.astype(F32) * gate_vals.astype(F32)[None], axis=2)
    weights = weights.reshape((-1,) + resid.shape[:2])
    expert_out = jnp.einsum("qab,qd->abd", weights, summed, precision=lax.Precision.HIGHEST)
    return (hidden_state.reshape(resid.shape) + expert_out).astype(BF16)


def solution(mesh):
    placed = (
        P("seq", None, "exp"),
        P("seq", None, "exp"),
        P(None, "exp"),
        P("exp"),
        P("exp", None),
        P(None, "exp"),
        P("exp"),
        P(None, "exp"),
        P("exp"),
        P("exp", None),
        P(("seq", "exp"), None, None),
        P(),
        P(("seq", "exp"), None, None),
        P(("seq", "exp"), None, None),
        P("exp", None, "seq"),
        P("exp", None, "seq"),
        P("exp", "seq", None),
    )
    return jax.shard_map(
        per_device,
        mesh=mesh,
        in_specs=placed,
        out_specs=P(("seq", "exp"), None, None),
        check_vma=False,
    )
```

```python
import jax
import jax.numpy as jnp
from jax import lax
from jax.experimental import pallas as pl
from jax.experimental.pallas import tpu as pltpu
from jax.sharding import PartitionSpec as P

D = 4096
STATE = 16
CONV = 4
RANK = 256
EXPERTS = 8
TOPK = 2
DOCS = 4
SECTION = 64
TOKENS = DOCS * SECTION
LANES = 128
F32 = jnp.float32
BF16 = jnp.bfloat16


def z_shift(by):
    return [(y * 4 + z, y * 4 + (z + by) % 4) for y in range(4) for z in range(4)]


def y_shift(by):
    return [(y * 4 + z, (y + by) % 4 * 4 + z) for y in range(4) for z in range(4)]


def x_shift(by):
    return [(x * 2 + c, (x + by) % 4 * 2 + c) for x in range(4) for c in range(2)]


CORE = [(x * 2 + c, x * 2 + 1 - c) for x in range(4) for c in range(2)]


def passed_along(value, axis, by):
    count = lax.axis_size(axis)
    pairs = [(i, i + by) for i in range(count) if 0 <= i + by < count]
    return lax.ppermute(value, axis, pairs)


def from_others(value, shift):
    return [lax.ppermute(value, "exp", shift(by)) for by in (1, 2, 3)]


def swapped(value):
    return lax.ppermute(value, "seq", CORE)


def document_major(back):
    row = lax.broadcasted_iota(jnp.int32, (TOKENS, TOKENS), 0)
    column = lax.broadcasted_iota(jnp.int32, (TOKENS, TOKENS), 1)
    if back:
        source = (row & (DOCS - 1)) * SECTION + (row >> 2)
    else:
        source = (row & (SECTION - 1)) * DOCS + (row >> 6)
    return jnp.where(column == source, 1.0, 0.0).astype(BF16)


def fetched(sources, targets, arrived):
    copies = [
        pltpu.make_async_copy(source, target, arrived.at[index])
        for index, (source, target) in enumerate(zip(sources, targets))
    ]
    for copy in copies:
        copy.start()
    return copies


def mixer_in_kernel(xin, edge, *refs):
    sources, (inner, projected, window, *targets, arrived) = refs[:3], refs[3:]
    copies = fetched(sources, targets, arrived)
    conv_weight, conv_bias, xproj = targets
    window[16 - edge.shape[0] : 16, :] = edge[...].astype(F32)
    window[16 : 16 + TOKENS, :] = xin[...].astype(F32)
    copies[0].wait()
    copies[1].wait()
    blocks = []
    for low in range(0, TOKENS, 64):
        running = jnp.broadcast_to(conv_bias[...], (64, xin.shape[1]))
        for offset in range(CONV):
            tap = window[pl.ds(low + 16 - DOCS * (CONV - 1 - offset), 64), :]
            running = running + conv_weight[offset : offset + 1, :] * tap
        blocks.append(jax.nn.silu(running).astype(BF16))
    by_position = jnp.concatenate(blocks, axis=0)
    ordered = jnp.dot(document_major(False), by_position, preferred_element_type=F32).astype(BF16)
    inner[...] = ordered
    copies[2].wait()
    projected[...] = lax.dot_general(
        xproj[...], ordered, (((1,), (1,)), ((), ())), preferred_element_type=F32
    ).astype(BF16)


def columns_from(states, doc, group):
    block = states[:, pl.ds(pl.multiple_of((doc >> 1) * LANES, LANES), LANES)]
    offset = (doc & 1) * SECTION + group * 8
    return pltpu.roll(block, (LANES - offset) & (LANES - 1), 1)


def in_all_lanes(turned, index):
    column = jnp.broadcast_to(turned[:, index : index + 1], (turned.shape[0], LANES))
    return jnp.concatenate([column] * 4, axis=1)


def section_kernel(p0, p1, p2, p3, inner, *refs):
    sources, (step, states, packed, taken, *targets, arrived) = refs[:3], refs[3:]
    copies = fetched(sources, targets, arrived)
    dtproj, dt_bias, a_log = targets
    total = (p0[...].astype(F32) + p1[...].astype(F32)) + (
        p2[...].astype(F32) + p3[...].astype(F32)
    )
    low_rank = total[:RANK].astype(BF16)
    states[...] = total[RANK : RANK + 2 * STATE]
    for copy in copies:
        copy.wait()
    step[...] = jax.nn.softplus(
        lax.dot_general(
            low_rank, dtproj[...], (((0,), (0,)), ((), ())), preferred_element_type=F32
        )
        + dt_bias[...]
    )
    taken[...] = step[...] * inner[...].astype(F32)
    rate = -jnp.exp(a_log[...])

    def document(doc, carry):
        def eight(group, state):
            first = pl.multiple_of(doc * SECTION + group * 8, 8)
            steps = step[pl.ds(first, 8), :]
            values = taken[pl.ds(first, 8), :]
            entering = columns_from(states, doc, group)[:STATE]
            for i in range(8):
                factor = jnp.exp(steps[i : i + 1] * rate)
                state = factor * state + values[i : i + 1] * in_all_lanes(entering, i)
            return state

        state = lax.fori_loop(0, SECTION // 8, eight, jnp.zeros(rate.shape, F32), unroll=8)
        packed[pl.ds(pl.multiple_of(doc * STATE, STATE), STATE), :] = state.astype(BF16)
        return carry

    lax.fori_loop(0, DOCS, document, 0)
    sums = jnp.concatenate(
        [
            jnp.sum(step[doc * SECTION : (doc + 1) * SECTION, :], axis=0, keepdims=True)
            for doc in range(DOCS)
        ],
        axis=0,
    )
    high = sums.astype(BF16).astype(F32)
    both = jnp.concatenate([high, sums - high], axis=0)
    packed[DOCS * STATE : DOCS * STATE + 2 * DOCS, :] = both.astype(BF16)


def mixer_out_kernel(
    section,
    *refs,
):
    earlier, refs = refs[:7], refs[7:]
    (
        step,
        states,
        inner,
        a_log,
        skip,
        zin,
        out_weight,
        rows,
        totals,
        finals,
        taken,
        scanned,
        weight,
        finished,
        arrived,
        left,
    ) = refs
    copy = pltpu.make_async_copy(out_weight, weight, arrived)
    copy.start()
    first = section[0] % 2 == 0
    partner = earlier[3][...].astype(F32)
    order = [jnp.where(first, 0.0, partner)]
    for by in (1, 2, 3):
        before = section[0] >= 2 * by
        mine = jnp.where(before, earlier[by - 1][...].astype(F32), 0.0)
        theirs = jnp.where(before, earlier[3 + by][...].astype(F32), 0.0)
        order = [jnp.where(first, mine, theirs), jnp.where(first, theirs, mine)] + order
    for index, packed in enumerate(order):
        both = packed[DOCS * STATE :]
        totals[8 * index : 8 * index + DOCS, :] = both[:DOCS] + both[DOCS:]
        finals[index] = packed[: DOCS * STATE]
    taken[...] = step[...] * inner[...].astype(F32)
    rate = -jnp.exp(a_log[...])

    def document(doc, carry):
        state = jnp.zeros(rate.shape, F32)
        for index in range(len(order)):
            total = totals[pl.ds(8 * index + doc, 1), :]
            final = finals[index, pl.ds(pl.multiple_of(doc * STATE, STATE), STATE), :]
            state = jnp.exp(total * rate) * state + final

        def eight(group, state):
            first = pl.multiple_of(doc * SECTION + group * 8, 8)
            steps = step[pl.ds(first, 8), :]
            values = taken[pl.ds(first, 8), :]
            turned = columns_from(states, doc, group)
            sums = []
            for i in range(8):
                factor = jnp.exp(steps[i : i + 1] * rate)
                state = factor * state + values[i : i + 1] * in_all_lanes(turned[:STATE], i)
                seen = state * in_all_lanes(turned[STATE:], i)
                sums.append(jnp.sum(seen, axis=0, keepdims=True))
            scanned[pl.ds(first, 8), :] = jnp.concatenate(sums, axis=0)
            return state

        lax.fori_loop(0, SECTION // 8, eight, state, unroll=2)
        return carry

    lax.fori_loop(0, DOCS, document, 0)
    gate = jnp.dot(document_major(False), zin[...], preferred_element_type=F32)
    mixed = (scanned[...] + skip[...] * inner[...].astype(F32)) * jax.nn.silu(gate)
    ordered = jnp.dot(
        document_major(True), mixed.astype(BF16), preferred_element_type=F32
    ).astype(BF16)
    copy.wait()
    leaving = []
    for index, low in enumerate(range(0, D, 1024)):
        finished[index] = jnp.dot(
            ordered, weight[:, low : low + 1024], preferred_element_type=F32
        ).astype(BF16)
        leaving.append(
            pltpu.make_async_copy(
                finished.at[index], rows.at[:, pl.ds(low, 1024)], left.at[index]
            )
        )
        leaving[-1].start()
    for copy in leaving:
        copy.wait()


def in_hbm(*values):
    return [pltpu.with_memory_space_constraint(value, pltpu.HBM) for value in values]


def whole(space=None):
    return pl.BlockSpec(memory_space=pltpu.VMEM if space is None else space)


def mixer_in(xin, edge, conv_weight, conv_bias, xproj):
    channels = xin.shape[1]
    return pl.pallas_call(
        mixer_in_kernel,
        out_shape=(
            jax.ShapeDtypeStruct((TOKENS, channels), BF16),
            jax.ShapeDtypeStruct((xproj.shape[0], TOKENS), BF16),
        ),
        in_specs=[whole()] * 2 + [whole(pltpu.HBM)] * 3,
        out_specs=(whole(), whole()),
        scratch_shapes=[
            pltpu.VMEM((16 + TOKENS, channels), F32),
            pltpu.VMEM(conv_weight.shape, F32),
            pltpu.VMEM(conv_bias.shape, F32),
            pltpu.VMEM(xproj.shape, BF16),
            pltpu.SemaphoreType.DMA((3,)),
        ],
        compiler_params=pltpu.CompilerParams(vmem_limit_bytes=16 << 20),
        name="mixer_in",
    )(xin, edge, *in_hbm(conv_weight, conv_bias, xproj))


def section_scan(parts, dtproj, dt_bias, a_log, inner):
    channels = inner.shape[1]
    return pl.pallas_call(
        section_kernel,
        out_shape=(
            jax.ShapeDtypeStruct((TOKENS, channels), F32),
            jax.ShapeDtypeStruct((2 * STATE, TOKENS), F32),
            jax.ShapeDtypeStruct((DOCS * (STATE + 2), channels), BF16),
        ),
        in_specs=[whole()] * 5 + [whole(pltpu.HBM)] * 3,
        out_specs=(whole(),) * 3,
        scratch_shapes=[
            pltpu.VMEM((TOKENS, channels), F32),
            pltpu.VMEM(dtproj.shape, BF16),
            pltpu.VMEM(dt_bias.shape, F32),
            pltpu.VMEM(a_log.shape, F32),
            pltpu.SemaphoreType.DMA((3,)),
        ],
        compiler_params=pltpu.CompilerParams(vmem_limit_bytes=16 << 20),
        name="section_scan",
    )(*parts, inner, *in_hbm(dtproj, dt_bias, a_log))


def mixer_out(section, earlier, step, states, inner, a_log, skip, zin, out_weight):
    channels = inner.shape[1]
    return pl.pallas_call(
        mixer_out_kernel,
        out_shape=jax.ShapeDtypeStruct((TOKENS, D), BF16),
        in_specs=[whole(pltpu.SMEM)] + [whole()] * 13 + [whole(pltpu.HBM)],
        out_specs=whole(pltpu.HBM),
        scratch_shapes=[
            pltpu.VMEM((64, channels), F32),
            pltpu.VMEM((7, DOCS * STATE, channels), F32),
            pltpu.VMEM((TOKENS, channels), F32),
            pltpu.VMEM((TOKENS, channels), F32),
            pltpu.VMEM(out_weight.shape, BF16),
            pltpu.VMEM((D // 1024, TOKENS, 1024), BF16),
            pltpu.SemaphoreType.DMA,
            pltpu.SemaphoreType.DMA((D // 1024,)),
        ],
        compiler_params=pltpu.CompilerParams(vmem_limit_bytes=32 << 20),
        name="mixer_out",
    )(section, *earlier, step, states, inner, a_log, skip, zin, *in_hbm(out_weight))


def expert_kernel(count, *refs):
    inputs, (w_gate, w_up, w_down, mine, other, rows, total) = refs[:count], refs[count:]
    size = rows.shape[0]
    low = 0
    for part in inputs:
        rows[low : low + part.shape[0], :] = part[...]
        low += part.shape[0]

    def units(block, carry):
        place = pl.ds(pl.multiple_of(block * 256, 256), 256)
        gate_act = jnp.dot(rows[...], w_gate[0, :, place], preferred_element_type=F32)
        up_act = jnp.dot(rows[...], w_up[0, :, place], preferred_element_type=F32)
        hidden = (jax.nn.silu(gate_act) * up_act).astype(BF16)
        for low in range(0, D, 1024):
            term = jnp.dot(
                hidden, w_down[0, place, low : low + 1024], preferred_element_type=F32
            )
            before = jnp.where(block == 0, 0.0, total[:, low : low + 1024])
            total[:, low : low + 1024] = before + term
        return carry

    lax.fori_loop(0, w_down.shape[1] // 256, units, 0)
    mine[...] = total[: size // 2, :].astype(BF16)
    other[...] = total[size // 2 :, :].astype(BF16)


def expert_block(parts, w_gate, w_up, w_down):
    size = sum(part.shape[0] for part in parts)
    units = w_down.shape[1]
    return pl.pallas_call(
        lambda *refs: expert_kernel(len(parts), *refs),
        out_shape=(jax.ShapeDtypeStruct((size // 2, D), BF16),) * 2,
        in_specs=[whole()] * (len(parts) + 3),
        out_specs=(whole(),) * 2,
        scratch_shapes=[pltpu.VMEM((size, D), BF16), pltpu.VMEM((size, D), F32)],
        compiler_params=pltpu.CompilerParams(vmem_limit_bytes=12 << 20),
        cost_estimate=pl.CostEstimate(
            flops=6 * size * D * units,
            bytes_accessed=4 * size * D,
            transcendentals=size * units,
        ),
        name=f"experts_{size}",
    )(*parts, w_gate, w_up, w_down)


def slot_select(route_ids, capacity):
    flat_ids = route_ids.reshape(-1)
    onehot = (flat_ids[:, None] == jnp.arange(EXPERTS, dtype=jnp.int32)[None, :]).astype(jnp.int32)
    before = jnp.sum((jnp.cumsum(onehot, axis=0) - onehot) * onehot, axis=1)
    target = flat_ids * capacity + before
    matches = jnp.arange(EXPERTS * capacity, dtype=jnp.int32)[:, None] == target[None, :]
    return matches.reshape(EXPERTS * capacity, route_ids.shape[0], route_ids.shape[1])


def after(values, *others):
    held = lax.optimization_barrier((tuple(values), others))
    return held[0]


def experts(own, w_gate, w_up, w_down):
    count = own.shape[0]
    half = count // 2

    def paired(mine, other):
        return mine.astype(F32) + swapped(other).astype(F32)

    w_gate, w_up, w_down = [
        pltpu.with_memory_space_constraint(w, pltpu.VMEM) for w in (w_gate, w_up, w_down)
    ]
    left = lax.ppermute(own, "seq", x_shift(1))
    right = lax.ppermute(own, "seq", x_shift(-1))
    own_out = expert_block([own, swapped(own)], w_gate, w_up, w_down)
    left, right = after((left, right), own_out)
    far = [
        lax.ppermute(left[:half], "seq", x_shift(1)),
        lax.ppermute(right[half:], "seq", x_shift(-1)),
    ]
    left_out = expert_block([left, swapped(left)], w_gate, w_up, w_down)
    right_out = expert_block([right, swapped(right)], w_gate, w_up, w_down)
    own_sum = paired(*own_out)
    far, left_out, right_out, own_sum = lax.optimization_barrier(
        (far, left_out, right_out, own_sum)
    )
    left_sum, right_sum = paired(*left_out), paired(*right_out)
    from_right = lax.ppermute(left_sum[:half].astype(BF16), "seq", x_shift(-1))
    from_left = lax.ppermute(right_sum[half:].astype(BF16), "seq", x_shift(1))
    far_out = expert_block(far + [swapped(part) for part in far], w_gate, w_up, w_down)
    far_out = after(far_out, from_right, from_left)
    far_sum = paired(*far_out).astype(BF16)
    for_right = lax.ppermute(far_sum[:half], "seq", x_shift(1))
    for_left = lax.ppermute(far_sum[half:], "seq", x_shift(-1))
    to_left = left_sum[half:] + for_left.astype(F32)
    to_right = right_sum[:half] + for_right.astype(F32)
    (own_sum,) = after((own_sum,), to_left, to_right)
    first_half = own_sum[:half] + from_right.astype(F32)
    second_half = own_sum[half:] + from_left.astype(F32)
    first_half, second_half = lax.optimization_barrier((first_half, second_half))
    then_right = lax.ppermute(to_left.astype(BF16), "seq", x_shift(-1))
    then_left = lax.ppermute(to_right.astype(BF16), "seq", x_shift(1))
    return jnp.concatenate(
        [first_half + then_left.astype(F32), second_half + then_right.astype(F32)]
    )


def per_device(
    xin,
    zin,
    conv_weight,
    conv_bias,
    xproj_weight,
    dtproj_weight,
    dt_bias,
    a_log,
    skip,
    out_weight,
    resid,
    norm_gain,
    expert_ids,
    gate_weights,
    w_gate,
    w_up,
    w_down,
):
    channels = xin.shape[2]
    xin = xin.reshape(TOKENS, channels)
    edge = passed_along(xin[TOKENS - (CONV - 1) * DOCS :], "seq", 1)
    inner, projected = mixer_in(xin, edge, conv_weight, conv_bias[None], xproj_weight.T)
    along_z = [projected] + from_others(projected, z_shift)
    projected = sum(part.astype(F32) for part in along_z).astype(BF16)
    parts = [projected] + from_others(projected, y_shift)
    step, states, packed = section_scan(parts, dtproj_weight, dt_bias[None], a_log, inner)
    columns = [lax.ppermute(packed, "seq", x_shift(by)) for by in (1, 2, 3)]
    partial_rows = mixer_out(
        lax.axis_index("seq").reshape(1),
        columns + [swapped(packed)] + [swapped(column) for column in columns],
        step,
        states,
        inner,
        a_log,
        skip[None],
        zin.reshape(TOKENS, channels),
        out_weight,
    )
    exchanged = lax.all_to_all(partial_rows, "exp", split_axis=0, concat_axis=0, tiled=True)
    row_count = resid.shape[0] * resid.shape[1]
    mamba_rows = jnp.sum(exchanged.reshape(-1, row_count, D).astype(F32), axis=0)
    hidden_state = resid.reshape(row_count, D).astype(F32) + mamba_rows
    norm_scale = lax.rsqrt(jnp.mean(hidden_state * hidden_state, axis=-1, keepdims=True) + 1e-05)
    tokens = (hidden_state * norm_scale * norm_gain).astype(BF16)
    capacity = 2 * TOPK * row_count // EXPERTS
    splits = lax.axis_size("exp") // EXPERTS
    route_ids = expert_ids.reshape(row_count, TOPK)
    gate_vals = gate_weights.reshape(row_count, TOPK)
    matches = slot_select(route_ids, capacity)
    chosen = jnp.sum(matches.astype(jnp.int32), axis=2).astype(BF16)
    outgoing = jnp.dot(chosen, tokens, preferred_element_type=F32).astype(BF16)
    arrived = lax.all_to_all(
        jnp.tile(outgoing, (splits, 1)), "exp", split_axis=0, concat_axis=0, tiled=True
    )
    own_rows = experts(arrived, w_gate, w_up, w_down)
    returned = lax.all_to_all(
        own_rows.astype(BF16), "exp", split_axis=0, concat_axis=0, tiled=True
    ).astype(F32)
    summed = jnp.sum(returned.reshape(splits, EXPERTS * capacity, D), axis=0)
    weights = jnp.sum(matches.astype(F32) * gate_vals.astype(F32)[None], axis=2)
    weights = weights.reshape((-1,) + resid.shape[:2])
    expert_out = jnp.einsum("qab,qd->abd", weights, summed, precision=lax.Precision.HIGHEST)
    return (hidden_state.reshape(resid.shape) + expert_out).astype(BF16)


def solution(mesh):
    placed = (
        P("seq", None, "exp"),
        P("seq", None, "exp"),
        P(None, "exp"),
        P("exp"),
        P("exp", None),
        P(None, "exp"),
        P("exp"),
        P(None, "exp"),
        P("exp"),
        P("exp", None),
        P(("seq", "exp"), None, None),
        P(),
        P(("seq", "exp"), None, None),
        P(("seq", "exp"), None, None),
        P("exp", None, "seq"),
        P("exp", None, "seq"),
        P("exp", "seq", None),
    )
    return jax.shard_map(
        per_device,
        mesh=mesh,
        in_specs=placed,
        out_specs=P(("seq", "exp"), None, None),
        check_vma=False,
    )
```
